32 devices in a mesh: wide: 8 (over y, x, core), narrow: 4 (over z).
Axes of the slice: x: 2, y: 2, z: 4, core: 2. Of those that a mesh axis runs over, the one named last changes fastest.
Arguments:
- latents: bfloat16 [32768, 1024], P(('wide', 'narrow')), may hold values from -6 to 6
- group_inputs: bfloat16 [32768, 1024], P(('wide', 'narrow')), may hold values from -6 to 6
- latent_images: int32 [32, 1024], P(('wide', 'narrow')), may hold values from 0 to 31, as said below
- input_images: int32 [32, 1024], P(('wide', 'narrow')), may hold values from 0 to 31, as said below
- cotangent: bfloat16 [32768, 1024], P(('wide', 'narrow')), may hold values from -6 to 6
- cross_gain: bfloat16 [1024], P(('wide', 'narrow')), may hold values from 0.5 to 1.5
- cross_shift: bfloat16 [1024], P(('wide', 'narrow')), may hold values from -1.25 to 1.25
- source_gain: bfloat16 [1024], P(('wide', 'narrow')), may hold values from 0.5 to 1.5
- source_shift: bfloat16 [1024], P(('wide', 'narrow')), may hold values from -1.25 to 1.25
- query_weight: bfloat16 [1024, 1024], P(('wide', 'narrow')), may hold values from -0.1875 to 0.1875
- keyval_weight: bfloat16 [1024, 2048], P(('wide', 'narrow')), may hold values from -0.1875 to 0.1875
- cross_out_weight: bfloat16 [1024, 1024], P(('wide', 'narrow')), may hold values from -0.5 to 0.5
- self_gain: bfloat16 [1024], P(('wide', 'narrow')), may hold values from 0.5 to 1.5
- self_shift: bfloat16 [1024], P(('wide', 'narrow')), may hold values from -1.25 to 1.25
- self_qkv_weight: bfloat16 [1024, 3072], P(('wide', 'narrow')), may hold values from -0.1875 to 0.1875
- self_out_weight: bfloat16 [1024, 1024], P(('wide', 'narrow')), may hold values from -0.5 to 0.5
- mlp_gain: bfloat16 [1024], P(('wide', 'narrow')), may hold values from 0.5 to 1.5
- mlp_shift: bfloat16 [1024], P(('wide', 'narrow')), may hold values from -1.25 to 1.25
- up_weight: bfloat16 [1024, 4096], P(('wide', 'narrow')), may hold values from -0.1875 to 0.1875
- up_bias: bfloat16 [4096], P(('wide', 'narrow')), may hold values from -1.25 to 1.25
- down_weight: bfloat16 [4096, 1024], P(('wide', 'narrow')), may hold values from -0.09375 to 0.09375
- down_bias: bfloat16 [1024], P(('wide', 'narrow')), may hold values from -1.25 to 1.25
Outputs:
- new_latents: bfloat16 [32768, 1024], P(('wide', 'narrow'))
- latent_grad: bfloat16 [32768, 1024], P(('wide', 'narrow'))
- input_grad: bfloat16 [32768, 1024], P(('wide', 'narrow'))
- cross_gain_grad: float32 [1024], P(('wide', 'narrow'))
- cross_shift_grad: float32 [1024], P(('wide', 'narrow'))
- source_gain_grad: float32 [1024], P(('wide', 'narrow'))
- source_shift_grad: float32 [1024], P(('wide', 'narrow'))
- query_weight_grad: float32 [1024, 1024], P(('wide', 'narrow'))
- keyval_weight_grad: float32 [1024, 2048], P(('wide', 'narrow'))
- cross_out_weight_grad: float32 [1024, 1024], P(('wide', 'narrow'))
- self_gain_grad: float32 [1024], P(('wide', 'narrow'))
- self_shift_grad: float32 [1024], P(('wide', 'narrow'))
- self_qkv_weight_grad: float32 [1024, 3072], P(('wide', 'narrow'))
- self_out_weight_grad: float32 [1024, 1024], P(('wide', 'narrow'))
- mlp_gain_grad: float32 [1024], P(('wide', 'narrow'))
- mlp_shift_grad: float32 [1024], P(('wide', 'narrow'))
- up_weight_grad: float32 [1024, 4096], P(('wide', 'narrow'))
- up_bias_grad: float32 [4096], P(('wide', 'narrow'))
- down_weight_grad: float32 [4096, 1024], P(('wide', 'narrow'))
- down_bias_grad: float32 [1024], P(('wide', 'narrow'))
The draws below stay inside these ranges and needn't reach their ends.
Inputs may be any that keep to these rules, and one draw needn't show every extreme that they name: `latent_images`: in each sample, group g holds 1 to 4 images with ids from 4 * g to 4 * g + 3; ids never fall along the group's 128 latents, the last latent of a group has 4 * g + 3, and every image of a group occurs among both its latents and its 128 input tokens. `input_images`: in each sample, the 128 input tokens of group g hold the same images as its latents, with the same ids, never falling along the group, the last token of a group having 4 * g + 3.
All inputs are finite; a program needn't handle non-finite values.
Results may differ from the reference program's by a relative error of at most 0.015.
Values may be sent and summed in bfloat16 or wider, within the bound.
A program may use at most 384 MiB of HBM per device.

```python
import jax
import jax.numpy as jnp
from jax import lax

D = 1024
HEADS = 8
HD = 128
FF = 4096
GROUPS = 8
GLAT = 128
GIN = 128
LAT = 1024
INP = 1024
SAMPLES = 32


def image_layout(key, length, salt_value):
    counts = jax.random.randint(jax.random.fold_in(key, 7), (SAMPLES, GROUPS, 1), 1, 5)
    scores = jax.random.randint(jax.random.fold_in(key, salt_value), (SAMPLES, GROUPS, length - 1), 0, 1 << 20)
    scores = scores * length + jnp.arange(length - 1, dtype=jnp.int32)
    ordering = jnp.argsort(scores, axis=-1, stable=True)
    cut_places = ordering[:, :, :3] + 1
    in_use = jnp.arange(3, dtype=jnp.int32)[None, None, :] < counts - 1
    positions = jnp.arange(length, dtype=jnp.int32)
    later_cuts = jnp.sum(((cut_places[:, :, None, :] > positions[None, None, :, None]) & in_use[:, :, None, :]).astype(jnp.int32), axis=-1)
    group_base = 4 * jnp.arange(GROUPS, dtype=jnp.int32)[None, :, None]
    image_ids = group_base + 3 - later_cuts
    return image_ids.reshape(SAMPLES, GROUPS * length).astype(jnp.int32)


def draw_latent_images(key, part):
    return image_layout(key, GLAT, 11)


def draw_input_images(key, part):
    return image_layout(key, GIN, 13)


def steps_of(rng, dims, cuts, smallest, top_value):
    loudness, own = 1.0, jax.random.fold_in(rng, 6)
    for axis_at, parts in cuts:
        heights = jnp.exp(jax.random.uniform(jax.random.fold_in(own, axis_at), (parts,), jnp.float32, smallest / len(cuts), top_value / len(cuts)))
        loudness = loudness * jnp.repeat(heights, dims[axis_at] // parts).reshape([-1 if axis == axis_at else 1 for axis in range(len(dims))])
    return loudness


def bell_draw(key, shape, width, reach, shards=(), kind=jnp.bfloat16):
    loudness = steps_of(key, shape, shards, -0.22, 0.18) if shards else 1.0
    entries = jax.random.normal(key, shape, jnp.float32) * width * loudness
    return jnp.minimum(jnp.maximum(entries, -reach), reach).astype(kind)


def setup_inputs(seed: int = 0) -> dict:
    seeds = jax.random.split(jax.random.key(seed), 23)
    latents = bell_draw(seeds[0], (SAMPLES * LAT, D), 1.0, 6.0, ((0, 32),))
    group_inputs = bell_draw(seeds[1], (SAMPLES * INP, D), 1.0, 6.0, ((0, 32),))
    latent_images = draw_latent_images(jax.random.fold_in(seeds[22], 71), 0)
    input_images = draw_input_images(jax.random.fold_in(seeds[22], 71), 0)
    cotangent = bell_draw(seeds[4], (SAMPLES * LAT, D), 1.0, 6.0, ((0, 32),))
    cross_gain = jnp.clip(1.0 + 0.1 * jax.random.normal(seeds[5], (D,), jnp.float32), 0.5, 1.5).astype(jnp.bfloat16)
    cross_shift = bell_draw(seeds[6], (D,), 0.2, 1.25, ((0, 32),))
    source_gain = jnp.clip(1.0 + 0.1 * jax.random.normal(seeds[7], (D,), jnp.float32), 0.5, 1.5).astype(jnp.bfloat16)
    source_shift = bell_draw(seeds[8], (D,), 0.2, 1.25, ((0, 32),))
    query_weight = bell_draw(seeds[9], (D, D), D ** -0.5, 0.1875, ((0, 32),))
    keyval_weight = bell_draw(seeds[10], (D, 2 * D), D ** -0.5, 0.1875, ((0, 32),))
    cross_out_weight = bell_draw(seeds[11], (D, D), (D // 8) ** -0.5, 0.5, ((0, 32),))
    self_gain = jnp.clip(1.0 + 0.1 * jax.random.normal(seeds[12], (D,), jnp.float32), 0.5, 1.5).astype(jnp.bfloat16)
    self_shift = bell_draw(seeds[13], (D,), 0.2, 1.25, ((0, 32),))
    self_qkv_weight = bell_draw(seeds[14], (D, 3 * D), D ** -0.5, 0.1875, ((0, 32),))
    self_out_weight = bell_draw(seeds[15], (D, D), (D // 8) ** -0.5, 0.5, ((0, 32),))
    mlp_gain = jnp.clip(1.0 + 0.1 * jax.random.normal(seeds[16], (D,), jnp.float32), 0.5, 1.5).astype(jnp.bfloat16)
    mlp_shift = bell_draw(seeds[17], (D,), 0.2, 1.25, ((0, 32),))
    up_weight = bell_draw(seeds[18], (D, FF), D ** -0.5, 0.1875, ((0, 32),))
    up_bias = bell_draw(seeds[19], (FF,), 0.2, 1.25, ((0, 32),))
    down_weight = bell_draw(seeds[20], (FF, D), FF ** -0.5, 0.09375, ((0, 32),))
    down_bias = bell_draw(seeds[21], (D,), 0.2, 1.25, ((0, 32),))
    return {"latents": latents, "group_inputs": group_inputs, "latent_images": latent_images, "input_images": input_images, "cotangent": cotangent, "cross_gain": cross_gain, "cross_shift": cross_shift, "source_gain": source_gain, "source_shift": source_shift, "query_weight": query_weight, "keyval_weight": keyval_weight, "cross_out_weight": cross_out_weight, "self_gain": self_gain, "self_shift": self_shift, "self_qkv_weight": self_qkv_weight, "self_out_weight": self_out_weight, "mlp_gain": mlp_gain, "mlp_shift": mlp_shift, "up_weight": up_weight, "up_bias": up_bias, "down_weight": down_weight, "down_bias": down_bias}


EPSILON = 1e-05
HIGHEST = lax.Precision.HIGHEST

@jax.custom_vjp
def low(v):
    return lax.optimization_barrier(v.astype(jnp.bfloat16)).astype(jnp.float32)

@jax.custom_vjp
def low_back(v):
    return v

def low_keep(v):
    return (low(v), None)

def low_pass(kept, grad):
    return (grad,)

def back_keep(v):
    return (v, None)

def back_low(kept, grad):
    return (low(grad),)
low.defvjp(low_keep, low_pass)
low_back.defvjp(back_keep, back_low)

def both_low(values):
    return low(low_back(values))

def norm_rows(values, scale_vec, shift_vec):
    center = values - lax.optimization_barrier(jnp.mean(values, axis=-1, keepdims=True))
    spread = lax.optimization_barrier(jnp.mean(center * center, axis=-1, keepdims=True))
    return center * lax.rsqrt(spread + EPSILON) * scale_vec + shift_vec

def matmul(left, right):
    return jnp.dot(left, right, precision=HIGHEST)

def split_heads(matrix, length):
    return matrix.reshape(-1, length, HEADS, HD)

def attention(queries, keys_in, values_in, allowed):
    scores = jnp.einsum('blhe,bmhe->bhlm', queries, keys_in, precision=HIGHEST) * HD ** (-0.5)
    scores = low_back(scores)
    scores = jnp.where(allowed[:, None], scores, -1e+30)
    row_top = lax.optimization_barrier(jnp.max(scores, axis=-1, keepdims=True))
    raised = jnp.exp(scores - row_top)
    softmax_rows = raised / lax.optimization_barrier(jnp.sum(raised, axis=-1, keepdims=True))
    mixture = jnp.einsum('bhlm,bmhe->blhe', low(softmax_rows), values_in, precision=HIGHEST)
    return both_low(mixture)

def layer_block(params, start_rows, source_rows, latent_ids, input_ids):
    cross_gain, cross_shift, source_gain, source_shift, query_weight, keyval_weight, cross_out_weight, self_gain, self_shift, self_qkv_weight, self_out_weight, mlp_gain, mlp_shift, up_weight, up_bias, down_weight, down_bias = params
    latent_rows = latent_ids.reshape(-1, GLAT)
    cross_allowed = latent_rows[:, :, None] == input_ids.reshape(-1, GIN)[:, None, :]
    self_allowed = latent_rows[:, :, None] == latent_rows[:, None, :]
    lat_low = low(norm_rows(start_rows, cross_gain, cross_shift))
    src_low = low(norm_rows(source_rows, source_gain, source_shift))
    queries = both_low(matmul(lat_low, query_weight))
    keyvals = both_low(matmul(src_low, keyval_weight))
    cross_mix = attention(split_heads(queries, GLAT), split_heads(keyvals[:, :D], GIN), split_heads(keyvals[:, D:], GIN), cross_allowed).reshape(-1, D)
    after_cross = start_rows + low_back(matmul(cross_mix, cross_out_weight))
    self_low = low(norm_rows(after_cross, self_gain, self_shift))
    triple = both_low(matmul(self_low, self_qkv_weight))
    self_mix = attention(split_heads(triple[:, :D], GLAT), split_heads(triple[:, D:2 * D], GLAT), split_heads(triple[:, 2 * D:], GLAT), self_allowed).reshape(-1, D)
    after_self = after_cross + low_back(matmul(self_mix, self_out_weight))
    mlp_low = low(norm_rows(after_self, mlp_gain, mlp_shift))
    hidden = low_back(matmul(mlp_low, up_weight) + up_bias)
    activated = low(jax.nn.gelu(hidden, approximate=False))
    return after_self + low_back(matmul(activated, down_weight) + down_bias)

def reference(latents, group_inputs, latent_images, input_images, cotangent, cross_gain, cross_shift, source_gain, source_shift, query_weight, keyval_weight, cross_out_weight, self_gain, self_shift, self_qkv_weight, self_out_weight, mlp_gain, mlp_shift, up_weight, up_bias, down_weight, down_bias):
    params = tuple((member.astype(jnp.float32) for member in (cross_gain, cross_shift, source_gain, source_shift, query_weight, keyval_weight, cross_out_weight, self_gain, self_shift, self_qkv_weight, self_out_weight, mlp_gain, mlp_shift, up_weight, up_bias, down_weight, down_bias)))
    start_rows = latents.astype(jnp.float32)
    source_rows = group_inputs.astype(jnp.float32)
    block_count = SAMPLES // 4
    latent_ids = latent_images.reshape(block_count, 4, LAT)
    input_ids = input_images.reshape(block_count, 4, INP)
    checked = jax.checkpoint(layer_block)

    def forward(start_all, source_all, weights_all):

        def advance(state_carry, block_data):
            return (state_carry, checked(weights_all, block_data[0], block_data[1], block_data[2], block_data[3]))
        block_items = (start_all.reshape(block_count, 4 * LAT, D), source_all.reshape(block_count, 4 * INP, D), latent_ids, input_ids)
        outcome = lax.scan(advance, jnp.zeros((), jnp.float32), block_items)[1]
        return outcome.reshape(SAMPLES * LAT, D)
    finished, pullback = jax.vjp(forward, start_rows, source_rows, params)
    grad_start, grad_source, grads = pullback(cotangent.astype(jnp.float32))
    return (finished.astype(jnp.bfloat16), grad_start.astype(jnp.bfloat16), grad_source.astype(jnp.bfloat16), grads[0], grads[1], grads[2], grads[3], grads[4], grads[5], grads[6], grads[7], grads[8], grads[9], grads[10], grads[11], grads[12], grads[13], grads[14], grads[15], grads[16])
```

```python
from functools import partial

import jax
import jax.numpy as jnp
from jax import lax
from jax.experimental import pallas as pl
from jax.experimental.pallas import tpu as pltpu
from jax.sharding import PartitionSpec as P

MESH = pl.DeviceIdType.MESH
BF16 = jnp.bfloat16
F32 = jnp.float32


class Place:
    def __init__(self, wide_size, narrow_size):
        self.wide = lax.axis_index("wide")
        self.narrow = lax.axis_index("narrow")
        self.n_narrow = narrow_size
        self.columns = wide_size // 2
        self.n_a = 2 if self.columns % 2 == 0 else 1
        self.n_b = self.columns // self.n_a
        self.core = lax.rem(self.wide, 2)
        column = self.wide // 2
        self.a = column // self.n_b
        self.b = lax.rem(column, self.n_b)
        self.coloured = self.n_a == self.n_b

    def index(self, a, b, core):
        return (a * self.n_b + b) * 2 + core

    def sibling(self):
        return self.wide + 1 - 2 * self.core

    def along_a(self, step):
        return self.index(lax.rem(self.a + step, self.n_a), self.b, self.core)

    def along_b(self, step):
        return self.index(self.a, lax.rem(self.b + step, self.n_b), self.core)

    def first_count(self):
        return self.n_b

    def second_count(self):
        return self.n_a

    def first(self, step):
        if not self.coloured:
            return self.along_b(step)
        return jnp.where(self.core == 0, self.along_b(step), self.along_a(step))

    def second(self, step):
        if not self.coloured:
            return self.along_a(step)
        return jnp.where(self.core == 0, self.along_a(step), self.along_b(step))

    def corner(self, first_step, second_step):
        if not self.coloured:
            return self.index(
                lax.rem(self.a + second_step, self.n_a),
                lax.rem(self.b + first_step, self.n_b),
                self.core,
            )
        step_a = jnp.where(self.core == 0, second_step, first_step)
        step_b = jnp.where(self.core == 0, first_step, second_step)
        return self.index(
            lax.rem(self.a + step_a, self.n_a), lax.rem(self.b + step_b, self.n_b), self.core
        )

    def depth(self, step):
        return lax.rem(self.narrow + step, self.n_narrow)

    def greet(self):
        barrier = pltpu.get_barrier_semaphore()
        count = 0
        for step in range(1, self.n_narrow):
            pl.semaphore_signal(
                barrier, inc=1, device_id=(self.wide, self.depth(step)), device_id_type=MESH
            )
            count += 1
        for step in range(1, self.n_b):
            pl.semaphore_signal(
                barrier, inc=1, device_id=(self.along_b(step), self.narrow), device_id_type=MESH
            )
            count += 1
        for step in range(1, self.n_a):
            pl.semaphore_signal(
                barrier, inc=1, device_id=(self.along_a(step), self.narrow), device_id_type=MESH
            )
            count += 1
        pl.semaphore_signal(
            barrier, inc=1, device_id=(self.sibling(), self.narrow), device_id_type=MESH
        )
        pl.semaphore_wait(barrier, count + 1)


class Gather:
    def __init__(self, place, unit, shard, full, sems):
        self.place = place
        self.unit = unit
        self.shard = shard
        self.full = full
        self.send, self.recv = sems
        self.pending = []
        p = place
        self.n_z = p.n_narrow - 1
        self.n_1 = (p.first_count() - 1) * p.n_narrow
        self.n_2 = (p.second_count() - 1) * p.first_count()

    def view(self, wide, narrow=None):
        r0, rh, c0, cw = self.unit
        n = self.place.n_narrow
        if narrow is None:
            return self.full.at[pl.ds(wide * n, n), pl.ds(r0, rh), pl.ds(c0, cw)]
        return self.full.at[wide * n + narrow, pl.ds(r0, rh), pl.ds(c0, cw)]

    def own(self):
        r0, rh, c0, cw = self.unit
        return self.shard.at[pl.ds(r0, rh), pl.ds(c0, cw)]

    def copy(self, src, dst, slot, device):
        return pltpu.make_async_remote_copy(
            src_ref=src,
            dst_ref=dst,
            send_sem=self.send.at[slot],
            recv_sem=self.recv.at[slot],
            device_id=device,
            device_id_type=MESH,
        )

    def go(self, copy):
        copy.start()
        self.pending.append(copy)

    def landed(self, view, slot):
        me = (self.place.wide, self.place.narrow)
        self.copy(view, view, slot, (self.place.sibling(), self.place.narrow)).wait_recv()

    def slot_first(self, step, k):
        return self.n_z + (step - 1) * self.place.n_narrow + k

    def slot_second(self, step, k):
        return self.n_z + self.n_1 + (step - 1) * self.place.first_count() + k

    def slot_sibling(self, k):
        return self.n_z + self.n_1 + self.n_2 + k

    def stage_1(self):
        p = self.place
        for step in range(1, p.n_narrow):
            self.go(
                self.copy(
                    self.own(),
                    self.view(p.wide, p.narrow),
                    step - 1,
                    (p.wide, p.depth(step)),
                )
            )
        for step in range(1, p.first_count()):
            self.go(
                self.copy(
                    self.own(),
                    self.view(p.wide, p.narrow),
                    self.slot_first(step, 0),
                    (p.first(step), p.narrow),
                )
            )

    def stage_2(self):
        p = self.place
        for step in range(1, p.n_narrow):
            source = p.depth(p.n_narrow - step)
            view = self.view(p.wide, source)
            self.landed(view, step - 1)
            for hop in range(1, p.first_count()):
                self.go(
                    self.copy(view, view, self.slot_first(hop, step), (p.first(hop), p.narrow))
                )
        view = self.view(p.wide)
        for hop in range(1, p.second_count()):
            self.go(self.copy(view, view, self.slot_second(hop, 0), (p.second(hop), p.narrow)))
        self.go(self.copy(view, view, self.slot_sibling(0), (p.sibling(), p.narrow)))

    def stage_3(self):
        p = self.place
        for step in range(1, p.first_count()):
            column = p.first(p.first_count() - step)
            for k in range(p.n_narrow):
                source = p.depth(p.n_narrow - k)
                self.landed(self.view(column, source), self.slot_first(step, k))
            view = self.view(column)
            for hop in range(1, p.second_count()):
                self.go(
                    self.copy(view, view, self.slot_second(hop, step), (p.second(hop), p.narrow))
                )
            self.go(self.copy(view, view, self.slot_sibling(step), (p.sibling(), p.narrow)))

    def stage_4(self):
        p = self.place
        for hop in range(1, p.second_count()):
            back = p.second_count() - hop
            for k in range(p.first_count()):
                column = p.corner((p.first_count() - k) % p.first_count(), back)
                view = self.view(column)
                self.landed(view, self.slot_second(hop, k))
                slot = self.slot_sibling(hop * p.first_count() + k)
                self.go(self.copy(view, view, slot, (p.sibling(), p.narrow)))

    def stage_5(self):
        p = self.place
        for hop in range(p.second_count()):
            for k in range(p.first_count()):
                back_1 = (p.first_count() - k) % p.first_count()
                back_2 = (p.second_count() - hop) % p.second_count()
                if p.coloured:
                    step_a = jnp.where(p.core == 1, back_2, back_1)
                    step_b = jnp.where(p.core == 1, back_1, back_2)
                else:
                    step_a, step_b = back_2, back_1
                column = p.index(
                    lax.rem(p.a + step_a, p.n_a), lax.rem(p.b + step_b, p.n_b), 1 - p.core
                )
                self.landed(self.view(column), self.slot_sibling(hop * p.first_count() + k))

    def drain(self):
        for copy in self.pending:
            copy.wait_send()


def gather_slots(wide_size, narrow_size):
    columns = wide_size // 2
    n_a = 2 if columns % 2 == 0 else 1
    n_b = columns // n_a
    return (narrow_size - 1) + (n_b - 1) * narrow_size + (n_a - 1) * n_b + n_a * n_b


class Scatter:
    def __init__(self, place, unit, grad, out, bufs, sems):
        self.place = place
        self.unit = unit
        self.grad = grad
        self.out = out
        self.held, self.from_sibling, self.from_second, self.from_first, self.from_depth = bufs
        self.send, self.recv, self.local = sems
        self.pending = []
        p = place
        self.n_1 = p.first_count()
        self.n_2 = p.second_count()
        self.blocks = self.n_1 * self.n_2

    def view(self, wide):
        r0, rh, c0, cw = self.unit
        n = self.place.n_narrow
        return self.grad.at[pl.ds(wide * n, n), pl.ds(r0, rh), pl.ds(c0, cw)]

    def copy(self, src, dst, slot, device):
        return pltpu.make_async_remote_copy(
            src_ref=src,
            dst_ref=dst,
            send_sem=self.send.at[slot],
            recv_sem=self.recv.at[slot],
            device_id=device,
            device_id_type=MESH,
        )

    def go(self, copy):
        copy.start()
        self.pending.append(copy)

    def landed(self, ref, slot):
        self.copy(ref, ref, slot, (self.place.sibling(), self.place.narrow)).wait_recv()

    def loads(self):
        p = self.place
        result = []
        for s in range(self.n_2):
            for f in range(self.n_1):
                block = s * self.n_1 + f
                result.append(
                    pltpu.make_async_copy(
                        self.view(p.corner(f, s)), self.held.at[block], self.local.at[block]
                    )
                )
        return result

    def stage_0(self):
        p = self.place
        for s in range(self.n_2):
            for f in range(self.n_1):
                if p.coloured:
                    step_a = jnp.where(p.core == 1, s, f)
                    step_b = jnp.where(p.core == 1, f, s)
                else:
                    step_a, step_b = s, f
                column = p.index(
                    lax.rem(p.a + step_a, p.n_a), lax.rem(p.b + step_b, p.n_b), 1 - p.core
                )
                block = s * self.n_1 + f
                self.go(
                    self.copy(
                        self.view(column),
                        self.from_sibling.at[block],
                        block,
                        (p.sibling(), p.narrow),
                    )
                )
        for load in self.loads():
            load.start()

    def add(self, block, *others):
        n = self.held.shape[1]

        def step(i, carry):
            total = self.held[block, i].astype(F32)
            for other in others:
                total = total + other[i].astype(F32)
            self.held[block, i] = total.astype(self.held.dtype)
            return carry

        lax.fori_loop(0, n, step, 0)

    def stage_1(self):
        p = self.place
        for load in self.loads():
            load.wait()
        for block in range(self.blocks):
            self.landed(self.from_sibling.at[block], block)
        for s in range(self.n_2 - 1, -1, -1):
            for f in range(self.n_1):
                block = s * self.n_1 + f
                self.add(block, self.from_sibling.at[block])
                if s > 0:
                    slot = (s - 1) * self.n_1 + f
                    self.go(
                        self.copy(
                            self.held.at[block],
                            self.from_second.at[slot],
                            self.blocks + slot,
                            (p.second(s), p.narrow),
                        )
                    )

    def stage_2(self):
        p = self.place
        base = self.blocks + (self.n_2 - 1) * self.n_1
        for f in range(self.n_1 - 1, -1, -1):
            slots = [s * self.n_1 + f for s in range(self.n_2 - 1)]
            for slot in slots:
                self.landed(self.from_second.at[slot], self.blocks + slot)
            self.add(f, *[self.from_second.at[slot] for slot in slots])
            if f > 0:
                self.go(
                    self.copy(
                        self.held.at[f],
                        self.from_first.at[f - 1],
                        base + f - 1,
                        (p.first(f), p.narrow),
                    )
                )

    def stage_3(self):
        p = self.place
        first_base = self.blocks + (self.n_2 - 1) * self.n_1
        base = first_base + self.n_1 - 1
        for f in range(1, self.n_1):
            self.landed(self.from_first.at[f - 1], first_base + f - 1)
        self.add(0, *[self.from_first.at[f - 1] for f in range(1, self.n_1)])
        for step in range(1, p.n_narrow):
            self.go(
                self.copy(
                    self.held.at[0, p.depth(step)],
                    self.from_depth.at[step - 1],
                    base + step - 1,
                    (p.wide, p.depth(step)),
                )
            )

    def stage_4(self):
        p = self.place
        base = self.blocks + (self.n_2 - 1) * self.n_1 + self.n_1 - 1
        for step in range(1, p.n_narrow):
            self.landed(self.from_depth.at[step - 1], base + step - 1)
        r0, rh, c0, cw = self.unit
        total = self.held[0, p.narrow].astype(F32)
        for step in range(1, p.n_narrow):
            total = total + self.from_depth[step - 1].astype(F32)
        self.out[pl.ds(r0, rh), pl.ds(c0, cw)] = total

    def drain(self):
        for copy in self.pending:
            copy.wait_send()


def scatter_slots(wide_size, narrow_size):
    columns = wide_size // 2
    n_a = 2 if columns % 2 == 0 else 1
    n_b = columns // n_a
    return n_a * n_b + (n_a - 1) * n_b + (n_b - 1) + (narrow_size - 1)


UNIT = 1024


def units_of(shards, rows):
    result = []
    for index, member in enumerate(shards):
        height, width = member.shape
        for r0 in range(0, height, rows):
            for c0 in range(0, width, UNIT):
                result.append((index, r0, min(rows, height - r0), c0, min(UNIT, width - c0)))
    return result


def gather_kernel(sizes, units, count, *refs):
    shards, fulls = refs[:count], refs[count : 2 * count]
    staged = refs[2 * count : 3 * count]
    send, recv, load_sem, store_sem = refs[3 * count :]
    place = Place(*sizes)
    mine = place.wide * place.n_narrow + place.narrow
    for k in range(count):
        pltpu.make_async_copy(shards[k], staged[k], load_sem.at[k]).start()
    place.greet()
    jobs = [
        Gather(place, unit[1:], shards[unit[0]], fulls[unit[0]], (send.at[i], recv.at[i]))
        for i, unit in enumerate(units)
    ]
    jobs[0].stage_1()
    for k in range(count):
        pltpu.make_async_copy(shards[k], staged[k], load_sem.at[k]).wait()
        pltpu.make_async_copy(staged[k], fulls[k].at[mine], store_sem.at[k]).start()
    jobs[1].stage_1()
    for k in range(count):
        pltpu.make_async_copy(staged[k], fulls[k].at[mine], store_sem.at[k]).wait()
    total = len(jobs)
    for t in range(1, total + 3):
        if t < total and t > 1:
            jobs[t].stage_1()
        if 0 <= t - 1 < total:
            jobs[t - 1].stage_2()
        if 0 <= t - 2 < total:
            jobs[t - 2].stage_3()
        if 0 <= t - 3 < total:
            jobs[t - 3].stage_4()
    for job in jobs:
        job.stage_5()
    for job in jobs:
        job.drain()


def gather_all(shards):
    sizes = (lax.axis_size("wide"), lax.axis_size("narrow"))
    everyone = sizes[0] * sizes[1]
    rows = min(member.shape[0] for member in shards[1:])
    units = units_of(shards, rows)
    slots = gather_slots(*sizes)
    count = len(shards)
    return pl.pallas_call(
        partial(gather_kernel, sizes, units, count),
        out_shape=[
            jax.ShapeDtypeStruct((everyone,) + member.shape, member.dtype) for member in shards
        ],
        in_specs=[pl.BlockSpec(memory_space=pl.ANY)] * count,
        out_specs=[pl.BlockSpec(memory_space=pl.ANY)] * count,
        scratch_shapes=[pltpu.VMEM(member.shape, member.dtype) for member in shards]
        + [
            pltpu.SemaphoreType.DMA((len(units), slots)),
            pltpu.SemaphoreType.DMA((len(units), slots)),
            pltpu.SemaphoreType.DMA((count,)),
            pltpu.SemaphoreType.DMA((count,)),
        ],
        compiler_params=pltpu.CompilerParams(collective_id=0, has_side_effects=True),
        name="gather_weights",
    )(*shards)


def scatter_kernel(sizes, units, count, *refs):
    grads, outs = refs[:count], refs[count : 2 * count]
    small_bufs, big_bufs = refs[2 * count : 2 * count + 5], refs[2 * count + 5 : 2 * count + 10]
    send, recv, local = refs[2 * count + 10 :]
    place = Place(*sizes)
    place.greet()
    jobs = []
    for i, unit in enumerate(units):
        bufs = small_bufs if i == 0 else tuple(buf.at[i - 1] for buf in big_bufs)
        jobs.append(
            Scatter(
                place,
                unit[1:],
                grads[unit[0]],
                outs[unit[0]],
                bufs,
                (send.at[i], recv.at[i], local.at[i]),
            )
        )
    total = len(jobs)
    for t in range(total + 4):
        for back, stage in enumerate(("stage_0", "stage_1", "stage_2", "stage_3", "stage_4")):
            if 0 <= t - back < total:
                getattr(jobs[t - back], stage)()
    for job in jobs:
        job.drain()


def scatter_all(grads):
    sizes = (lax.axis_size("wide"), lax.axis_size("narrow"))
    everyone = sizes[0] * sizes[1]
    outs = [jax.ShapeDtypeStruct(member.shape[1:], F32) for member in grads]
    rows = min(member.shape[0] for member in outs[1:])
    units = units_of(outs, rows)
    columns = sizes[0] // 2
    n_2 = 2 if columns % 2 == 0 else 1
    n_1 = columns // n_2
    count = len(grads)
    n = sizes[1]

    def bufs(lead, shape, kind):
        return [
            pltpu.VMEM(lead + (columns, n) + shape, kind),
            pltpu.VMEM(lead + (columns, n) + shape, kind),
            pltpu.VMEM(lead + ((n_2 - 1) * n_1, n) + shape, kind),
            pltpu.VMEM(lead + (n_1 - 1, n) + shape, kind),
            pltpu.VMEM(lead + (n - 1,) + shape, kind),
        ]

    slots = scatter_slots(*sizes)
    return pl.pallas_call(
        partial(scatter_kernel, sizes, units, count),
        out_shape=outs,
        in_specs=[pl.BlockSpec(memory_space=pl.ANY)] * count,
        out_specs=[pl.BlockSpec(memory_space=pltpu.VMEM)] * count,
        scratch_shapes=bufs((), outs[0].shape, grads[0].dtype)
        + bufs((len(units) - 1,), (rows, UNIT), BF16)
        + [
            pltpu.SemaphoreType.DMA((len(units), slots)),
            pltpu.SemaphoreType.DMA((len(units), slots)),
            pltpu.SemaphoreType.DMA((len(units), columns)),
        ],
        compiler_params=pltpu.CompilerParams(
            collective_id=1, has_side_effects=True, vmem_limit_bytes=63 * 2**20
        ),
        name="scatter_gradients",
    )(*grads)


EPSILON = 1e-05
HEADS = 8
HD = 128
GLAT = 128
GIN = 128


def norm_rows(values, scale_vec, shift_vec):
    center = values - jnp.mean(values, axis=-1, keepdims=True)
    spread = jnp.mean(center * center, axis=-1, keepdims=True)
    return center * lax.rsqrt(spread + EPSILON) * scale_vec + shift_vec


def matmul(left, right):
    return jnp.dot(left, right, preferred_element_type=F32)


def transposed_times(left, right):
    return lax.dot_general(left, right, (((0,), (0,)), ((), ())), preferred_element_type=F32)


def times_transposed(left, right):
    return lax.dot_general(left, right, (((1,), (1,)), ((), ())), preferred_element_type=F32)


def split_heads(matrix, length):
    return matrix.reshape(-1, length, HEADS, HD)


def attend(queries, keys_in, values_in, allowed):
    scale = queries.shape[-1] ** (-0.5)
    scores = jnp.einsum("blhe,bmhe->bhlm", queries, keys_in, preferred_element_type=F32) * scale
    scores = jnp.where(allowed[:, None], scores, -1e30)
    row_top = jnp.max(scores, axis=-1, keepdims=True)
    raised = jnp.exp(scores - row_top)
    row_total = jnp.sum(raised, axis=-1, keepdims=True)
    softmax_low = (raised / row_total).astype(BF16)
    mixture = jnp.einsum("bhlm,bmhe->blhe", softmax_low, values_in, preferred_element_type=F32)
    return (mixture.astype(BF16), row_top + jnp.log(row_total))


def attend_back(queries, keys_in, values_in, allowed, log_total, grad_mixture):
    scale = queries.shape[-1] ** (-0.5)
    scores = jnp.einsum("blhe,bmhe->bhlm", queries, keys_in, preferred_element_type=F32) * scale
    scores = jnp.where(allowed[:, None], scores, -1e30)
    softmax_rows = jnp.exp(scores - log_total)
    grad_values = jnp.einsum(
        "bhlm,blhe->bmhe", softmax_rows.astype(BF16), grad_mixture, preferred_element_type=F32
    )
    grad_softmax = jnp.einsum(
        "blhe,bmhe->bhlm", grad_mixture, values_in, preferred_element_type=F32
    )
    row_inner = jnp.sum(softmax_rows * grad_softmax, axis=-1, keepdims=True)
    grad_scores = (softmax_rows * (grad_softmax - row_inner)).astype(BF16)
    grad_queries = (
        jnp.einsum("bhlm,bmhe->blhe", grad_scores, keys_in, preferred_element_type=F32) * scale
    )
    grad_keys = (
        jnp.einsum("bhlm,blhe->bmhe", grad_scores, queries, preferred_element_type=F32) * scale
    )
    return (grad_queries.astype(BF16), grad_keys.astype(BF16), grad_values.astype(BF16))


def pack_vectors(vectors, wide_vector):
    flat = jnp.concatenate(list(vectors) + [wide_vector]).astype(F32)
    return jnp.pad(flat, (0, 1024 - flat.size)).reshape(8, 128)


def unpack_vectors(gathered, count, short, long):
    everyone = gathered.shape[0]
    flat = gathered.reshape(everyone, -1)
    rows = flat[:, : count * short].reshape(everyone, count, short).transpose(1, 0, 2)
    return rows.reshape(count, everyone * short), flat[:, count * short : count * short + long].reshape(-1)


def body(
    latents,
    group_inputs,
    latent_images,
    input_images,
    cotangent,
    cross_gain,
    cross_shift,
    source_gain,
    source_shift,
    query_weight,
    keyval_weight,
    cross_out_weight,
    self_gain,
    self_shift,
    self_qkv_weight,
    self_out_weight,
    mlp_gain,
    mlp_shift,
    up_weight,
    up_bias,
    down_weight,
    down_bias,
):
    model_width = latents.shape[1]
    latent_rows = latent_images.reshape(-1, GLAT)
    cross_allowed = latent_rows[:, :, None] == input_images.reshape(-1, GIN)[:, None, :]
    self_allowed = latent_rows[:, :, None] == latent_rows[:, None, :]
    start_rows = latents.astype(F32)
    source_rows = group_inputs.astype(F32)
    vectors = (
        cross_gain,
        cross_shift,
        source_gain,
        source_shift,
        self_gain,
        self_shift,
        mlp_gain,
        mlp_shift,
        down_bias,
    )
    packed = pack_vectors(vectors, up_bias)
    gathered = gather_all(
        (
            packed,
            query_weight,
            keyval_weight,
            cross_out_weight,
            self_qkv_weight,
            self_out_weight,
            down_weight,
            up_weight,
        )
    )
    rows, full_up_bias = unpack_vectors(gathered[0], 9, cross_gain.size, up_bias.size)
    gain_c, shift_c, gain_i, shift_i, gain_s, shift_s, gain_m, shift_m, bias_d = rows
    w_q, w_kv, w_co, w_qkv, w_so, w_down, w_up = [
        member.reshape(-1, member.shape[2]) for member in gathered[1:]
    ]
    lat_low = norm_rows(start_rows, gain_c, shift_c).astype(BF16)
    src_low = norm_rows(source_rows, gain_i, shift_i).astype(BF16)
    queries = matmul(lat_low, w_q).astype(BF16)
    keyvals = matmul(src_low, w_kv).astype(BF16)
    cross_query = split_heads(queries, GLAT)
    cross_keys = split_heads(keyvals[:, :model_width], GIN)
    cross_values = split_heads(keyvals[:, model_width:], GIN)
    cross_mix, cross_lse = attend(cross_query, cross_keys, cross_values, cross_allowed)
    cross_flat = cross_mix.reshape(-1, model_width)
    after_cross = start_rows + matmul(cross_flat, w_co)
    self_low = norm_rows(after_cross, gain_s, shift_s).astype(BF16)
    triple = matmul(self_low, w_qkv).astype(BF16)
    self_query = split_heads(triple[:, :model_width], GLAT)
    self_keys = split_heads(triple[:, model_width : 2 * model_width], GLAT)
    self_values = split_heads(triple[:, 2 * model_width :], GLAT)
    self_mix, self_lse = attend(self_query, self_keys, self_values, self_allowed)
    self_flat = self_mix.reshape(-1, model_width)
    after_self = after_cross + matmul(self_flat, w_so)
    mlp_low = norm_rows(after_self, gain_m, shift_m).astype(BF16)
    hidden_pre = matmul(mlp_low, w_up) + full_up_bias
    activated = jax.nn.gelu(hidden_pre, approximate=False).astype(BF16)
    finished = after_self + matmul(activated, w_down) + bias_d
    grad_down = transposed_times(activated, cotangent)
    grad_down_bias = jnp.sum(cotangent.astype(F32), axis=0)
    grad_active = times_transposed(cotangent, w_down)
    gelu_back = jax.vjp(partial(jax.nn.gelu, approximate=False), hidden_pre)[1]
    grad_hidden = gelu_back(grad_active)[0].astype(BF16)
    grad_up = transposed_times(mlp_low, grad_hidden)
    grad_up_bias = jnp.sum(grad_hidden.astype(F32), axis=0)
    mlp_norm_back = jax.vjp(norm_rows, after_self, gain_m, shift_m)[1]
    grad_rows_mlp, grad_mlp_gain, grad_mlp_shift = mlp_norm_back(
        times_transposed(grad_hidden, w_up)
    )
    grad_after_self = cotangent.astype(F32) + grad_rows_mlp
    grad_self_low = grad_after_self.astype(BF16)
    grad_self_out = transposed_times(self_flat, grad_self_low)
    grad_self_mix = split_heads(times_transposed(grad_self_low, w_so).astype(BF16), GLAT)
    grad_self_query, grad_self_keys, grad_self_values = attend_back(
        self_query, self_keys, self_values, self_allowed, self_lse, grad_self_mix
    )
    grad_triple = jnp.concatenate(
        [
            grad_self_query.reshape(-1, model_width),
            grad_self_keys.reshape(-1, model_width),
            grad_self_values.reshape(-1, model_width),
        ],
        axis=1,
    )
    grad_qkv = transposed_times(self_low, grad_triple)
    self_norm_back = jax.vjp(norm_rows, after_cross, gain_s, shift_s)[1]
    grad_rows_self, grad_self_gain, grad_self_shift = self_norm_back(
        times_transposed(grad_triple, w_qkv)
    )
    grad_after_cross = grad_after_self + grad_rows_self
    grad_cross_low = grad_after_cross.astype(BF16)
    grad_cross_out = transposed_times(cross_flat, grad_cross_low)
    grad_cross_mix = split_heads(times_transposed(grad_cross_low, w_co).astype(BF16), GLAT)
    grad_cross_query, grad_cross_keys, grad_cross_values = attend_back(
        cross_query, cross_keys, cross_values, cross_allowed, cross_lse, grad_cross_mix
    )
    grad_queries = grad_cross_query.reshape(-1, model_width)
    grad_keyvals = jnp.concatenate(
        [grad_cross_keys.reshape(-1, model_width), grad_cross_values.reshape(-1, model_width)],
        axis=1,
    )
    grad_query_weight = transposed_times(lat_low, grad_queries)
    grad_keyval_weight = transposed_times(src_low, grad_keyvals)
    lat_norm_back = jax.vjp(norm_rows, start_rows, gain_c, shift_c)[1]
    grad_start, grad_cross_gain, grad_cross_shift = lat_norm_back(
        times_transposed(grad_queries, w_q)
    )
    src_norm_back = jax.vjp(norm_rows, source_rows, gain_i, shift_i)[1]
    grad_source, grad_source_gain, grad_source_shift = src_norm_back(
        times_transposed(grad_keyvals, w_kv)
    )
    everyone = gathered[0].shape[0]
    vector_grads = jnp.stack(
        [
            grad_cross_gain,
            grad_cross_shift,
            grad_source_gain,
            grad_source_shift,
            grad_self_gain,
            grad_self_shift,
            grad_mlp_gain,
            grad_mlp_shift,
            grad_down_bias,
        ]
    )
    short = cross_gain.size
    flat = jnp.concatenate(
        [
            vector_grads.reshape(9, everyone, short).transpose(1, 0, 2).reshape(everyone, -1),
            grad_up_bias.reshape(everyone, -1),
        ],
        axis=1,
    )
    flat = jnp.pad(flat, ((0, 0), (0, 1024 - flat.shape[1]))).reshape(everyone, 8, 128)
    shares = scatter_all(
        [flat]
        + [
            member.astype(BF16).reshape(everyone, -1, member.shape[1])
            for member in (
                grad_up,
                grad_down,
                grad_self_out,
                grad_qkv,
                grad_cross_out,
                grad_query_weight,
                grad_keyval_weight,
            )
        ]
    )
    small = shares[0].reshape(-1)
    vec = [small[k * short : (k + 1) * short] for k in range(9)]
    own_up_bias = small[9 * short : 9 * short + up_bias.size]
    g_up, g_down, g_so, g_qkv, g_co, g_q, g_kv = shares[1:]
    return (
        finished.astype(BF16),
        (grad_after_cross + grad_start).astype(BF16),
        grad_source.astype(BF16),
        vec[0],
        vec[1],
        vec[2],
        vec[3],
        g_q,
        g_kv,
        g_co,
        vec[4],
        vec[5],
        g_qkv,
        g_so,
        vec[6],
        vec[7],
        g_up,
        own_up_bias,
        g_down,
        vec[8],
    )


def solution(mesh):
    rows = P(("wide", "narrow"), None)
    line = P(("wide", "narrow"))
    return jax.shard_map(
        body,
        mesh=mesh,
        in_specs=(rows,) * 5
        + (line,) * 4
        + (rows,) * 3
        + (line,) * 2
        + (rows,) * 2
        + (line,) * 2
        + (rows, line, rows, line),
        out_specs=(rows,) * 3
        + (line,) * 4
        + (rows,) * 3
        + (line,) * 2
        + (rows,) * 2
        + (line,) * 2
        + (rows, line, rows, line),
        check_vma=False,
    )
```

```python
from functools import partial

import jax
import jax.numpy as jnp
from jax import lax
from jax.experimental import pallas as pl
from jax.experimental.pallas import tpu as pltpu
from jax.sharding import PartitionSpec as P

MESH = pl.DeviceIdType.MESH
BF16 = jnp.bfloat16
F32 = jnp.float32


class Place:
    def __init__(self, wide_size, narrow_size):
        self.wide = lax.axis_index("wide")
        self.narrow = lax.axis_index("narrow")
        self.n_narrow = narrow_size
        self.wide_count = wide_size
        self.columns = wide_size // 2
        self.n_a = 2 if self.columns % 2 == 0 else 1
        self.n_b = self.columns // self.n_a
        self.core = lax.rem(self.wide, 2)
        column = self.wide // 2
        self.a = column // self.n_b
        self.b = lax.rem(column, self.n_b)
        self.coloured = self.n_a == self.n_b

    def index(self, a, b, core):
        return (a * self.n_b + b) * 2 + core

    def sibling(self):
        return self.wide + 1 - 2 * self.core

    def along_a(self, step):
        return self.index(lax.rem(self.a + step, self.n_a), self.b, self.core)

    def along_b(self, step):
        return self.index(self.a, lax.rem(self.b + step, self.n_b), self.core)

    def first_count(self):
        return self.n_b

    def second_count(self):
        return self.n_a

    def first(self, step):
        if not self.coloured:
            return self.along_b(step)
        return jnp.where(self.core == 0, self.along_b(step), self.along_a(step))

    def second(self, step):
        if not self.coloured:
            return self.along_a(step)
        return jnp.where(self.core == 0, self.along_a(step), self.along_b(step))

    def corner(self, first_step, second_step):
        if not self.coloured:
            return self.index(
                lax.rem(self.a + second_step, self.n_a),
                lax.rem(self.b + first_step, self.n_b),
                self.core,
            )
        step_a = jnp.where(self.core == 0, second_step, first_step)
        step_b = jnp.where(self.core == 0, first_step, second_step)
        return self.index(
            lax.rem(self.a + step_a, self.n_a), lax.rem(self.b + step_b, self.n_b), self.core
        )

    def depth(self, step):
        return lax.rem(self.narrow + step, self.n_narrow)

    def greet(self):
        barrier = pltpu.get_barrier_semaphore()
        count = 0
        for step in range(1, self.n_narrow):
            pl.semaphore_signal(
                barrier, inc=1, device_id=(self.wide, self.depth(step)), device_id_type=MESH
            )
            count += 1
        for step in range(1, self.n_b):
            pl.semaphore_signal(
                barrier, inc=1, device_id=(self.along_b(step), self.narrow), device_id_type=MESH
            )
            count += 1
        for step in range(1, self.n_a):
            pl.semaphore_signal(
                barrier, inc=1, device_id=(self.along_a(step), self.narrow), device_id_type=MESH
            )
            count += 1
        pl.semaphore_signal(
            barrier, inc=1, device_id=(self.sibling(), self.narrow), device_id_type=MESH
        )
        pl.semaphore_wait(barrier, count + 1)


class Gather:
    def __init__(self, place, own, full, sems):
        self.place = place
        self.own = own
        self.full = full
        self.send, self.recv = sems
        self.rows = own.shape[0]
        self.pending = []
        p = place
        self.n_z = p.n_narrow - 1
        self.n_1 = (p.first_count() - 1) * p.n_narrow
        self.n_2 = (p.second_count() - 1) * p.first_count()

    def view(self, wide, narrow=None):
        n = self.place.n_narrow
        if narrow is None:
            start, size = wide * n * self.rows, n * self.rows
        else:
            start, size = (wide * n + narrow) * self.rows, self.rows
        return self.full.at[pl.ds(pl.multiple_of(start, self.rows), size), :]

    def copy(self, src, dst, slot, device):
        return pltpu.make_async_remote_copy(
            src_ref=src,
            dst_ref=dst,
            send_sem=self.send.at[slot],
            recv_sem=self.recv.at[slot],
            device_id=device,
            device_id_type=MESH,
        )

    def go(self, copy):
        copy.start()
        self.pending.append(copy)

    def landed(self, view, slot):
        self.copy(view, view, slot, (self.place.sibling(), self.place.narrow)).wait_recv()

    def slot_first(self, step, k):
        return self.n_z + (step - 1) * self.place.n_narrow + k

    def slot_second(self, step, k):
        return self.n_z + self.n_1 + (step - 1) * self.place.first_count() + k

    def slot_sibling(self, k):
        return self.n_z + self.n_1 + self.n_2 + k

    def stage_1(self):
        p = self.place
        for step in range(1, p.n_narrow):
            self.go(
                self.copy(
                    self.own,
                    self.view(p.wide, p.narrow),
                    step - 1,
                    (p.wide, p.depth(step)),
                )
            )
        for step in range(1, p.first_count()):
            self.go(
                self.copy(
                    self.own,
                    self.view(p.wide, p.narrow),
                    self.slot_first(step, 0),
                    (p.first(step), p.narrow),
                )
            )

    def stage_2(self):
        p = self.place
        for step in range(1, p.n_narrow):
            source = p.depth(p.n_narrow - step)
            view = self.view(p.wide, source)
            self.landed(view, step - 1)
            for hop in range(1, p.first_count()):
                self.go(
                    self.copy(view, view, self.slot_first(hop, step), (p.first(hop), p.narrow))
                )
        view = self.view(p.wide)
        for hop in range(1, p.second_count()):
            self.go(self.copy(view, view, self.slot_second(hop, 0), (p.second(hop), p.narrow)))
        self.go(self.copy(view, view, self.slot_sibling(0), (p.sibling(), p.narrow)))

    def stage_3(self):
        p = self.place
        for step in range(1, p.first_count()):
            column = p.first(p.first_count() - step)
            for k in range(p.n_narrow):
                source = p.depth(p.n_narrow - k)
                self.landed(self.view(column, source), self.slot_first(step, k))
            view = self.view(column)
            for hop in range(1, p.second_count()):
                self.go(
                    self.copy(view, view, self.slot_second(hop, step), (p.second(hop), p.narrow))
                )
            self.go(self.copy(view, view, self.slot_sibling(step), (p.sibling(), p.narrow)))

    def stage_4(self):
        p = self.place
        for hop in range(1, p.second_count()):
            back = p.second_count() - hop
            for k in range(p.first_count()):
                column = p.corner((p.first_count() - k) % p.first_count(), back)
                view = self.view(column)
                self.landed(view, self.slot_second(hop, k))
                slot = self.slot_sibling(hop * p.first_count() + k)
                self.go(self.copy(view, view, slot, (p.sibling(), p.narrow)))

    def stage_5(self):
        p = self.place
        for hop in range(p.second_count()):
            for k in range(p.first_count()):
                back_1 = (p.first_count() - k) % p.first_count()
                back_2 = (p.second_count() - hop) % p.second_count()
                if p.coloured:
                    step_a = jnp.where(p.core == 1, back_2, back_1)
                    step_b = jnp.where(p.core == 1, back_1, back_2)
                else:
                    step_a, step_b = back_2, back_1
                column = p.index(
                    lax.rem(p.a + step_a, p.n_a), lax.rem(p.b + step_b, p.n_b), 1 - p.core
                )
                self.landed(self.view(column), self.slot_sibling(hop * p.first_count() + k))

    def drain(self):
        for copy in self.pending:
            copy.wait_send()


def gather_slots(wide_size, narrow_size):
    columns = wide_size // 2
    n_a = 2 if columns % 2 == 0 else 1
    n_b = columns // n_a
    return (narrow_size - 1) + (n_b - 1) * narrow_size + (n_a - 1) * n_b + n_a * n_b


class Scatter:
    def __init__(self, place, grad, out, bufs, sems):
        self.place = place
        self.grad = grad
        self.out = out
        self.held, self.from_sibling, self.from_second, self.from_first, self.from_depth = bufs
        self.send, self.recv, self.local = sems
        self.pending = []
        p = place
        self.n_1 = p.first_count()
        self.n_2 = p.second_count()
        self.blocks = self.n_1 * self.n_2
        self.rows = out.shape[0]

    def view(self, wide):
        size = self.place.n_narrow * self.rows
        return self.grad.at[pl.ds(pl.multiple_of(wide * size, size), size), :]

    def copy(self, src, dst, slot, device):
        return pltpu.make_async_remote_copy(
            src_ref=src,
            dst_ref=dst,
            send_sem=self.send.at[slot],
            recv_sem=self.recv.at[slot],
            device_id=device,
            device_id_type=MESH,
        )

    def go(self, copy):
        copy.start()
        self.pending.append(copy)

    def landed(self, ref, slot):
        self.copy(ref, ref, slot, (self.place.sibling(), self.place.narrow)).wait_recv()

    def loads(self):
        p = self.place
        result = []
        for s in range(self.n_2):
            for f in range(self.n_1):
                block = s * self.n_1 + f
                result.append(
                    pltpu.make_async_copy(
                        self.view(p.corner(f, s)), self.held.at[block], self.local.at[block]
                    )
                )
        return result

    def stage_0(self):
        p = self.place
        for s in range(self.n_2):
            for f in range(self.n_1):
                if p.coloured:
                    step_a = jnp.where(p.core == 1, s, f)
                    step_b = jnp.where(p.core == 1, f, s)
                else:
                    step_a, step_b = s, f
                column = p.index(
                    lax.rem(p.a + step_a, p.n_a), lax.rem(p.b + step_b, p.n_b), 1 - p.core
                )
                block = s * self.n_1 + f
                self.go(
                    self.copy(
                        self.view(column),
                        self.from_sibling.at[block],
                        block,
                        (p.sibling(), p.narrow),
                    )
                )
        for load in self.loads():
            load.start()

    def add(self, block, *others):
        rows = self.rows

        def step(i, carry):
            part = pl.ds(pl.multiple_of(i * rows, rows), rows)
            total = self.held[block, part, :].astype(F32)
            for other in others:
                total = total + other[part, :].astype(F32)
            self.held[block, part, :] = total.astype(self.held.dtype)
            return carry

        lax.fori_loop(0, self.place.n_narrow, step, 0)

    def piece(self, narrow):
        return pl.ds(pl.multiple_of(narrow * self.rows, self.rows), self.rows)

    def stage_1(self):
        p = self.place
        for load in self.loads():
            load.wait()
        for block in range(self.blocks):
            self.landed(self.from_sibling.at[block], block)
        for s in range(self.n_2 - 1, -1, -1):
            for f in range(self.n_1):
                block = s * self.n_1 + f
                self.add(block, self.from_sibling.at[block])
                if s > 0:
                    slot = (s - 1) * self.n_1 + f
                    self.go(
                        self.copy(
                            self.held.at[block],
                            self.from_second.at[slot],
                            self.blocks + slot,
                            (p.second(s), p.narrow),
                        )
                    )

    def stage_2(self):
        p = self.place
        base = self.blocks + (self.n_2 - 1) * self.n_1
        for f in range(self.n_1 - 1, -1, -1):
            slots = [s * self.n_1 + f for s in range(self.n_2 - 1)]
            for slot in slots:
                self.landed(self.from_second.at[slot], self.blocks + slot)
            self.add(f, *[self.from_second.at[slot] for slot in slots])
            if f > 0:
                self.go(
                    self.copy(
                        self.held.at[f],
                        self.from_first.at[f - 1],
                        base + f - 1,
                        (p.first(f), p.narrow),
                    )
                )

    def stage_3(self):
        p = self.place
        first_base = self.blocks + (self.n_2 - 1) * self.n_1
        base = first_base + self.n_1 - 1
        for f in range(1, self.n_1):
            self.landed(self.from_first.at[f - 1], first_base + f - 1)
        self.add(0, *[self.from_first.at[f - 1] for f in range(1, self.n_1)])
        for step in range(1, p.n_narrow):
            self.go(
                self.copy(
                    self.held.at[0, self.piece(p.depth(step)), :],
                    self.from_depth.at[step - 1],
                    base + step - 1,
                    (p.wide, p.depth(step)),
                )
            )

    def stage_4(self):
        p = self.place
        base = self.blocks + (self.n_2 - 1) * self.n_1 + self.n_1 - 1
        for step in range(1, p.n_narrow):
            self.landed(self.from_depth.at[step - 1], base + step - 1)
        total = self.held[0, self.piece(p.narrow), :].astype(F32)
        for step in range(1, p.n_narrow):
            total = total + self.from_depth[step - 1].astype(F32)
        self.out[...] = total

    def drain(self):
        for copy in self.pending:
            copy.wait_send()


def scatter_slots(wide_size, narrow_size):
    columns = wide_size // 2
    n_a = 2 if columns % 2 == 0 else 1
    n_b = columns // n_a
    return n_a * n_b + (n_a - 1) * n_b + (n_b - 1) + (narrow_size - 1)


D = 1024
HEADS = 8
HD = 128
GROUP = 128
EPSILON = 1e-05
SCALE = HD ** (-0.5)
NN = (((1,), (0,)), ((), ()))
NT = (((1,), (1,)), ((), ()))
TN = (((0,), (0,)), ((), ()))

U_Q, U_K, U_V, U_CO, U_SQ, U_SK, U_SV, U_SO, U_D, U_U = 0, 1, 2, 3, 4, 5, 6, 7, 8, 9
UNITS = 16
VECTORS = 16
V_CG, V_CS, V_IG, V_IS, V_SG, V_SS, V_MG, V_MS, V_BD, V_BU = range(10)
(S_LAT, S_SRC, S_Q, S_K, S_V, S_MIX, S_SL, S_SQ, S_SK, S_SV, S_SMIX) = range(11)


def dot(left, right, dims=NN):
    return lax.dot_general(left, right, dims, preferred_element_type=F32)


def for_each(count, step, unroll=1):
    def run(i, carry):
        step(i)
        return carry

    lax.fori_loop(0, count, run, 0, unroll=unroll)


def part(i, size):
    return pl.ds(pl.multiple_of(i * size, size), size)


def gather_units(sizes, shards):
    rows = D // (sizes[0] * sizes[1])
    q, kv, co, qkv, so, down, up = range(7)
    units = [(q, 0, 0), (kv, 0, 0), (kv, 0, 1), (co, 0, 0), (qkv, 0, 0), (qkv, 0, 1), (qkv, 0, 2)]
    units.append((so, 0, 0))
    for i in range(4):
        units.append((down, i * rows, 0))
        units.append((up, 0, i))
    return rows, units


def norm_stats(x):
    mean = jnp.mean(x, axis=-1, keepdims=True)
    center = x - mean
    spread = jnp.mean(center * center, axis=-1, keepdims=True)
    return center, lax.rsqrt(spread + EPSILON)


def group_mask(row_ids, column_ids):
    across = jnp.broadcast_to(row_ids.astype(F32), (GROUP, GROUP)).T
    return across == jnp.broadcast_to(column_ids.astype(F32), (GROUP, GROUP))


def softmax_rows(scores):
    raised = jnp.exp(scores - jnp.max(scores, axis=-1, keepdims=True))
    return raised * (1.0 / jnp.sum(raised, axis=-1, keepdims=True))


def gelu_parts(x):
    half = 0.5 * (1.0 + lax.erf(x * (2.0**-0.5)))
    return x * half, half + x * (jnp.exp(-0.5 * x * x) * ((2.0 * jnp.pi) ** -0.5))


class Ticks:
    def __init__(self, jobs):
        self.jobs = jobs
        self.done = 0
        self.last = len(jobs) + 3

    def one(self):
        t = self.done
        if t >= self.last:
            return
        for back, stage in ((3, "stage_5"), (2, "stage_4"), (1, "stage_3"), (0, "stage_2"), (-1, "stage_1")):
            if 0 <= t - back < len(self.jobs):
                getattr(self.jobs[t - back], stage)()
        self.done = t + 1

    def until(self, job):
        while self.done < job + 4:
            self.one()


def forward_kernel(sizes, *refs):
    (vec_shard, *rest) = refs
    shards, rest = rest[:7], rest[7:]
    latents, inputs, cot, lat_ids, in_ids = rest[:5]
    full, vec_full, finished, kept, kept_f, g_mlp, small = rest[5:12]
    (
        staged,
        vec_staged,
        vec_all,
        vec,
        pool,
        fpool,
        send,
        recv,
        vsend,
        vrecv,
        sem_stage,
        sem_own,
        sem_in,
        sem_w,
        sem_keep,
        sem_keep_f,
        sem_g,
    ) = rest[12:]
    place = Place(*sizes)
    rows, units = gather_units(sizes, shards)
    mine = place.wide * place.n_narrow + place.narrow

    LAT, INP, LLOW, SLOW, Q, K, V, MIX = 0, 1, 2, 3, 8, 9, 10, 11
    W0 = 4
    W1 = 12
    ML, COT = 2, 3

    copies_in = [
        pltpu.make_async_copy(latents, pool.at[LAT], sem_in.at[0]),
        pltpu.make_async_copy(inputs, pool.at[INP], sem_in.at[1]),
    ]
    stage_in = []
    for u, (k, r0, c0) in enumerate(units):
        source = shards[k].at[pl.ds(r0, rows), pl.ds(c0 * D, D)]
        stage_in.append(pltpu.make_async_copy(source, staged.at[u], sem_stage.at[u]))
    stage_in.append(pltpu.make_async_copy(vec_shard, vec_staged, sem_stage.at[UNITS]))
    own_out = [
        pltpu.make_async_copy(staged.at[u], full.at[u, part(mine, rows), :], sem_own.at[u])
        for u in range(UNITS)
    ]
    own_out.append(
        pltpu.make_async_copy(vec_staged, vec_full.at[part(mine, VECTORS), :], sem_own.at[UNITS])
    )
    for copy in stage_in[::-1]:
        copy.start()
    for copy in copies_in:
        copy.start()
    place.greet()
    jobs = [Gather(place, vec_shard, vec_full, (vsend, vrecv))]
    for u, (k, r0, c0) in enumerate(units):
        source = shards[k].at[pl.ds(r0, rows), pl.ds(c0 * D, D)]
        jobs.append(Gather(place, source, full.at[u], (send.at[u], recv.at[u])))
    ticks = Ticks(jobs)
    jobs[0].stage_1()
    for i in range(UNITS, -1, -1):
        stage_in[i].wait()
        own_out[i].start()
    for i in range(UNITS, -1, -1):
        own_out[i].wait()

    def load(unit, slot):
        return pltpu.make_async_copy(full.at[unit], pool.at[slot], sem_w.at[slot])

    def fetch(unit, slot):
        ticks.until(unit + 1)
        load(unit, slot).start()

    def keep(slot, index):
        return pltpu.make_async_copy(pool.at[slot], kept.at[index], sem_keep.at[index])

    def keep_f(slot, index):
        return pltpu.make_async_copy(fpool.at[slot], kept_f.at[index], sem_keep_f.at[index])

    def vector(k, columns=slice(None)):
        return vec[k : k + 1, columns]

    ticks.until(0)
    copy = pltpu.make_async_copy(vec_full, vec_all, sem_in.at[2])
    copy.start()
    copy.wait()
    lane_groups = D // 128
    per = place.wide_count * place.n_narrow // lane_groups
    for g in range(lane_groups):
        total = vec_all[pl.ds(g * per * VECTORS, VECTORS), :]
        for j in range(1, per):
            total = total + vec_all[pl.ds((g * per + j) * VECTORS, VECTORS), :]
        vec[:, g * 128 : (g + 1) * 128] = total

    def norm_low(read, slot, gain, shift):
        def step(i):
            sl = part(i, 64)
            center, rate = norm_stats(read(sl))
            pool[slot, sl, :] = (center * rate * vector(gain) + vector(shift)).astype(BF16)

        for_each(16, step)

    def product(out, left, weight):
        def step(j):
            sl = part(j, 512)
            pool[out, :, sl] = dot(pool[left], pool[weight, :, sl]).astype(BF16)

        for_each(2, step)

    def attend(q, k, v, out, ids, groups):
        def step(g):
            sl = part(g, GROUP)
            mask = group_mask(lat_ids[pl.ds(g, 1), :], ids[pl.ds(g, 1), :])
            for h in range(HEADS):
                hs = slice(h * HD, (h + 1) * HD)
                scores = dot(pool[q, sl, hs], pool[k, sl, hs], NT) * SCALE
                weights = softmax_rows(jnp.where(mask, scores, -1e30)).astype(BF16)
                pool[out, sl, hs] = dot(weights, pool[v, sl, hs]).astype(BF16)

        lo, hi = groups

        def run(g, carry):
            step(g)
            return carry

        lax.fori_loop(lo, hi, run, 0)

    copies_in[0].wait()
    norm_low(lambda sl: pool[LAT, sl, :].astype(F32), LLOW, V_CG, V_CS)
    keep(LLOW, S_LAT).start()
    fetch(U_Q, W0)
    copies_in[1].wait()
    norm_low(lambda sl: pool[INP, sl, :].astype(F32), SLOW, V_IG, V_IS)
    keep(SLOW, S_SRC).start()
    load(U_Q, W0).wait()
    product(Q, LLOW, W0)
    keep(Q, S_Q).start()
    fetch(U_K, W0 + 1)
    load(U_K, W0 + 1).wait()
    product(K, SLOW, W0 + 1)
    keep(K, S_K).start()
    fetch(U_V, W0 + 2)
    load(U_V, W0 + 2).wait()
    product(V, SLOW, W0 + 2)
    keep(V, S_V).start()
    attend(Q, K, V, MIX, in_ids, (0, 4))
    fetch(U_CO, W0 + 3)
    attend(Q, K, V, MIX, in_ids, (4, 8))
    keep(MIX, S_MIX).start()
    load(U_CO, W0 + 3).wait()

    def cross_out(j):
        sl = part(j, 512)
        fpool[0, :, sl] = pool[LAT, :, sl].astype(F32) + dot(pool[MIX], pool[W0 + 3, :, sl])

    for_each(2, cross_out)
    keep_f(0, 0).start()
    fetch(U_SQ, W1)
    norm_low(lambda sl: fpool[0, sl, :], LAT, V_SG, V_SS)
    keep(LAT, S_SL).start()
    keep(Q, S_Q).wait()
    keep(K, S_K).wait()
    keep(V, S_V).wait()
    for offset, (slot, index, before) in enumerate(((Q, S_SQ, 0), (K, S_SK, 0), (V, S_SV, 0))):
        load(U_SQ + offset, W1 + offset).wait()
        product(slot, LAT, W1 + offset)
        keep(slot, index).start()
        fetch(U_SQ + offset + 1, W1 + offset + 1)
    keep(MIX, S_MIX).wait()
    attend(Q, K, V, MIX, lat_ids, (0, 4))
    ticks.one()
    attend(Q, K, V, MIX, lat_ids, (4, 8))
    keep(MIX, S_SMIX).start()
    load(U_SO, W1 + 3).wait()

    def self_out(j):
        sl = part(j, 512)
        fpool[1, :, sl] = fpool[0, :, sl] + dot(pool[MIX], pool[W1 + 3, :, sl])

    for_each(2, self_out)
    keep_f(1, 1).start()
    keep(LLOW, S_LAT).wait()
    keep(SLOW, S_SRC).wait()
    cot_in = pltpu.make_async_copy(cot, pool.at[COT], sem_in.at[3])
    cot_in.start()
    norm_low(lambda sl: fpool[1, sl, :], ML, V_MG, V_MS)
    cot_in.wait()
    for slot, index in ((LAT, S_SL), (Q, S_SQ), (K, S_SK), (V, S_SV), (MIX, S_SMIX)):
        keep(slot, index).wait()
    keep_f(1, 1).wait()

    ACT, GH = 8, 9
    GD, GU = 10, 12
    C = 512
    R = 256
    small[...] = jnp.zeros_like(small)

    def spread(chunk):
        i, h = divmod(chunk, 2)
        down, up = W0 + 2 * (i % 2), W0 + 2 * (i % 2) + 1
        cols = pl.ds(h * C, C)
        fpool[3, :, 0:C] = dot(pool[ML], pool[up, :, cols])
        fpool[3, :, C : 2 * C] = dot(pool[COT], pool[down, cols, :], NT)

    def bend(chunk, sl):
        i, h = divmod(chunk, 2)
        cols = pl.ds(h * C, C)
        value, slope = gelu_parts(fpool[3, sl, 0:C] + vec[V_BU + i : V_BU + i + 1, cols])
        grad = (slope * fpool[3, sl, C : 2 * C]).astype(BF16)
        out = pl.ds((chunk % 2) * C, C)
        pool[ACT, sl, out] = value.astype(BF16)
        pool[GH, sl, out] = grad
        small[i : i + 1, cols] += jnp.sum(grad.astype(F32), axis=0, keepdims=True)

    def fold(chunk, sl):
        i, h = divmod(chunk, 2)
        down, up = W0 + 2 * (i % 2), W0 + 2 * (i % 2) + 1
        cols = pl.ds(h * C, C)
        out = pl.ds((chunk % 2) * C, C)
        fpool[1, sl, :] += dot(pool[ACT, sl, out], pool[down, cols, :])
        grad = dot(pool[GH, sl, out], pool[up, :, cols], NT)
        if chunk == 0:
            fpool[2, sl, :] = grad
        else:
            fpool[2, sl, :] += grad

    def grad_out(i):
        return [
            pltpu.make_async_copy(pool.at[GD + i % 2], g_mlp.at[2 * i], sem_g.at[2 * i]),
            pltpu.make_async_copy(pool.at[GU + i % 2], g_mlp.at[2 * i + 1], sem_g.at[2 * i + 1]),
        ]

    def weigh(chunk):
        i, h = divmod(chunk, 2)
        cols = pl.ds(h * C, C)
        out = pl.ds((chunk % 2) * C, C)
        pool[GD + i % 2, cols, :] = dot(pool[ACT, :, out], pool[COT], TN).astype(BF16)
        pool[GU + i % 2, :, cols] = dot(pool[ML], pool[GH, :, out], TN).astype(BF16)

    for chunk in range(8):
        i, h = divmod(chunk, 2)
        if h == 0:
            fetch(U_D + 2 * i, W0 + 2 * (i % 2))
            fetch(U_U + 2 * i, W0 + 2 * (i % 2) + 1)
            load(U_D + 2 * i, W0 + 2 * (i % 2)).wait()
            load(U_U + 2 * i, W0 + 2 * (i % 2) + 1).wait()
        else:
            ticks.one()
        spread(chunk)

        def rows_step(r):
            sl = part(r, R)
            if chunk > 0:
                fold(chunk - 1, sl)
            bend(chunk, sl)

        for_each(D // R, rows_step)
        if h == 0 and i >= 2:
            for copy in grad_out(i - 2):
                copy.wait()
        weigh(chunk)
        if h == 1:
            for copy in grad_out(i):
                copy.start()

    def last(r):
        sl = part(r, R)
        fold(7, sl)
        pool[ML, sl, :] = (fpool[1, sl, :] + vector(V_BD)).astype(BF16)

    for_each(D // R, last)
    done = pltpu.make_async_copy(pool.at[ML], finished, sem_in.at[4])
    done.start()
    keep_f(2, 2).start()
    done.wait()
    keep_f(2, 2).wait()
    keep_f(0, 0).wait()
    for i in (2, 3):
        for copy in grad_out(i):
            copy.wait()
    while ticks.done < ticks.last:
        ticks.one()
    for job in jobs:
        job.drain()


def run_forward(vec_shard, shards, latents, inputs, cot, lat_ids, in_ids):
    sizes = (lax.axis_size("wide"), lax.axis_size("narrow"))
    everyone = sizes[0] * sizes[1]
    rows = D // everyone
    slots = gather_slots(*sizes)
    any_spec = pl.BlockSpec(memory_space=pl.ANY)
    vmem_spec = pl.BlockSpec(memory_space=pltpu.VMEM)
    dma = pltpu.SemaphoreType.DMA
    return pl.pallas_call(
        partial(forward_kernel, sizes),
        out_shape=[
            jax.ShapeDtypeStruct((UNITS, D, D), BF16),
            jax.ShapeDtypeStruct((everyone * VECTORS, 128), F32),
            jax.ShapeDtypeStruct((D, D), BF16),
            jax.ShapeDtypeStruct((11, D, D), BF16),
            jax.ShapeDtypeStruct((3, D, D), F32),
            jax.ShapeDtypeStruct((8, D, D), BF16),
            jax.ShapeDtypeStruct((8, D), F32),
        ],
        in_specs=[any_spec] * 11 + [vmem_spec] * 2,
        out_specs=[any_spec] * 6 + [vmem_spec],
        scratch_shapes=[
            pltpu.VMEM((UNITS, rows, D), BF16),
            pltpu.VMEM((VECTORS, 128), F32),
            pltpu.VMEM((everyone * VECTORS, 128), F32),
            pltpu.VMEM((VECTORS, D), F32),
            pltpu.VMEM((16, D, D), BF16),
            pltpu.VMEM((4, D, D), F32),
            dma((UNITS, slots)),
            dma((UNITS, slots)),
            dma((slots,)),
            dma((slots,)),
            dma((UNITS + 1,)),
            dma((UNITS + 1,)),
            dma((5,)),
            dma((16,)),
            dma((11,)),
            dma((3,)),
            dma((8,)),
        ],
        compiler_params=pltpu.CompilerParams(
            collective_id=0, has_side_effects=True, vmem_limit_bytes=63 * 2**20
        ),
        name="gather_forward",
    )(vec_shard, *shards, latents, inputs, cot, lat_ids, in_ids)


def scatter_units():
    units = []
    for i in range(4):
        units.append((1, 2 * i, 0, 1, i, 0))
        units.append((1, 2 * i + 1, 0, 2, 0, i))
    units.append((2, None, 0, 3, 0, 0))
    for c in range(3):
        units.append((3, None, c, 4, 0, c))
    units.append((4, None, 0, 5, 0, 0))
    units.append((5, None, 0, 6, 0, 0))
    for c in range(2):
        units.append((6, None, c, 7, 0, c))
    return units


def scatter_kernel(sizes, count, n_out, *refs):
    grads, outs = refs[:count], refs[count : count + n_out]
    rest = refs[count + n_out :]
    small_bufs, big_bufs = rest[:5], rest[5:10]
    send, recv, local = rest[10:]
    place = Place(*sizes)
    place.greet()
    rows = D // (sizes[0] * sizes[1])
    jobs = [Scatter(place, grads[0], outs[0], small_bufs, (send.at[0], recv.at[0], local.at[0]))]
    for i, (k, lead, c0, p, r, c) in enumerate(scatter_units(), 1):
        grad = grads[k] if lead is None else grads[k].at[lead]
        grad = grad.at[:, pl.ds(c0 * D, D)]
        out = outs[p].at[pl.ds(r * rows, rows), pl.ds(c * D, D)]
        bufs = tuple(buf.at[i - 1] for buf in big_bufs)
        jobs.append(Scatter(place, grad, out, bufs, (send.at[i], recv.at[i], local.at[i])))
    total = len(jobs)
    for t in range(total + 4):
        for back, stage in enumerate(("stage_0", "stage_1", "stage_2", "stage_3", "stage_4")):
            if 0 <= t - back < total:
                getattr(jobs[t - back], stage)()
    for job in jobs:
        job.drain()


def scatter_all(grads):
    sizes = (lax.axis_size("wide"), lax.axis_size("narrow"))
    everyone = sizes[0] * sizes[1]
    rows = D // everyone
    widths = ((4 * rows, D), (rows, 4 * D), (rows, D), (rows, 3 * D), (rows, D), (rows, D), (rows, 2 * D))
    outs = [jax.ShapeDtypeStruct((VECTORS, 128), F32)]
    outs += [jax.ShapeDtypeStruct(shape, F32) for shape in widths]
    columns = sizes[0] // 2
    n_2 = 2 if columns % 2 == 0 else 1
    n_1 = columns // n_2
    count = len(grads)
    n = sizes[1]

    def bufs(lead, high, width, kind):
        return [
            pltpu.VMEM(lead + (columns, n * high, width), kind),
            pltpu.VMEM(lead + (columns, n * high, width), kind),
            pltpu.VMEM(lead + ((n_2 - 1) * n_1, n * high, width), kind),
            pltpu.VMEM(lead + (n_1 - 1, n * high, width), kind),
            pltpu.VMEM(lead + (n - 1, high, width), kind),
        ]

    slots = scatter_slots(*sizes)
    total = UNITS + 1
    return pl.pallas_call(
        partial(scatter_kernel, sizes, count, len(outs)),
        out_shape=outs,
        in_specs=[pl.BlockSpec(memory_space=pl.ANY)] * count,
        out_specs=[pl.BlockSpec(memory_space=pltpu.VMEM)] * len(outs),
        scratch_shapes=bufs((), VECTORS, 128, F32)
        + bufs((UNITS,), rows, D, BF16)
        + [
            pltpu.SemaphoreType.DMA((total, slots)),
            pltpu.SemaphoreType.DMA((total, slots)),
            pltpu.SemaphoreType.DMA((total, columns)),
        ],
        compiler_params=pltpu.CompilerParams(
            collective_id=1, has_side_effects=True, vmem_limit_bytes=63 * 2**20
        ),
        name="scatter_gradients",
    )(*grads)
def norm_rows(values, scale_vec, shift_vec):
    center = values - jnp.mean(values, axis=-1, keepdims=True)
    spread = jnp.mean(center * center, axis=-1, keepdims=True)
    return center * lax.rsqrt(spread + EPSILON) * scale_vec + shift_vec


def matmul(left, right):
    return jnp.dot(left, right, preferred_element_type=F32)


def transposed_times(left, right):
    return lax.dot_general(left, right, (((0,), (0,)), ((), ())), preferred_element_type=F32)


def times_transposed(left, right):
    return lax.dot_general(left, right, (((1,), (1,)), ((), ())), preferred_element_type=F32)


def split_heads(matrix, length):
    return matrix.reshape(-1, length, HEADS, HD)


def attend_back(queries, keys_in, values_in, allowed, grad_mixture):
    scale = queries.shape[-1] ** (-0.5)
    scores = jnp.einsum("blhe,bmhe->bhlm", queries, keys_in, preferred_element_type=F32) * scale
    scores = jnp.where(allowed[:, None], scores, -1e30)
    weights = jax.nn.softmax(scores, axis=-1)
    grad_values = jnp.einsum(
        "bhlm,blhe->bmhe", weights.astype(BF16), grad_mixture, preferred_element_type=F32
    )
    grad_softmax = jnp.einsum(
        "blhe,bmhe->bhlm", grad_mixture, values_in, preferred_element_type=F32
    )
    row_inner = jnp.sum(weights * grad_softmax, axis=-1, keepdims=True)
    grad_scores = (weights * (grad_softmax - row_inner)).astype(BF16)
    grad_queries = (
        jnp.einsum("bhlm,bmhe->blhe", grad_scores, keys_in, preferred_element_type=F32) * scale
    )
    grad_keys = (
        jnp.einsum("bhlm,blhe->bmhe", grad_scores, queries, preferred_element_type=F32) * scale
    )
    return (grad_queries.astype(BF16), grad_keys.astype(BF16), grad_values.astype(BF16))


def body(
    latents,
    group_inputs,
    latent_images,
    input_images,
    cotangent,
    cross_gain,
    cross_shift,
    source_gain,
    source_shift,
    query_weight,
    keyval_weight,
    cross_out_weight,
    self_gain,
    self_shift,
    self_qkv_weight,
    self_out_weight,
    mlp_gain,
    mlp_shift,
    up_weight,
    up_bias,
    down_weight,
    down_bias,
):
    model_width = latents.shape[1]
    latent_rows = latent_images.reshape(-1, GROUP)
    cross_allowed = latent_rows[:, :, None] == input_images.reshape(-1, GROUP)[:, None, :]
    self_allowed = latent_rows[:, :, None] == latent_rows[:, None, :]
    start_rows = latents.astype(F32)
    source_rows = group_inputs.astype(F32)
    sizes = (lax.axis_size("wide"), lax.axis_size("narrow"))
    everyone = sizes[0] * sizes[1]
    short = cross_gain.shape[0]
    per = 128 // short
    me = lax.axis_index(("wide", "narrow"))
    vectors = (
        cross_gain,
        cross_shift,
        source_gain,
        source_shift,
        self_gain,
        self_shift,
        mlp_gain,
        mlp_shift,
        down_bias,
    )
    stacked = jnp.concatenate(
        [jnp.stack(vectors), up_bias.reshape(4, short), jnp.zeros((3, short), BF16)]
    ).astype(F32)
    lane = lax.broadcasted_iota(jnp.int32, (VECTORS, 128), 1) // short
    packed = jnp.where(lane == lax.rem(me, per), jnp.tile(stacked, (1, per)), 0.0)
    up_chunks = up_weight.reshape(short, everyone, 4, short).transpose(0, 2, 1, 3).reshape(short, -1)
    full, vec_full, finished, kept, kept_f, g_mlp, small = run_forward(
        packed,
        (
            query_weight,
            keyval_weight,
            cross_out_weight,
            self_qkv_weight,
            self_out_weight,
            down_weight,
            up_chunks,
        ),
        latents,
        group_inputs,
        cotangent,
        latent_images.reshape(-1, GROUP),
        input_images.reshape(-1, GROUP),
    )
    lanes = vec_full.reshape(D // 128, per, VECTORS, 128).sum(axis=1)
    rows = lanes.transpose(1, 0, 2).reshape(VECTORS, D)
    gain_c, shift_c, gain_i, shift_i, gain_s, shift_s, gain_m, shift_m, bias_d = rows[:9]
    w_q, w_co, w_so = full[U_Q], full[U_CO], full[U_SO]
    w_kv = jnp.concatenate([full[U_K], full[U_V]], axis=1)
    w_qkv = jnp.concatenate([full[U_SQ], full[U_SK], full[U_SV]], axis=1)
    lat_low, src_low, self_low = kept[S_LAT], kept[S_SRC], kept[S_SL]
    cross_query, cross_keys, cross_values = [split_heads(kept[k], GROUP) for k in (S_Q, S_K, S_V)]
    self_query, self_keys, self_values = [split_heads(kept[k], GROUP) for k in (S_SQ, S_SK, S_SV)]
    cross_flat, self_flat = kept[S_MIX], kept[S_SMIX]
    after_cross, after_self, grad_mlp_in = kept_f[0], kept_f[1], kept_f[2]
    grad_down_bias = jnp.sum(cotangent.astype(F32), axis=0)
    mlp_norm_back = jax.vjp(norm_rows, after_self, gain_m, shift_m)[1]
    grad_rows_mlp, grad_mlp_gain, grad_mlp_shift = mlp_norm_back(
        grad_mlp_in
    )
    grad_after_self = cotangent.astype(F32) + grad_rows_mlp
    grad_self_low = grad_after_self.astype(BF16)
    grad_self_out = transposed_times(self_flat, grad_self_low)
    grad_self_mix = split_heads(times_transposed(grad_self_low, w_so).astype(BF16), GROUP)
    grad_self_query, grad_self_keys, grad_self_values = attend_back(
        self_query, self_keys, self_values, self_allowed, grad_self_mix
    )
    grad_triple = jnp.concatenate(
        [
            grad_self_query.reshape(-1, model_width),
            grad_self_keys.reshape(-1, model_width),
            grad_self_values.reshape(-1, model_width),
        ],
        axis=1,
    )
    grad_qkv = transposed_times(self_low, grad_triple)
    self_norm_back = jax.vjp(norm_rows, after_cross, gain_s, shift_s)[1]
    grad_rows_self, grad_self_gain, grad_self_shift = self_norm_back(
        times_transposed(grad_triple, w_qkv)
    )
    grad_after_cross = grad_after_self + grad_rows_self
    grad_cross_low = grad_after_cross.astype(BF16)
    grad_cross_out = transposed_times(cross_flat, grad_cross_low)
    grad_cross_mix = split_heads(times_transposed(grad_cross_low, w_co).astype(BF16), GROUP)
    grad_cross_query, grad_cross_keys, grad_cross_values = attend_back(
        cross_query, cross_keys, cross_values, cross_allowed, grad_cross_mix
    )
    grad_queries = grad_cross_query.reshape(-1, model_width)
    grad_keyvals = jnp.concatenate(
        [grad_cross_keys.reshape(-1, model_width), grad_cross_values.reshape(-1, model_width)],
        axis=1,
    )
    grad_query_weight = transposed_times(lat_low, grad_queries)
    grad_keyval_weight = transposed_times(src_low, grad_keyvals)
    lat_norm_back = jax.vjp(norm_rows, start_rows, gain_c, shift_c)[1]
    grad_start, grad_cross_gain, grad_cross_shift = lat_norm_back(
        times_transposed(grad_queries, w_q)
    )
    src_norm_back = jax.vjp(norm_rows, source_rows, gain_i, shift_i)[1]
    grad_source, grad_source_gain, grad_source_shift = src_norm_back(
        times_transposed(grad_keyvals, w_kv)
    )
    vector_grads = jnp.concatenate(
        [
            jnp.stack(
                [
                    grad_cross_gain,
                    grad_cross_shift,
                    grad_source_gain,
                    grad_source_shift,
                    grad_self_gain,
                    grad_self_shift,
                    grad_mlp_gain,
                    grad_mlp_shift,
                    grad_down_bias,
                ]
            ),
            small[:4],
            jnp.zeros((3, D), F32),
        ]
    )
    flat = vector_grads.reshape(VECTORS, D // 128, 1, 128).transpose(1, 2, 0, 3)
    flat = jnp.broadcast_to(flat, (D // 128, per, VECTORS, 128)).reshape(-1, 128)
    shares = scatter_all(
        [
            flat,
            g_mlp,
            grad_self_out.astype(BF16),
            grad_qkv.astype(BF16),
            grad_cross_out.astype(BF16),
            grad_query_weight.astype(BF16),
            grad_keyval_weight.astype(BF16),
        ]
    )
    vec = lax.dynamic_slice_in_dim(shares[0], lax.rem(me, per) * short, short, axis=1)
    own_up_bias = vec[9:13].reshape(-1)
    g_down, g_up, g_so, g_qkv, g_co, g_q, g_kv = shares[1:]
    g_up = g_up.reshape(short, 4, everyone, short).transpose(0, 2, 1, 3).reshape(short, -1)
    return (
        finished,
        (grad_after_cross + grad_start).astype(BF16),
        grad_source.astype(BF16),
        vec[0],
        vec[1],
        vec[2],
        vec[3],
        g_q,
        g_kv,
        g_co,
        vec[4],
        vec[5],
        g_qkv,
        g_so,
        vec[6],
        vec[7],
        g_up,
        own_up_bias,
        g_down,
        vec[8],
    )


def solution(mesh):
    rows = P(("wide", "narrow"), None)
    line = P(("wide", "narrow"))
    return jax.shard_map(
        body,
        mesh=mesh,
        in_specs=(rows,) * 5
        + (line,) * 4
        + (rows,) * 3
        + (line,) * 2
        + (rows,) * 2
        + (line,) * 2
        + (rows, line, rows, line),
        out_specs=(rows,) * 3
        + (line,) * 4
        + (rows,) * 3
        + (line,) * 2
        + (rows,) * 2
        + (line,) * 2
        + (rows, line, rows, line),
        check_vma=False,
    )
```

```python
from functools import partial

import jax
import jax.numpy as jnp
from jax import lax
from jax.experimental import pallas as pl
from jax.experimental.pallas import tpu as pltpu
from jax.sharding import PartitionSpec as P

MESH = pl.DeviceIdType.MESH
BF16 = jnp.bfloat16
F32 = jnp.float32


class Place:
    def __init__(self, wide_size, narrow_size):
        self.wide = lax.axis_index("wide")
        self.narrow = lax.axis_index("narrow")
        self.n_narrow = narrow_size
        self.wide_count = wide_size
        self.columns = wide_size // 2
        self.n_a = 2 if self.columns % 2 == 0 else 1
        self.n_b = self.columns // self.n_a
        self.core = lax.rem(self.wide, 2)
        column = self.wide // 2
        self.a = column // self.n_b
        self.b = lax.rem(column, self.n_b)
        self.coloured = self.n_a == self.n_b

    def index(self, a, b, core):
        return (a * self.n_b + b) * 2 + core

    def sibling(self):
        return self.wide + 1 - 2 * self.core

    def along_a(self, step):
        return self.index(lax.rem(self.a + step, self.n_a), self.b, self.core)

    def along_b(self, step):
        return self.index(self.a, lax.rem(self.b + step, self.n_b), self.core)

    def first_count(self):
        return self.n_b

    def second_count(self):
        return self.n_a

    def first(self, step):
        if not self.coloured:
            return self.along_b(step)
        return jnp.where(self.core == 0, self.along_b(step), self.along_a(step))

    def second(self, step):
        if not self.coloured:
            return self.along_a(step)
        return jnp.where(self.core == 0, self.along_a(step), self.along_b(step))

    def corner(self, first_step, second_step):
        if not self.coloured:
            return self.index(
                lax.rem(self.a + second_step, self.n_a),
                lax.rem(self.b + first_step, self.n_b),
                self.core,
            )
        step_a = jnp.where(self.core == 0, second_step, first_step)
        step_b = jnp.where(self.core == 0, first_step, second_step)
        return self.index(
            lax.rem(self.a + step_a, self.n_a), lax.rem(self.b + step_b, self.n_b), self.core
        )

    def depth(self, step):
        return lax.rem(self.narrow + step, self.n_narrow)

    def greet(self):
        barrier = pltpu.get_barrier_semaphore()
        count = 0
        for step in range(1, self.n_narrow):
            pl.semaphore_signal(
                barrier, inc=1, device_id=(self.wide, self.depth(step)), device_id_type=MESH
            )
            count += 1
        for step in range(1, self.n_b):
            pl.semaphore_signal(
                barrier, inc=1, device_id=(self.along_b(step), self.narrow), device_id_type=MESH
            )
            count += 1
        for step in range(1, self.n_a):
            pl.semaphore_signal(
                barrier, inc=1, device_id=(self.along_a(step), self.narrow), device_id_type=MESH
            )
            count += 1
        pl.semaphore_signal(
            barrier, inc=1, device_id=(self.sibling(), self.narrow), device_id_type=MESH
        )
        pl.semaphore_wait(barrier, count + 1)


class Gather:
    def __init__(self, place, own, full, sems):
        self.place = place
        self.own = own
        self.full = full
        self.send, self.recv = sems
        self.rows = own.shape[0]
        self.pending = []
        p = place
        self.n_z = p.n_narrow - 1
        self.n_1 = (p.first_count() - 1) * p.n_narrow
        self.n_2 = (p.second_count() - 1) * p.first_count()

    def view(self, wide, narrow=None):
        n = self.place.n_narrow
        if narrow is None:
            start, size = wide * n * self.rows, n * self.rows
        else:
            start, size = (wide * n + narrow) * self.rows, self.rows
        return self.full.at[pl.ds(pl.multiple_of(start, self.rows), size), :]

    def copy(self, src, dst, slot, device):
        return pltpu.make_async_remote_copy(
            src_ref=src,
            dst_ref=dst,
            send_sem=self.send.at[slot],
            recv_sem=self.recv.at[slot],
            device_id=device,
            device_id_type=MESH,
        )

    def go(self, copy):
        copy.start()
        self.pending.append(copy)

    def landed(self, view, slot):
        self.copy(view, view, slot, (self.place.sibling(), self.place.narrow)).wait_recv()

    def slot_first(self, step, k):
        return self.n_z + (step - 1) * self.place.n_narrow + k

    def slot_second(self, step, k):
        return self.n_z + self.n_1 + (step - 1) * self.place.first_count() + k

    def slot_sibling(self, k):
        return self.n_z + self.n_1 + self.n_2 + k

    def stage_1(self):
        p = self.place
        for step in range(1, p.n_narrow):
            self.go(
                self.copy(
                    self.own,
                    self.view(p.wide, p.narrow),
                    step - 1,
                    (p.wide, p.depth(step)),
                )
            )
        for step in range(1, p.first_count()):
            self.go(
                self.copy(
                    self.own,
                    self.view(p.wide, p.narrow),
                    self.slot_first(step, 0),
                    (p.first(step), p.narrow),
                )
            )

    def stage_2(self):
        p = self.place
        for step in range(1, p.n_narrow):
            source = p.depth(p.n_narrow - step)
            view = self.view(p.wide, source)
            self.landed(view, step - 1)
            for hop in range(1, p.first_count()):
                self.go(
                    self.copy(view, view, self.slot_first(hop, step), (p.first(hop), p.narrow))
                )
        view = self.view(p.wide)
        for hop in range(1, p.second_count()):
            self.go(self.copy(view, view, self.slot_second(hop, 0), (p.second(hop), p.narrow)))
        self.go(self.copy(view, view, self.slot_sibling(0), (p.sibling(), p.narrow)))

    def stage_3(self):
        p = self.place
        for step in range(1, p.first_count()):
            column = p.first(p.first_count() - step)
            for k in range(p.n_narrow):
                source = p.depth(p.n_narrow - k)
                self.landed(self.view(column, source), self.slot_first(step, k))
            view = self.view(column)
            for hop in range(1, p.second_count()):
                self.go(
                    self.copy(view, view, self.slot_second(hop, step), (p.second(hop), p.narrow))
                )
            self.go(self.copy(view, view, self.slot_sibling(step), (p.sibling(), p.narrow)))

    def stage_4(self):
        p = self.place
        for hop in range(1, p.second_count()):
            back = p.second_count() - hop
            for k in range(p.first_count()):
                column = p.corner((p.first_count() - k) % p.first_count(), back)
                view = self.view(column)
                self.landed(view, self.slot_second(hop, k))
                slot = self.slot_sibling(hop * p.first_count() + k)
                self.go(self.copy(view, view, slot, (p.sibling(), p.narrow)))

    def stage_5(self):
        p = self.place
        for hop in range(p.second_count()):
            for k in range(p.first_count()):
                back_1 = (p.first_count() - k) % p.first_count()
                back_2 = (p.second_count() - hop) % p.second_count()
                if p.coloured:
                    step_a = jnp.where(p.core == 1, back_2, back_1)
                    step_b = jnp.where(p.core == 1, back_1, back_2)
                else:
                    step_a, step_b = back_2, back_1
                column = p.index(
                    lax.rem(p.a + step_a, p.n_a), lax.rem(p.b + step_b, p.n_b), 1 - p.core
                )
                self.landed(self.view(column), self.slot_sibling(hop * p.first_count() + k))

    def drain(self):
        for copy in self.pending:
            copy.wait_send()


def gather_slots(wide_size, narrow_size):
    columns = wide_size // 2
    n_a = 2 if columns % 2 == 0 else 1
    n_b = columns // n_a
    return (narrow_size - 1) + (n_b - 1) * narrow_size + (n_a - 1) * n_b + n_a * n_b


class Scatter:
    def __init__(self, place, grad, out, bufs, sems):
        self.place = place
        self.grad = grad
        self.out = out
        self.held, self.from_sibling, self.from_second, self.from_first, self.from_depth = bufs
        self.send, self.recv, self.local = sems
        self.pending = []
        p = place
        self.n_1 = p.first_count()
        self.n_2 = p.second_count()
        self.blocks = self.n_1 * self.n_2
        self.rows = out.shape[0]

    def view(self, wide):
        size = self.place.n_narrow * self.rows
        return self.grad.at[pl.ds(pl.multiple_of(wide * size, size), size), :]

    def copy(self, src, dst, slot, device):
        return pltpu.make_async_remote_copy(
            src_ref=src,
            dst_ref=dst,
            send_sem=self.send.at[slot],
            recv_sem=self.recv.at[slot],
            device_id=device,
            device_id_type=MESH,
        )

    def go(self, copy):
        copy.start()
        self.pending.append(copy)

    def landed(self, ref, slot):
        self.copy(ref, ref, slot, (self.place.sibling(), self.place.narrow)).wait_recv()

    def loads(self):
        p = self.place
        result = []
        for s in range(self.n_2):
            for f in range(self.n_1):
                block = s * self.n_1 + f
                result.append(
                    pltpu.make_async_copy(
                        self.view(p.corner(f, s)), self.held.at[block], self.local.at[block]
                    )
                )
        return result

    def stage_0(self):
        p = self.place
        for s in range(self.n_2):
            for f in range(self.n_1):
                if p.coloured:
                    step_a = jnp.where(p.core == 1, s, f)
                    step_b = jnp.where(p.core == 1, f, s)
                else:
                    step_a, step_b = s, f
                column = p.index(
                    lax.rem(p.a + step_a, p.n_a), lax.rem(p.b + step_b, p.n_b), 1 - p.core
                )
                block = s * self.n_1 + f
                self.go(
                    self.copy(
                        self.view(column),
                        self.from_sibling.at[block],
                        block,
                        (p.sibling(), p.narrow),
                    )
                )
        for load in self.loads():
            load.start()

    def add(self, block, *others):
        rows = self.rows

        def step(i, carry):
            part = pl.ds(pl.multiple_of(i * rows, rows), rows)
            total = self.held[block, part, :]
            for other in others:
                total = total + other[part, :]
            self.held[block, part, :] = total
            return carry

        lax.fori_loop(0, self.place.n_narrow, step, 0)

    def piece(self, narrow):
        return pl.ds(pl.multiple_of(narrow * self.rows, self.rows), self.rows)

    def stage_1(self):
        p = self.place
        for load in self.loads():
            load.wait()
        for block in range(self.blocks):
            self.landed(self.from_sibling.at[block], block)
        for s in range(self.n_2 - 1, -1, -1):
            for f in range(self.n_1):
                block = s * self.n_1 + f
                self.add(block, self.from_sibling.at[block])
                if s > 0:
                    slot = (s - 1) * self.n_1 + f
                    self.go(
                        self.copy(
                            self.held.at[block],
                            self.from_second.at[slot],
                            self.blocks + slot,
                            (p.second(s), p.narrow),
                        )
                    )

    def stage_2(self):
        p = self.place
        base = self.blocks + (self.n_2 - 1) * self.n_1
        for f in range(self.n_1 - 1, -1, -1):
            slots = [s * self.n_1 + f for s in range(self.n_2 - 1)]
            for slot in slots:
                self.landed(self.from_second.at[slot], self.blocks + slot)
            self.add(f, *[self.from_second.at[slot] for slot in slots])
            if f > 0:
                self.go(
                    self.copy(
                        self.held.at[f],
                        self.from_first.at[f - 1],
                        base + f - 1,
                        (p.first(f), p.narrow),
                    )
                )

    def stage_3(self):
        p = self.place
        first_base = self.blocks + (self.n_2 - 1) * self.n_1
        base = first_base + self.n_1 - 1
        for f in range(1, self.n_1):
            self.landed(self.from_first.at[f - 1], first_base + f - 1)
        self.add(0, *[self.from_first.at[f - 1] for f in range(1, self.n_1)])
        for step in range(1, p.n_narrow):
            self.go(
                self.copy(
                    self.held.at[0, self.piece(p.depth(step)), :],
                    self.from_depth.at[step - 1],
                    base + step - 1,
                    (p.wide, p.depth(step)),
                )
            )

    def stage_4(self):
        p = self.place
        base = self.blocks + (self.n_2 - 1) * self.n_1 + self.n_1 - 1
        for step in range(1, p.n_narrow):
            self.landed(self.from_depth.at[step - 1], base + step - 1)
        total = self.held[0, self.piece(p.narrow), :].astype(F32)
        for step in range(1, p.n_narrow):
            total = total + self.from_depth[step - 1].astype(F32)
        self.out[...] = total

    def drain(self):
        for copy in self.pending:
            copy.wait_send()


def scatter_slots(wide_size, narrow_size):
    columns = wide_size // 2
    n_a = 2 if columns % 2 == 0 else 1
    n_b = columns // n_a
    return n_a * n_b + (n_a - 1) * n_b + (n_b - 1) + (narrow_size - 1)


D = 1024
HEADS = 8
HD = 128
GROUP = 128
EPSILON = 1e-05
SCALE = HD ** (-0.5)
NN = (((1,), (0,)), ((), ()))
NT = (((1,), (1,)), ((), ()))
TN = (((0,), (0,)), ((), ()))

U_Q, U_K, U_V, U_CO, U_SQ, U_SK, U_SV, U_SO, U_D, U_U = 0, 1, 2, 3, 4, 5, 6, 7, 8, 9
UNITS = 16
VECTORS = 16
V_CG, V_CS, V_IG, V_IS, V_SG, V_SS, V_MG, V_MS, V_BD, V_BU = range(10)
(S_LAT, S_SRC, S_Q, S_K, S_V, S_MIX, S_SL, S_SQ, S_SK, S_SV, S_SMIX) = range(11)


def dot(left, right, dims=NN):
    return lax.dot_general(left, right, dims, preferred_element_type=F32)


def for_each(count, step, unroll=1):
    def run(i, carry):
        step(i)
        return carry

    lax.fori_loop(0, count, run, 0, unroll=unroll)


def part(i, size):
    return pl.ds(pl.multiple_of(i * size, size), size)


def gather_units(sizes, shards):
    rows = D // (sizes[0] * sizes[1])
    q, kv, co, qkv, so, down, up = range(7)
    units = [(q, 0, 0), (kv, 0, 0), (kv, 0, 1), (co, 0, 0), (qkv, 0, 0), (qkv, 0, 1), (qkv, 0, 2)]
    units.append((so, 0, 0))
    for i in range(4):
        units.append((down, i * rows, 0))
        units.append((up, 0, i))
    return rows, units


def norm_stats(x):
    mean = jnp.mean(x, axis=-1, keepdims=True)
    center = x - mean
    spread = jnp.mean(center * center, axis=-1, keepdims=True)
    return center, lax.rsqrt(spread + EPSILON)


def group_mask(row_ids, column_ids):
    across = jnp.broadcast_to(row_ids.astype(F32), (GROUP, GROUP)).T
    return across == jnp.broadcast_to(column_ids.astype(F32), (GROUP, GROUP))


def softmax_rows(scores):
    raised = jnp.exp(scores - jnp.max(scores, axis=-1, keepdims=True))
    return raised * (1.0 / jnp.sum(raised, axis=-1, keepdims=True))


def gelu_parts(x):
    half = 0.5 * (1.0 + lax.erf(x * (2.0**-0.5)))
    return x * half, half + x * (jnp.exp(-0.5 * x * x) * ((2.0 * jnp.pi) ** -0.5))


class Ticks:
    def __init__(self, jobs):
        self.jobs = jobs
        self.done = 0
        self.last = len(jobs) + 3

    def one(self):
        t = self.done
        if t >= self.last:
            return
        for back, stage in ((3, "stage_5"), (2, "stage_4"), (1, "stage_3"), (0, "stage_2"), (-1, "stage_1")):
            if 0 <= t - back < len(self.jobs):
                getattr(self.jobs[t - back], stage)()
        self.done = t + 1

    def until(self, job):
        while self.done < job + 4:
            self.one()


def forward_kernel(sizes, *refs):
    (vec_shard, *rest) = refs
    shards, rest = rest[:7], rest[7:]
    latents, inputs, cot, lat_ids, in_ids = rest[:5]
    full, vec_full, finished, kept, kept_f, g_mlp, small, vec = rest[5:13]
    (
        staged,
        vec_staged,
        vec_all,
        pool,
        fpool,
        send,
        recv,
        vsend,
        vrecv,
        sem_stage,
        sem_own,
        sem_in,
        sem_w,
        sem_keep,
        sem_keep_f,
        sem_g,
    ) = rest[13:]
    place = Place(*sizes)
    rows, units = gather_units(sizes, shards)
    mine = place.wide * place.n_narrow + place.narrow

    LAT, INP, LLOW, SLOW, Q, K, V, MIX = 0, 1, 2, 3, 8, 9, 10, 11
    W0 = 4
    W1 = 12
    ML, COT = 2, 3

    copies_in = [
        pltpu.make_async_copy(latents, pool.at[LAT], sem_in.at[0]),
        pltpu.make_async_copy(inputs, pool.at[INP], sem_in.at[1]),
    ]
    stage_in = []
    for u, (k, r0, c0) in enumerate(units):
        source = shards[k].at[pl.ds(r0, rows), pl.ds(c0 * D, D)]
        stage_in.append(pltpu.make_async_copy(source, staged.at[u], sem_stage.at[u]))
    stage_in.append(pltpu.make_async_copy(vec_shard, vec_staged, sem_stage.at[UNITS]))
    own_out = [
        pltpu.make_async_copy(staged.at[u], full.at[u, part(mine, rows), :], sem_own.at[u])
        for u in range(UNITS)
    ]
    own_out.append(
        pltpu.make_async_copy(vec_staged, vec_full.at[part(mine, VECTORS), :], sem_own.at[UNITS])
    )
    for copy in stage_in[::-1]:
        copy.start()
    for copy in copies_in:
        copy.start()
    place.greet()
    jobs = [Gather(place, vec_shard, vec_full, (vsend, vrecv))]
    for u, (k, r0, c0) in enumerate(units):
        source = shards[k].at[pl.ds(r0, rows), pl.ds(c0 * D, D)]
        jobs.append(Gather(place, source, full.at[u], (send.at[u], recv.at[u])))
    ticks = Ticks(jobs)
    jobs[0].stage_1()
    for i in range(UNITS, -1, -1):
        stage_in[i].wait()
        own_out[i].start()
    for i in range(UNITS, -1, -1):
        own_out[i].wait()

    def load(unit, slot):
        return pltpu.make_async_copy(full.at[unit], pool.at[slot], sem_w.at[slot])

    def fetch(unit, slot):
        ticks.until(unit + 1)
        load(unit, slot).start()

    def keep(slot, index):
        return pltpu.make_async_copy(pool.at[slot], kept.at[index], sem_keep.at[index])

    def keep_f(slot, index):
        return pltpu.make_async_copy(fpool.at[slot], kept_f.at[index], sem_keep_f.at[index])

    def vector(k, columns=slice(None)):
        return vec[k : k + 1, columns]

    ticks.until(0)
    copy = pltpu.make_async_copy(vec_full, vec_all, sem_in.at[2])
    copy.start()
    copy.wait()
    lane_groups = D // 128
    per = place.wide_count * place.n_narrow // lane_groups
    for g in range(lane_groups):
        total = vec_all[pl.ds(g * per * VECTORS, VECTORS), :]
        for j in range(1, per):
            total = total + vec_all[pl.ds((g * per + j) * VECTORS, VECTORS), :]
        vec[:, g * 128 : (g + 1) * 128] = total

    def norm_low(read, slot, gain, shift):
        def step(i):
            sl = part(i, 64)
            center, rate = norm_stats(read(sl))
            pool[slot, sl, :] = (center * rate * vector(gain) + vector(shift)).astype(BF16)

        for_each(16, step)

    def product(out, left, weight):
        def step(j):
            sl = part(j, 512)
            pool[out, :, sl] = dot(pool[left], pool[weight, :, sl]).astype(BF16)

        for_each(2, step)

    def attend(q, k, v, out, ids, groups):
        def step(g):
            sl = part(g, GROUP)
            mask = group_mask(lat_ids[pl.ds(g, 1), :], ids[pl.ds(g, 1), :])
            for h in range(HEADS):
                hs = slice(h * HD, (h + 1) * HD)
                scores = dot(pool[q, sl, hs], pool[k, sl, hs], NT) * SCALE
                weights = softmax_rows(jnp.where(mask, scores, -1e30)).astype(BF16)
                pool[out, sl, hs] = dot(weights, pool[v, sl, hs]).astype(BF16)

        lo, hi = groups

        def run(g, carry):
            step(g)
            return carry

        lax.fori_loop(lo, hi, run, 0)

    copies_in[0].wait()
    norm_low(lambda sl: pool[LAT, sl, :].astype(F32), LLOW, V_CG, V_CS)
    keep(LLOW, S_LAT).start()
    fetch(U_Q, W0)
    copies_in[1].wait()
    norm_low(lambda sl: pool[INP, sl, :].astype(F32), SLOW, V_IG, V_IS)
    keep(SLOW, S_SRC).start()
    load(U_Q, W0).wait()
    product(Q, LLOW, W0)
    keep(Q, S_Q).start()
    fetch(U_K, W0 + 1)
    load(U_K, W0 + 1).wait()
    product(K, SLOW, W0 + 1)
    keep(K, S_K).start()
    fetch(U_V, W0 + 2)
    load(U_V, W0 + 2).wait()
    product(V, SLOW, W0 + 2)
    keep(V, S_V).start()
    attend(Q, K, V, MIX, in_ids, (0, 4))
    fetch(U_CO, W0 + 3)
    attend(Q, K, V, MIX, in_ids, (4, 8))
    keep(MIX, S_MIX).start()
    load(U_CO, W0 + 3).wait()

    def cross_out(j):
        sl = part(j, 512)
        fpool[0, :, sl] = pool[LAT, :, sl].astype(F32) + dot(pool[MIX], pool[W0 + 3, :, sl])

    for_each(2, cross_out)
    keep_f(0, 0).start()
    fetch(U_SQ, W1)
    norm_low(lambda sl: fpool[0, sl, :], LAT, V_SG, V_SS)
    keep(LAT, S_SL).start()
    keep(Q, S_Q).wait()
    keep(K, S_K).wait()
    keep(V, S_V).wait()
    for offset, (slot, index, before) in enumerate(((Q, S_SQ, 0), (K, S_SK, 0), (V, S_SV, 0))):
        load(U_SQ + offset, W1 + offset).wait()
        product(slot, LAT, W1 + offset)
        keep(slot, index).start()
        fetch(U_SQ + offset + 1, W1 + offset + 1)
    keep(MIX, S_MIX).wait()
    attend(Q, K, V, MIX, lat_ids, (0, 4))
    ticks.one()
    attend(Q, K, V, MIX, lat_ids, (4, 8))
    keep(MIX, S_SMIX).start()
    load(U_SO, W1 + 3).wait()

    def self_out(j):
        sl = part(j, 512)
        fpool[1, :, sl] = fpool[0, :, sl] + dot(pool[MIX], pool[W1 + 3, :, sl])

    for_each(2, self_out)
    keep_f(1, 1).start()
    keep(LLOW, S_LAT).wait()
    keep(SLOW, S_SRC).wait()
    cot_in = pltpu.make_async_copy(cot, pool.at[COT], sem_in.at[3])
    cot_in.start()
    norm_low(lambda sl: fpool[1, sl, :], ML, V_MG, V_MS)
    cot_in.wait()
    for slot, index in ((LAT, S_SL), (Q, S_SQ), (K, S_SK), (V, S_SV), (MIX, S_SMIX)):
        keep(slot, index).wait()
    keep_f(1, 1).wait()

    ACT, GH = 8, 9
    GD, GU = 10, 12
    C = 512
    R = 256
    small[...] = jnp.zeros_like(small)

    def spread(chunk):
        i, h = divmod(chunk, 2)
        down, up = W0 + 2 * (i % 2), W0 + 2 * (i % 2) + 1
        cols = pl.ds(h * C, C)
        fpool[3, :, 0:C] = dot(pool[ML], pool[up, :, cols])
        fpool[3, :, C : 2 * C] = dot(pool[COT], pool[down, cols, :], NT)

    def bend(chunk, sl):
        i, h = divmod(chunk, 2)
        cols = pl.ds(h * C, C)
        value, slope = gelu_parts(fpool[3, sl, 0:C] + vec[V_BU + i : V_BU + i + 1, cols])
        grad = (slope * fpool[3, sl, C : 2 * C]).astype(BF16)
        out = pl.ds((chunk % 2) * C, C)
        pool[ACT, sl, out] = value.astype(BF16)
        pool[GH, sl, out] = grad
        small[i : i + 1, cols] += jnp.sum(grad.astype(F32), axis=0, keepdims=True)

    def fold(chunk, sl):
        i, h = divmod(chunk, 2)
        down, up = W0 + 2 * (i % 2), W0 + 2 * (i % 2) + 1
        cols = pl.ds(h * C, C)
        out = pl.ds((chunk % 2) * C, C)
        fpool[1, sl, :] += dot(pool[ACT, sl, out], pool[down, cols, :])
        grad = dot(pool[GH, sl, out], pool[up, :, cols], NT)
        if chunk == 0:
            fpool[2, sl, :] = grad
        else:
            fpool[2, sl, :] += grad

    def grad_out(i):
        return [
            pltpu.make_async_copy(pool.at[GD + i % 2], g_mlp.at[2 * i], sem_g.at[2 * i]),
            pltpu.make_async_copy(pool.at[GU + i % 2], g_mlp.at[2 * i + 1], sem_g.at[2 * i + 1]),
        ]

    def weigh(chunk):
        i, h = divmod(chunk, 2)
        cols = pl.ds(h * C, C)
        out = pl.ds((chunk % 2) * C, C)
        pool[GD + i % 2, cols, :] = dot(pool[ACT, :, out], pool[COT], TN).astype(BF16)
        pool[GU + i % 2, :, cols] = dot(pool[ML], pool[GH, :, out], TN).astype(BF16)

    for chunk in range(8):
        i, h = divmod(chunk, 2)
        if h == 0:
            fetch(U_D + 2 * i, W0 + 2 * (i % 2))
            fetch(U_U + 2 * i, W0 + 2 * (i % 2) + 1)
            load(U_D + 2 * i, W0 + 2 * (i % 2)).wait()
            load(U_U + 2 * i, W0 + 2 * (i % 2) + 1).wait()
        else:
            ticks.one()
        spread(chunk)

        def rows_step(r):
            sl = part(r, R)
            if chunk > 0:
                fold(chunk - 1, sl)
            bend(chunk, sl)

        for_each(D // R, rows_step)
        if h == 0 and i >= 2:
            for copy in grad_out(i - 2):
                copy.wait()
        weigh(chunk)
        if h == 1:
            for copy in grad_out(i):
                copy.start()

    def last(r):
        sl = part(r, R)
        fold(7, sl)
        pool[ML, sl, :] = (fpool[1, sl, :] + vector(V_BD)).astype(BF16)

    for_each(D // R, last)
    done = pltpu.make_async_copy(pool.at[ML], finished, sem_in.at[4])
    done.start()
    keep_f(2, 2).start()
    done.wait()
    keep_f(2, 2).wait()
    keep_f(0, 0).wait()
    for i in (2, 3):
        for copy in grad_out(i):
            copy.wait()
    while ticks.done < ticks.last:
        ticks.one()
    for job in jobs:
        job.drain()


def run_forward(vec_shard, shards, latents, inputs, cot, lat_ids, in_ids):
    sizes = (lax.axis_size("wide"), lax.axis_size("narrow"))
    everyone = sizes[0] * sizes[1]
    rows = D // everyone
    slots = gather_slots(*sizes)
    any_spec = pl.BlockSpec(memory_space=pl.ANY)
    vmem_spec = pl.BlockSpec(memory_space=pltpu.VMEM)
    dma = pltpu.SemaphoreType.DMA
    return pl.pallas_call(
        partial(forward_kernel, sizes),
        out_shape=[
            jax.ShapeDtypeStruct((UNITS, D, D), BF16),
            jax.ShapeDtypeStruct((everyone * VECTORS, 128), F32),
            jax.ShapeDtypeStruct((D, D), BF16),
            jax.ShapeDtypeStruct((11, D, D), BF16),
            jax.ShapeDtypeStruct((3, D, D), F32),
            jax.ShapeDtypeStruct((8, D, D), BF16),
            jax.ShapeDtypeStruct((8, D), F32),
            jax.ShapeDtypeStruct((VECTORS, D), F32),
        ],
        in_specs=[any_spec] * 11 + [vmem_spec] * 2,
        out_specs=[any_spec] * 6 + [vmem_spec] * 2,
        scratch_shapes=[
            pltpu.VMEM((UNITS, rows, D), BF16),
            pltpu.VMEM((VECTORS, 128), F32),
            pltpu.VMEM((everyone * VECTORS, 128), F32),
            pltpu.VMEM((16, D, D), BF16),
            pltpu.VMEM((4, D, D), F32),
            dma((UNITS, slots)),
            dma((UNITS, slots)),
            dma((slots,)),
            dma((slots,)),
            dma((UNITS + 1,)),
            dma((UNITS + 1,)),
            dma((5,)),
            dma((16,)),
            dma((11,)),
            dma((3,)),
            dma((8,)),
        ],
        compiler_params=pltpu.CompilerParams(
            collective_id=0, has_side_effects=True, vmem_limit_bytes=63 * 2**20
        ),
        name="gather_forward",
    )(vec_shard, *shards, latents, inputs, cot, lat_ids, in_ids)


HELD = 6
NEAR = 3
(G_SO, G_SQ, G_SK, G_SV, G_CO, G_Q, G_K, G_V) = range(8)


def scatter_targets():
    targets = []
    for i in range(4):
        targets.append((0, i, 0))
        targets.append((1, 0, i))
    targets.append((2, 0, 0))
    for c in range(3):
        targets.append((3, 0, c))
    targets += [(4, 0, 0), (5, 0, 0), (6, 0, 0), (6, 0, 1)]
    return targets


class Sums:
    STAGES = ("stage_0", "stage_1", "stage_2", "stage_3", "stage_4")

    def __init__(self, jobs, credit, place):
        self.jobs = jobs
        self.credit = credit
        self.place = place
        self.stage = [0] * len(jobs)
        self.started = 0
        self.drained = 0
        self.waits = {}

    def one(self, start=True):
        big = len(self.jobs) - 1
        running = [j for j in range(self.started) if self.stage[j] < 5]
        if start and self.started < len(self.jobs):
            j = self.started
            for copy in self.waits.pop(j, ()):
                copy.wait()
            if j < big and j >= NEAR:
                pl.semaphore_wait(self.credit, 1)
            if j < big and j >= HELD:
                self.jobs[j - HELD].drain()
                self.drained = j - HELD + 1
            running.append(j)
            self.started += 1
        for j in running[::-1]:
            getattr(self.jobs[j], self.STAGES[self.stage[j]])()
            if self.stage[j] == 1 and j + NEAR < big:
                pl.semaphore_signal(
                    self.credit,
                    inc=1,
                    device_id=(self.place.sibling(), self.place.narrow),
                    device_id_type=MESH,
                )
            self.stage[j] += 1

    def finish(self):
        while self.started < len(self.jobs) or self.stage[-1] < 5:
            self.one()
        for job in self.jobs[self.drained :]:
            job.drain()


def backward_kernel(sizes, *refs):
    (full, vec, kept, kept_f, g_mlp, small, latents, inputs, cot, lat_ids, in_ids) = refs[:11]
    latent_grad, input_grad, g_att, vec_sent, vec_out, *outs = refs[11:23]
    (
        pool,
        fpool,
        vacc,
        vflat,
        held,
        near,
        from_second,
        from_first,
        from_depth,
        vheld,
        vnear,
        vsecond,
        vfirst,
        vdepth,
        send,
        recv,
        local,
        credit,
        sem_p,
        sem_f,
        sem_g,
        sem_o,
    ) = refs[23:]
    place = Place(*sizes)
    rows = D // (sizes[0] * sizes[1])
    A, B, C, DD, E, F, G, S1, S2 = range(9)

    def load(source, slot):
        return pltpu.make_async_copy(source, pool.at[slot], sem_p.at[slot])

    def load_f(index, slot):
        return pltpu.make_async_copy(kept_f.at[index], fpool.at[slot], sem_f.at[slot])

    first = [
        load_f(1, 0),
        load_f(2, 1),
        load(cot, DD),
        load(full.at[U_SO], C),
        load(kept.at[S_SMIX], B),
        load(kept.at[S_SQ], E),
        load(kept.at[S_SK], F),
        load(kept.at[S_SV], G),
    ]
    for copy in first:
        copy.start()
    place.greet()

    jobs = []
    for i, (p, r, c) in enumerate(scatter_targets()):
        grad = g_mlp.at[i] if i < 8 else g_att.at[i - 8]
        out = outs[p].at[pl.ds(r * rows, rows), pl.ds(c * D, D)]
        bufs = (
            held.at[i % HELD],
            near.at[i % NEAR],
            from_second.at[i],
            from_first.at[i],
            from_depth.at[i],
        )
        jobs.append(Scatter(place, grad, out, bufs, (send.at[i], recv.at[i], local.at[i])))
    jobs.append(
        Scatter(
            place,
            vec_sent,
            vec_out,
            (vheld, vnear, vsecond, vfirst, vdepth),
            (send.at[UNITS], recv.at[UNITS], local.at[UNITS]),
        )
    )
    sums = Sums(jobs, credit, place)
    sums.one()
    vacc[...] = jnp.zeros_like(vacc)
    sums.one()

    def gather_rows(k, value):
        vacc[k] += jnp.sum(value.reshape(-1, 8, D), axis=0)

    def norm_back(read_x, grad_slot, gain, shift, write):
        def step(i):
            sl = part(i, 64)
            center, rate = norm_stats(read_x(sl))
            normal = center * rate
            grad = fpool[grad_slot, sl, :]
            gather_rows(gain, grad * normal)
            gather_rows(shift, grad)
            grad = grad * vec[gain : gain + 1, :]
            mean_1 = jnp.mean(grad, axis=-1, keepdims=True)
            mean_2 = jnp.mean(grad * normal, axis=-1, keepdims=True)
            write(sl, rate * (grad - mean_1 - normal * mean_2))

        for lo, hi in ((0, 8), (8, 16)):

            def run(i, carry):
                step(i)
                return carry

            lax.fori_loop(lo, hi, run, 0)
            sums.one(start=sums.started < limit[0])

    limit = [8]

    def tick():
        sums.one(start=sums.started < limit[0])

    staging = [S1, S2]
    saved = [None, None]

    def weight_grad(index, left, right):
        turn = index % 2
        if saved[turn] is not None and saved[turn] in sums.waits:
            for copy in sums.waits.pop(saved[turn]):
                copy.wait()
        slot = staging[turn]

        def step(j):
            sl = part(j, 512)
            pool[slot, :, sl] = dot(pool[left], pool[right, :, sl], TN).astype(BF16)

        for_each(2, step)
        copy = pltpu.make_async_copy(pool.at[slot], g_att.at[index], sem_g.at[index])
        copy.start()
        sums.waits[8 + index] = (copy,)
        saved[turn] = 8 + index
        limit[0] = 8 + index + 1

    def back_product(out, left, weight):
        def step(j):
            sl = part(j, 512)
            pool[out, :, sl] = dot(pool[left], pool[weight, sl, :], NT).astype(BF16)

        for_each(2, step)

    def back_sum(out, left, weight, fresh):
        def step(j):
            sl = part(j, 512)
            value = dot(pool[left], pool[weight, sl, :], NT)
            if fresh:
                fpool[out, :, sl] = value
            else:
                fpool[out, :, sl] += value

        for_each(2, step)

    def attend_back(q, k, v, grad, ids):
        def step(g, carry):
            sl = part(g, GROUP)
            mask = group_mask(lat_ids[pl.ds(g, 1), :], ids[pl.ds(g, 1), :])
            for h in range(HEADS):
                hs = slice(h * HD, (h + 1) * HD)
                qb, kb, vb, gb = pool[q, sl, hs], pool[k, sl, hs], pool[v, sl, hs], pool[grad, sl, hs]
                weights = softmax_rows(jnp.where(mask, dot(qb, kb, NT) * SCALE, -1e30))
                slope = dot(gb, vb, NT)
                inner = jnp.sum(weights * slope, axis=-1, keepdims=True)
                slope = (weights * (slope - inner)).astype(BF16)
                pool[v, sl, hs] = dot(weights.astype(BF16), gb, TN).astype(BF16)
                pool[q, sl, hs] = (dot(slope, kb) * SCALE).astype(BF16)
                pool[k, sl, hs] = (dot(slope, qb, TN) * SCALE).astype(BF16)
            return carry

        for lo in range(0, 8, 2):
            lax.fori_loop(lo, lo + 2, step, 0)
            tick()

    for copy in first[:3]:
        copy.wait()

    def after_self(sl, grad):
        cot_rows = pool[DD, sl, :].astype(F32)
        gather_rows(V_BD, cot_rows)
        total = cot_rows + grad
        fpool[2, sl, :] = total
        pool[A, sl, :] = total.astype(BF16)

    norm_back(lambda sl: fpool[0, sl, :], 1, V_MG, V_MS, after_self)
    load_f(0, 0).start()

    for copy in first[3:]:
        copy.wait()
    weight_grad(G_SO, B, A)
    load(kept.at[S_SL], B).start()
    back_product(DD, A, C)
    load(full.at[U_SQ], A).start()
    load(full.at[U_SK], C).start()
    tick()
    attend_back(E, F, G, DD, lat_ids)
    load(full.at[U_SV], DD).start()
    load(kept.at[S_SL], B).wait()
    for index, slot, weight, unit in ((G_SQ, E, A, U_SQ), (G_SK, F, C, U_SK), (G_SV, G, DD, U_SV)):
        weight_grad(index, B, slot)
        load(full.at[unit], weight).wait()
        back_sum(1, slot, weight, index == G_SQ)
        tick()
        if index == G_SQ:
            load(kept.at[S_Q], E).start()
            load(full.at[U_CO], A).start()
        elif index == G_SK:
            load(kept.at[S_K], F).start()
        else:
            load(kept.at[S_V], G).start()
            load(kept.at[S_MIX], B).start()
    load_f(0, 0).wait()

    def after_cross(sl, grad):
        total = fpool[2, sl, :] + grad
        fpool[2, sl, :] = total
        pool[C, sl, :] = total.astype(BF16)

    norm_back(lambda sl: fpool[0, sl, :], 1, V_SG, V_SS, after_cross)

    load(kept.at[S_MIX], B).wait()
    weight_grad(G_CO, B, C)
    load(kept.at[S_LAT], B).start()
    load(full.at[U_CO], A).wait()
    back_product(DD, C, A)
    load(full.at[U_Q], A).start()
    load(kept.at[S_SRC], C).start()
    tick()
    load(kept.at[S_Q], E).wait()
    load(kept.at[S_K], F).wait()
    load(kept.at[S_V], G).wait()
    attend_back(E, F, G, DD, in_ids)
    load(full.at[U_K], DD).start()
    load(kept.at[S_LAT], B).wait()
    weight_grad(G_Q, B, E)
    load(latents, B).start()
    load(full.at[U_Q], A).wait()
    back_sum(1, E, A, True)
    load(full.at[U_V], A).start()
    tick()
    load(kept.at[S_SRC], C).wait()
    weight_grad(G_K, C, F)
    tick()
    weight_grad(G_V, C, G)
    load(inputs, C).start()
    tick()
    load(full.at[U_K], DD).wait()
    back_sum(0, F, DD, True)
    load(full.at[U_V], A).wait()
    back_sum(0, G, A, False)
    load(latents, B).wait()

    def latent_out(sl, grad):
        pool[E, sl, :] = (fpool[2, sl, :] + grad).astype(BF16)

    norm_back(lambda sl: pool[B, sl, :].astype(F32), 1, V_CG, V_CS, latent_out)
    done_1 = pltpu.make_async_copy(pool.at[E], latent_grad, sem_o.at[0])
    done_1.start()
    load(inputs, C).wait()

    def input_out(sl, grad):
        pool[F, sl, :] = grad.astype(BF16)

    norm_back(lambda sl: pool[C, sl, :].astype(F32), 0, V_IG, V_IS, input_out)
    done_2 = pltpu.make_async_copy(pool.at[F], input_grad, sem_o.at[1])
    done_2.start()

    lane_groups = D // 128
    per = sizes[0] * sizes[1] // lane_groups
    for k in range(9):
        vacc[k, 0:1, :] = jnp.sum(vacc[k], axis=0, keepdims=True)
    for g in range(lane_groups):
        lanes = slice(g * 128, (g + 1) * 128)
        block = [vacc[k, 0:1, lanes] for k in range(9)]
        block += [small[0:4, lanes], jnp.zeros((3, 128), F32)]
        block = jnp.concatenate(block, axis=0)

        def put(j, carry):
            vflat[part(g * per + j, VECTORS), :] = block
            return carry

        lax.fori_loop(0, per, put, 0)
    copy = pltpu.make_async_copy(vflat, vec_sent, sem_o.at[2])
    copy.start()
    copy.wait()
    limit[0] = len(jobs)
    sums.finish()
    done_1.wait()
    done_2.wait()


def run_backward(full, vec, kept, kept_f, g_mlp, small, latents, inputs, cot, lat_ids, in_ids):
    sizes = (lax.axis_size("wide"), lax.axis_size("narrow"))
    everyone = sizes[0] * sizes[1]
    rows = D // everyone
    columns = sizes[0] // 2
    n_2 = 2 if columns % 2 == 0 else 1
    n_1 = columns // n_2
    n = sizes[1]
    widths = ((4 * rows, D), (rows, 4 * D), (rows, D), (rows, 3 * D), (rows, D), (rows, D), (rows, 2 * D))
    any_spec = pl.BlockSpec(memory_space=pl.ANY)
    vmem_spec = pl.BlockSpec(memory_space=pltpu.VMEM)
    dma = pltpu.SemaphoreType.DMA
    slots = scatter_slots(*sizes)
    total = UNITS + 1
    return pl.pallas_call(
        partial(backward_kernel, sizes),
        out_shape=[
            jax.ShapeDtypeStruct((D, D), BF16),
            jax.ShapeDtypeStruct((D, D), BF16),
            jax.ShapeDtypeStruct((8, D, D), BF16),
            jax.ShapeDtypeStruct((everyone * VECTORS, 128), F32),
            jax.ShapeDtypeStruct((VECTORS, 128), F32),
        ]
        + [jax.ShapeDtypeStruct(shape, F32) for shape in widths],
        in_specs=[any_spec, vmem_spec]
        + [any_spec] * 3
        + [vmem_spec]
        + [any_spec] * 3
        + [vmem_spec] * 2,
        out_specs=[any_spec] * 4 + [vmem_spec] * 8,
        scratch_shapes=[
            pltpu.VMEM((9, D, D), BF16),
            pltpu.VMEM((3, D, D), F32),
            pltpu.VMEM((9, 8, D), F32),
            pltpu.VMEM((everyone * VECTORS, 128), F32),
            pltpu.VMEM((HELD, columns, n * rows, D), BF16),
            pltpu.VMEM((NEAR, columns, n * rows, D), BF16),
            pltpu.VMEM((UNITS, (n_2 - 1) * n_1, n * rows, D), BF16),
            pltpu.VMEM((UNITS, n_1 - 1, n * rows, D), BF16),
            pltpu.VMEM((UNITS, n - 1, rows, D), BF16),
            pltpu.VMEM((columns, n * VECTORS, 128), F32),
            pltpu.VMEM((columns, n * VECTORS, 128), F32),
            pltpu.VMEM(((n_2 - 1) * n_1, n * VECTORS, 128), F32),
            pltpu.VMEM((n_1 - 1, n * VECTORS, 128), F32),
            pltpu.VMEM((n - 1, VECTORS, 128), F32),
            dma((total, slots)),
            dma((total, slots)),
            dma((total, columns)),
            pltpu.SemaphoreType.REGULAR,
            dma((9,)),
            dma((3,)),
            dma((8,)),
            dma((3,)),
        ],
        compiler_params=pltpu.CompilerParams(
            collective_id=1, has_side_effects=True, vmem_limit_bytes=63 * 2**20
        ),
        name="backward_scatter",
    )(full, vec, kept, kept_f, g_mlp, small, latents, inputs, cot, lat_ids, in_ids)


def body(
    latents,
    group_inputs,
    latent_images,
    input_images,
    cotangent,
    cross_gain,
    cross_shift,
    source_gain,
    source_shift,
    query_weight,
    keyval_weight,
    cross_out_weight,
    self_gain,
    self_shift,
    self_qkv_weight,
    self_out_weight,
    mlp_gain,
    mlp_shift,
    up_weight,
    up_bias,
    down_weight,
    down_bias,
):
    lat_ids = latent_images.reshape(-1, GROUP)
    in_ids = input_images.reshape(-1, GROUP)
    sizes = (lax.axis_size("wide"), lax.axis_size("narrow"))
    everyone = sizes[0] * sizes[1]
    short = cross_gain.shape[0]
    per = 128 // short
    me = lax.axis_index(("wide", "narrow"))
    vectors = (
        cross_gain,
        cross_shift,
        source_gain,
        source_shift,
        self_gain,
        self_shift,
        mlp_gain,
        mlp_shift,
        down_bias,
    )
    stacked = jnp.concatenate(
        [jnp.stack(vectors), up_bias.reshape(4, short), jnp.zeros((3, short), BF16)]
    ).astype(F32)
    lane = lax.broadcasted_iota(jnp.int32, (VECTORS, 128), 1) // short
    packed = jnp.where(lane == lax.rem(me, per), jnp.tile(stacked, (1, per)), 0.0)
    up_chunks = up_weight.reshape(short, everyone, 4, short).transpose(0, 2, 1, 3).reshape(short, -1)
    full, vec_full, finished, kept, kept_f, g_mlp, small, rows = run_forward(
        packed,
        (
            query_weight,
            keyval_weight,
            cross_out_weight,
            self_qkv_weight,
            self_out_weight,
            down_weight,
            up_chunks,
        ),
        latents,
        group_inputs,
        cotangent,
        lat_ids,
        in_ids,
    )
    latent_grad, input_grad, _, _, own_vec, g_down, g_up, g_so, g_qkv, g_co, g_q, g_kv = run_backward(
        full, rows, kept, kept_f, g_mlp, small, latents, group_inputs, cotangent, lat_ids, in_ids
    )
    vec = lax.dynamic_slice_in_dim(own_vec, lax.rem(me, per) * short, short, axis=1)
    own_up_bias = vec[9:13].reshape(-1)
    g_up = g_up.reshape(short, 4, everyone, short).transpose(0, 2, 1, 3).reshape(short, -1)
    return (
        finished,
        latent_grad,
        input_grad,
        vec[0],
        vec[1],
        vec[2],
        vec[3],
        g_q,
        g_kv,
        g_co,
        vec[4],
        vec[5],
        g_qkv,
        g_so,
        vec[6],
        vec[7],
        g_up,
        own_up_bias,
        g_down,
        vec[8],
    )


def solution(mesh):
    rows = P(("wide", "narrow"), None)
    line = P(("wide", "narrow"))
    return jax.shard_map(
        body,
        mesh=mesh,
        in_specs=(rows,) * 5
        + (line,) * 4
        + (rows,) * 3
        + (line,) * 2
        + (rows,) * 2
        + (line,) * 2
        + (rows, line, rows, line),
        out_specs=(rows,) * 3
        + (line,) * 4
        + (rows,) * 3
        + (line,) * 2
        + (rows,) * 2
        + (line,) * 2
        + (rows, line, rows, line),
        check_vma=False,
    )
```

```python
from functools import partial

import jax
import jax.numpy as jnp
from jax import lax
from jax.experimental import pallas as pl
from jax.experimental.pallas import tpu as pltpu
from jax.sharding import PartitionSpec as P

MESH = pl.DeviceIdType.MESH
BF16 = jnp.bfloat16
F32 = jnp.float32


class Place:
    def __init__(self, wide_size, narrow_size):
        self.wide = lax.axis_index("wide")
        self.narrow = lax.axis_index("narrow")
        self.n_narrow = narrow_size
        self.wide_count = wide_size
        self.columns = wide_size // 2
        self.n_a = 2 if self.columns % 2 == 0 else 1
        self.n_b = self.columns // self.n_a
        self.core = lax.rem(self.wide, 2)
        column = self.wide // 2
        self.a = column // self.n_b
        self.b = lax.rem(column, self.n_b)
        self.coloured = self.n_a == self.n_b

    def index(self, a, b, core):
        return (a * self.n_b + b) * 2 + core

    def sibling(self):
        return self.wide + 1 - 2 * self.core

    def along_a(self, step):
        return self.index(lax.rem(self.a + step, self.n_a), self.b, self.core)

    def along_b(self, step):
        return self.index(self.a, lax.rem(self.b + step, self.n_b), self.core)

    def first_count(self):
        return self.n_b

    def second_count(self):
        return self.n_a

    def first(self, step):
        if not self.coloured:
            return self.along_b(step)
        return jnp.where(self.core == 0, self.along_b(step), self.along_a(step))

    def second(self, step):
        if not self.coloured:
            return self.along_a(step)
        return jnp.where(self.core == 0, self.along_a(step), self.along_b(step))

    def corner(self, first_step, second_step):
        if not self.coloured:
            return self.index(
                lax.rem(self.a + second_step, self.n_a),
                lax.rem(self.b + first_step, self.n_b),
                self.core,
            )
        step_a = jnp.where(self.core == 0, second_step, first_step)
        step_b = jnp.where(self.core == 0, first_step, second_step)
        return self.index(
            lax.rem(self.a + step_a, self.n_a), lax.rem(self.b + step_b, self.n_b), self.core
        )

    def depth(self, step):
        return lax.rem(self.narrow + step, self.n_narrow)

    def greet(self):
        barrier = pltpu.get_barrier_semaphore()
        count = 0
        for step in range(1, self.n_narrow):
            pl.semaphore_signal(
                barrier, inc=1, device_id=(self.wide, self.depth(step)), device_id_type=MESH
            )
            count += 1
        for step in range(1, self.n_b):
            pl.semaphore_signal(
                barrier, inc=1, device_id=(self.along_b(step), self.narrow), device_id_type=MESH
            )
            count += 1
        for step in range(1, self.n_a):
            pl.semaphore_signal(
                barrier, inc=1, device_id=(self.along_a(step), self.narrow), device_id_type=MESH
            )
            count += 1
        pl.semaphore_signal(
            barrier, inc=1, device_id=(self.sibling(), self.narrow), device_id_type=MESH
        )
        pl.semaphore_wait(barrier, count + 1)


class Gather:
    def __init__(self, place, own, full, sems):
        self.place = place
        self.own = own
        self.full = full
        self.send, self.recv = sems
        self.rows = own.shape[0]
        self.pending = []
        p = place
        self.n_z = p.n_narrow - 1
        self.n_1 = (p.first_count() - 1) * p.n_narrow
        self.n_2 = (p.second_count() - 1) * p.first_count()

    def view(self, wide, narrow=None):
        n = self.place.n_narrow
        if narrow is None:
            start, size = wide * n * self.rows, n * self.rows
        else:
            start, size = (wide * n + narrow) * self.rows, self.rows
        return self.full.at[pl.ds(pl.multiple_of(start, self.rows), size), :]

    def copy(self, src, dst, slot, device):
        return pltpu.make_async_remote_copy(
            src_ref=src,
            dst_ref=dst,
            send_sem=self.send.at[slot],
            recv_sem=self.recv.at[slot],
            device_id=device,
            device_id_type=MESH,
        )

    def go(self, copy):
        copy.start()
        self.pending.append(copy)

    def landed(self, view, slot):
        self.copy(view, view, slot, (self.place.sibling(), self.place.narrow)).wait_recv()

    def slot_first(self, step, k):
        return self.n_z + (step - 1) * self.place.n_narrow + k

    def slot_second(self, step, k):
        return self.n_z + self.n_1 + (step - 1) * self.place.first_count() + k

    def slot_sibling(self, k):
        return self.n_z + self.n_1 + self.n_2 + k

    def stage_1(self):
        p = self.place
        for step in range(1, p.n_narrow):
            self.go(
                self.copy(
                    self.own,
                    self.view(p.wide, p.narrow),
                    step - 1,
                    (p.wide, p.depth(step)),
                )
            )
        for step in range(1, p.first_count()):
            self.go(
                self.copy(
                    self.own,
                    self.view(p.wide, p.narrow),
                    self.slot_first(step, 0),
                    (p.first(step), p.narrow),
                )
            )

    def stage_2(self):
        p = self.place
        for step in range(1, p.n_narrow):
            source = p.depth(p.n_narrow - step)
            view = self.view(p.wide, source)
            self.landed(view, step - 1)
            for hop in range(1, p.first_count()):
                self.go(
                    self.copy(view, view, self.slot_first(hop, step), (p.first(hop), p.narrow))
                )
        view = self.view(p.wide)
        for hop in range(1, p.second_count()):
            self.go(self.copy(view, view, self.slot_second(hop, 0), (p.second(hop), p.narrow)))
        self.go(self.copy(view, view, self.slot_sibling(0), (p.sibling(), p.narrow)))

    def stage_3(self):
        p = self.place
        for step in range(1, p.first_count()):
            column = p.first(p.first_count() - step)
            for k in range(p.n_narrow):
                source = p.depth(p.n_narrow - k)
                self.landed(self.view(column, source), self.slot_first(step, k))
            view = self.view(column)
            for hop in range(1, p.second_count()):
                self.go(
                    self.copy(view, view, self.slot_second(hop, step), (p.second(hop), p.narrow))
                )
            self.go(self.copy(view, view, self.slot_sibling(step), (p.sibling(), p.narrow)))

    def stage_4(self):
        p = self.place
        for hop in range(1, p.second_count()):
            back = p.second_count() - hop
            for k in range(p.first_count()):
                column = p.corner((p.first_count() - k) % p.first_count(), back)
                view = self.view(column)
                self.landed(view, self.slot_second(hop, k))
                slot = self.slot_sibling(hop * p.first_count() + k)
                self.go(self.copy(view, view, slot, (p.sibling(), p.narrow)))

    def stage_5(self):
        p = self.place
        for hop in range(p.second_count()):
            for k in range(p.first_count()):
                back_1 = (p.first_count() - k) % p.first_count()
                back_2 = (p.second_count() - hop) % p.second_count()
                if p.coloured:
                    step_a = jnp.where(p.core == 1, back_2, back_1)
                    step_b = jnp.where(p.core == 1, back_1, back_2)
                else:
                    step_a, step_b = back_2, back_1
                column = p.index(
                    lax.rem(p.a + step_a, p.n_a), lax.rem(p.b + step_b, p.n_b), 1 - p.core
                )
                self.landed(self.view(column), self.slot_sibling(hop * p.first_count() + k))

    def drain(self):
        for copy in self.pending:
            copy.wait_send()


def gather_slots(wide_size, narrow_size):
    columns = wide_size // 2
    n_a = 2 if columns % 2 == 0 else 1
    n_b = columns // n_a
    return (narrow_size - 1) + (n_b - 1) * narrow_size + (n_a - 1) * n_b + n_a * n_b


class Scatter:
    def __init__(self, place, grad, out, bufs, sems):
        self.place = place
        self.grad = grad
        self.out = out
        self.held, self.from_sibling, self.from_second, self.from_first, self.from_depth = bufs
        self.send, self.recv, self.local = sems
        self.pending = []
        p = place
        self.n_1 = p.first_count()
        self.n_2 = p.second_count()
        self.blocks = self.n_1 * self.n_2
        self.rows = out.shape[0]

    def view(self, wide):
        size = self.place.n_narrow * self.rows
        return self.grad.at[pl.ds(pl.multiple_of(wide * size, size), size), :]

    def copy(self, src, dst, slot, device):
        return pltpu.make_async_remote_copy(
            src_ref=src,
            dst_ref=dst,
            send_sem=self.send.at[slot],
            recv_sem=self.recv.at[slot],
            device_id=device,
            device_id_type=MESH,
        )

    def go(self, copy):
        copy.start()
        self.pending.append(copy)

    def landed(self, ref, slot):
        self.copy(ref, ref, slot, (self.place.sibling(), self.place.narrow)).wait_recv()

    def loads(self):
        p = self.place
        result = []
        for s in range(self.n_2):
            for f in range(self.n_1):
                block = s * self.n_1 + f
                result.append(
                    pltpu.make_async_copy(
                        self.view(p.corner(f, s)), self.held.at[block], self.local.at[block]
                    )
                )
        return result

    def stage_0(self):
        p = self.place
        for s in range(self.n_2):
            for f in range(self.n_1):
                if p.coloured:
                    step_a = jnp.where(p.core == 1, s, f)
                    step_b = jnp.where(p.core == 1, f, s)
                else:
                    step_a, step_b = s, f
                column = p.index(
                    lax.rem(p.a + step_a, p.n_a), lax.rem(p.b + step_b, p.n_b), 1 - p.core
                )
                block = s * self.n_1 + f
                self.go(
                    self.copy(
                        self.view(column),
                        self.from_sibling.at[block],
                        block,
                        (p.sibling(), p.narrow),
                    )
                )
        for load in self.loads():
            load.start()

    def add(self, block, *others):
        rows = self.rows

        def step(i, carry):
            part = pl.ds(pl.multiple_of(i * rows, rows), rows)
            total = self.held[block, part, :]
            for other in others:
                total = total + other[part, :]
            self.held[block, part, :] = total
            return carry

        lax.fori_loop(0, self.place.n_narrow, step, 0)

    def piece(self, narrow):
        return pl.ds(pl.multiple_of(narrow * self.rows, self.rows), self.rows)

    def stage_1(self):
        p = self.place
        for load in self.loads():
            load.wait()
        for block in range(self.blocks):
            self.landed(self.from_sibling.at[block], block)
        for s in range(self.n_2 - 1, -1, -1):
            for f in range(self.n_1):
                block = s * self.n_1 + f
                self.add(block, self.from_sibling.at[block])
                if s > 0:
                    slot = (s - 1) * self.n_1 + f
                    self.go(
                        self.copy(
                            self.held.at[block],
                            self.from_second.at[slot],
                            self.blocks + slot,
                            (p.second(s), p.narrow),
                        )
                    )

    def stage_2(self):
        p = self.place
        base = self.blocks + (self.n_2 - 1) * self.n_1
        for f in range(self.n_1 - 1, -1, -1):
            slots = [s * self.n_1 + f for s in range(self.n_2 - 1)]
            for slot in slots:
                self.landed(self.from_second.at[slot], self.blocks + slot)
            self.add(f, *[self.from_second.at[slot] for slot in slots])
            if f > 0:
                self.go(
                    self.copy(
                        self.held.at[f],
                        self.from_first.at[f - 1],
                        base + f - 1,
                        (p.first(f), p.narrow),
                    )
                )

    def stage_3(self):
        p = self.place
        first_base = self.blocks + (self.n_2 - 1) * self.n_1
        base = first_base + self.n_1 - 1
        for f in range(1, self.n_1):
            self.landed(self.from_first.at[f - 1], first_base + f - 1)
        self.add(0, *[self.from_first.at[f - 1] for f in range(1, self.n_1)])
        for step in range(1, p.n_narrow):
            self.go(
                self.copy(
                    self.held.at[0, self.piece(p.depth(step)), :],
                    self.from_depth.at[step - 1],
                    base + step - 1,
                    (p.wide, p.depth(step)),
                )
            )

    def stage_4(self):
        p = self.place
        base = self.blocks + (self.n_2 - 1) * self.n_1 + self.n_1 - 1
        for step in range(1, p.n_narrow):
            self.landed(self.from_depth.at[step - 1], base + step - 1)
        total = self.held[0, self.piece(p.narrow), :].astype(F32)
        for step in range(1, p.n_narrow):
            total = total + self.from_depth[step - 1].astype(F32)
        self.out[...] = total

    def drain(self):
        for copy in self.pending:
            copy.wait_send()


def scatter_slots(wide_size, narrow_size):
    columns = wide_size // 2
    n_a = 2 if columns % 2 == 0 else 1
    n_b = columns // n_a
    return n_a * n_b + (n_a - 1) * n_b + (n_b - 1) + (narrow_size - 1)


D = 1024
HEADS = 8
HD = 128
GROUP = 128
EPSILON = 1e-05
SCALE = HD ** (-0.5)
NN = (((1,), (0,)), ((), ()))
NT = (((1,), (1,)), ((), ()))
TN = (((0,), (0,)), ((), ()))

U_Q, U_K, U_V, U_CO, U_SQ, U_SK, U_SV, U_SO, U_D, U_U = 0, 1, 2, 3, 4, 5, 6, 7, 8, 9
UNITS = 16
VECTORS = 16
V_CG, V_CS, V_IG, V_IS, V_SG, V_SS, V_MG, V_MS, V_BD, V_BU = range(10)
(S_LAT, S_SRC, S_Q, S_K, S_V, S_MIX, S_SL, S_SQ, S_SK, S_SV, S_SMIX) = range(11)


def dot(left, right, dims=NN):
    return lax.dot_general(left, right, dims, preferred_element_type=F32)


def for_each(count, step, unroll=1):
    def run(i, carry):
        step(i)
        return carry

    lax.fori_loop(0, count, run, 0, unroll=unroll)


def part(i, size):
    return pl.ds(pl.multiple_of(i * size, size), size)


def gather_units(sizes, shards):
    rows = D // (sizes[0] * sizes[1])
    q, kv, co, qkv, so, down, up = range(7)
    units = [(q, 0, 0), (kv, 0, 0), (kv, 0, 1), (co, 0, 0), (qkv, 0, 0), (qkv, 0, 1), (qkv, 0, 2)]
    units.append((so, 0, 0))
    for i in range(4):
        units.append((down, i * rows, 0))
        units.append((up, 0, i))
    return rows, units


def norm_stats(x):
    mean = jnp.mean(x, axis=-1, keepdims=True)
    center = x - mean
    spread = jnp.mean(center * center, axis=-1, keepdims=True)
    return center, lax.rsqrt(spread + EPSILON)


def group_mask(row_ids, column_ids):
    across = jnp.broadcast_to(row_ids.astype(F32), (GROUP, GROUP)).T
    return across == jnp.broadcast_to(column_ids.astype(F32), (GROUP, GROUP))


def softmax_columns(scores):
    raised = jnp.exp(scores - jnp.max(scores, axis=0, keepdims=True))
    return raised * (1.0 / jnp.sum(raised, axis=0, keepdims=True))


HEAD_COLUMNS = [slice(h * HD, (h + 1) * HD) for h in range(HEADS)]
HALVES = (slice(0, 512), slice(512, 1024))


def gelu_parts(x):
    half = 0.5 * (1.0 + lax.erf(x * (2.0**-0.5)))
    return x * half, half + x * (jnp.exp(-0.5 * x * x) * ((2.0 * jnp.pi) ** -0.5))


class Ticks:
    def __init__(self, jobs):
        self.jobs = jobs
        self.done = 0
        self.last = len(jobs) + 3

    def one(self):
        t = self.done
        if t >= self.last:
            return
        for back, stage in ((3, "stage_5"), (2, "stage_4"), (1, "stage_3"), (0, "stage_2"), (-1, "stage_1")):
            if 0 <= t - back < len(self.jobs):
                getattr(self.jobs[t - back], stage)()
        self.done = t + 1

    def until(self, job):
        while self.done < job + 4:
            self.one()


HELD = 5
FROM = 4
NEAR = 3
(G_SO, G_SQ, G_SK, G_SV, G_CO, G_Q, G_K, G_V) = range(8)


def fold_rows(value):
    return jnp.sum(value.reshape(-1, 8, D), axis=0)


def scatter_targets():
    targets = []
    for i in range(4):
        targets.append((0, i, 0))
        targets.append((1, 0, i))
    targets.append((2, 0, 0))
    for c in range(3):
        targets.append((3, 0, c))
    targets += [(4, 0, 0), (5, 0, 0), (6, 0, 0), (6, 0, 1)]
    return targets


class Sums:
    STAGES = ("stage_0", "stage_1", "stage_2", "stage_3", "stage_4")

    def __init__(self, jobs, credit, place):
        self.jobs = jobs
        self.credit = credit
        self.place = place
        self.stage = [0] * len(jobs)
        self.started = 0
        self.drained = 0
        self.waits = {}

    def one(self, start=True):
        big = len(self.jobs) - 1
        running = [j for j in range(self.started) if self.stage[j] < 5]
        if start and self.started < len(self.jobs):
            j = self.started
            for copy in self.waits.pop(j, ()):
                copy.wait()
            if j < big and j >= NEAR:
                pl.semaphore_wait(self.credit, 1)
            if j < big and j >= HELD:
                self.jobs[j - HELD].drain()
                self.drained = j - HELD + 1
            running.append(j)
            self.started += 1
        for j in running[::-1]:
            getattr(self.jobs[j], self.STAGES[self.stage[j]])()
            if self.stage[j] == 1 and j + NEAR < big:
                pl.semaphore_signal(
                    self.credit,
                    inc=1,
                    device_id=(self.place.sibling(), self.place.narrow),
                    device_id_type=MESH,
                )
            self.stage[j] += 1

    def finish(self):
        while self.started < len(self.jobs) or self.stage[-1] < 5:
            self.one()
        for job in self.jobs[self.drained :]:
            job.drain()


def layer_kernel(sizes, *refs):
    vec_shard, shards, rest = refs[0], refs[1:8], refs[8:]
    latents, inputs, cot, lat_ids, in_ids = rest[:5]
    finished, latent_grad, input_grad, full, vec_full, kept, kept_f, g_mlp, g_att, vec_sent = rest[5:15]
    vec_out, *outs = rest[15:23]
    (
        vec_staged,
        vec_all,
        vec,
        small,
        pool,
        fpool,
        vacc,
        held,
        near,
        from_second,
        from_first,
        from_depth,
        vheld,
        vnear,
        vsecond,
        vfirst,
        vdepth,
        send,
        recv,
        vsend,
        vrecv,
        rsend,
        rrecv,
        local,
        credit,
        sem_stage,
        sem_own,
        sem_in,
        sem_w,
        sem_f,
        sem_keep,
        sem_keep_f,
        sem_g,
        sem_o,
    ) = rest[23:]
    place = Place(*sizes)
    rows, units = gather_units(sizes, shards)
    mine = place.wide * place.n_narrow + place.narrow

    LAT, INP, LLOW, SLOW, Q, K, V, MIX = 0, 1, 2, 3, 8, 9, 10, 11
    W0 = 4
    SELF = (12, 13, 4, 5)
    ML, COT = 2, 3
    STAGE = 13

    copies_in = [
        pltpu.make_async_copy(latents, pool.at[LAT], sem_in.at[0]),
        pltpu.make_async_copy(inputs, pool.at[INP], sem_in.at[1]),
    ]
    stage_in = []
    for u, (k, r0, c0) in enumerate(units):
        source = shards[k].at[pl.ds(r0, rows), pl.ds(c0 * D, D)]
        stage_in.append(
            pltpu.make_async_copy(source, pool.at[STAGE, part(u, rows), :], sem_stage.at[u])
        )
    stage_in.append(pltpu.make_async_copy(vec_shard, vec_staged, sem_stage.at[UNITS]))
    own_out = [
        pltpu.make_async_copy(
            pool.at[STAGE, part(u, rows), :], full.at[u, part(mine, rows), :], sem_own.at[u]
        )
        for u in range(UNITS)
    ]
    own_out.append(
        pltpu.make_async_copy(vec_staged, vec_full.at[part(mine, VECTORS), :], sem_own.at[UNITS])
    )
    for copy in stage_in[::-1]:
        copy.start()
    for copy in copies_in:
        copy.start()
    place.greet()
    jobs = [Gather(place, vec_shard, vec_full, (vsend, vrecv))]
    for u, (k, r0, c0) in enumerate(units):
        source = shards[k].at[pl.ds(r0, rows), pl.ds(c0 * D, D)]
        jobs.append(Gather(place, source, full.at[u], (send.at[u], recv.at[u])))
    ticks = Ticks(jobs)
    limit = [0]
    sum_jobs = []
    for i, (p, r, c) in enumerate(scatter_targets()):
        grad = g_mlp.at[i] if i < 8 else g_att.at[i - 8]
        out = outs[p].at[pl.ds(r * rows, rows), pl.ds(c * D, D)]
        turn = i % HELD
        bufs = (
            held.at[turn],
            near.at[i % NEAR],
            from_second.at[i % FROM],
            from_first.at[i % FROM],
            from_depth.at[i % FROM],
        )
        sum_jobs.append(Scatter(place, grad, out, bufs, (rsend.at[i], rrecv.at[i], local.at[i])))
    sum_jobs.append(
        Scatter(
            place,
            vec_sent,
            vec_out,
            (vheld, vnear, vsecond, vfirst, vdepth),
            (rsend.at[UNITS], rrecv.at[UNITS], local.at[UNITS]),
        )
    )
    sums = Sums(sum_jobs, credit, place)

    def tick():
        sums.one(start=sums.started < limit[0])

    jobs[0].stage_1()
    for i in range(UNITS, -1, -1):
        stage_in[i].wait()
        own_out[i].start()
    for i in range(UNITS, -1, -1):
        own_out[i].wait()

    def load(unit, slot):
        return pltpu.make_async_copy(full.at[unit], pool.at[slot], sem_w.at[slot])

    def fetch(unit, slot):
        ticks.until(unit + 1)
        load(unit, slot).start()

    def keep(slot, index):
        return pltpu.make_async_copy(pool.at[slot], kept.at[index], sem_keep.at[index])

    def keep_f(slot, index):
        return pltpu.make_async_copy(fpool.at[slot], kept_f.at[index], sem_keep_f.at[index])

    def vector(k, columns=slice(None)):
        return vec[k : k + 1, columns]

    ticks.until(0)
    copy = pltpu.make_async_copy(vec_full, vec_all, sem_in.at[2])
    copy.start()
    copy.wait()
    lane_groups = D // 128
    per = place.wide_count * place.n_narrow // lane_groups
    for g in range(lane_groups):
        total = vec_all[pl.ds(g * per * VECTORS, VECTORS), :]
        for j in range(1, per):
            total = total + vec_all[pl.ds((g * per + j) * VECTORS, VECTORS), :]
        vec[:, g * 128 : (g + 1) * 128] = total

    def norm_low(read, slot, gain, shift):
        def step(i):
            sl = part(i, 64)
            center, rate = norm_stats(read(sl))
            pool[slot, sl, :] = (center * rate * vector(gain) + vector(shift)).astype(BF16)

        for_each(16, step)

    def product(out, left, weight):
        values = [dot(pool[left], pool[weight, :, sl]) for sl in HALVES]
        for sl, value in zip(HALVES, values):
            pool[out, :, sl] = value.astype(BF16)

    def attend(q, k, v, out, ids, groups):
        def step(g):
            sl = part(g, GROUP)
            mask = group_mask(ids[pl.ds(g, 1), :], lat_ids[pl.ds(g, 1), :])
            scores = [dot(pool[k, sl, hs], pool[q, sl, hs], NT) for hs in HEAD_COLUMNS]
            weights = [softmax_columns(jnp.where(mask, x * SCALE, -1e30)).astype(BF16) for x in scores]
            mixed = [dot(x, pool[v, sl, hs], TN) for x, hs in zip(weights, HEAD_COLUMNS)]
            for x, hs in zip(mixed, HEAD_COLUMNS):
                pool[out, sl, hs] = x.astype(BF16)

        lo, hi = groups

        def run(g, carry):
            step(g)
            return carry

        lax.fori_loop(lo, hi, run, 0)

    copies_in[0].wait()
    norm_low(lambda sl: pool[LAT, sl, :].astype(F32), LLOW, V_CG, V_CS)
    keep(LLOW, S_LAT).start()
    fetch(U_Q, W0)
    copies_in[1].wait()
    norm_low(lambda sl: pool[INP, sl, :].astype(F32), SLOW, V_IG, V_IS)
    keep(SLOW, S_SRC).start()
    load(U_Q, W0).wait()
    product(Q, LLOW, W0)
    keep(Q, S_Q).start()
    fetch(U_K, W0 + 1)
    load(U_K, W0 + 1).wait()
    product(K, SLOW, W0 + 1)
    keep(K, S_K).start()
    fetch(U_V, W0 + 2)
    load(U_V, W0 + 2).wait()
    product(V, SLOW, W0 + 2)
    keep(V, S_V).start()
    attend(Q, K, V, MIX, in_ids, (0, 4))
    fetch(U_CO, W0 + 3)
    attend(Q, K, V, MIX, in_ids, (4, 8))
    keep(MIX, S_MIX).start()
    load(U_CO, W0 + 3).wait()

    values = [dot(pool[MIX], pool[W0 + 3, :, sl]) for sl in HALVES]
    for sl, value in zip(HALVES, values):
        fpool[0, :, sl] = pool[LAT, :, sl].astype(F32) + value
    keep_f(0, 0).start()
    fetch(U_SQ, SELF[0])
    norm_low(lambda sl: fpool[0, sl, :], LAT, V_SG, V_SS)
    keep(LAT, S_SL).start()
    keep(Q, S_Q).wait()
    keep(K, S_K).wait()
    keep(V, S_V).wait()
    for offset, (slot, index, before) in enumerate(((Q, S_SQ, 0), (K, S_SK, 0), (V, S_SV, 0))):
        load(U_SQ + offset, SELF[offset]).wait()
        product(slot, LAT, SELF[offset])
        keep(slot, index).start()
        fetch(U_SQ + offset + 1, SELF[offset + 1])
    keep(MIX, S_MIX).wait()
    attend(Q, K, V, MIX, lat_ids, (0, 4))
    ticks.one()
    attend(Q, K, V, MIX, lat_ids, (4, 8))
    keep(MIX, S_SMIX).start()
    load(U_SO, SELF[3]).wait()

    values = [dot(pool[MIX], pool[SELF[3], :, sl]) for sl in HALVES]
    for sl, value in zip(HALVES, values):
        fpool[1, :, sl] = fpool[0, :, sl] + value
    keep_f(1, 1).start()
    keep(LLOW, S_LAT).wait()
    keep(SLOW, S_SRC).wait()
    cot_in = pltpu.make_async_copy(cot, pool.at[COT], sem_in.at[3])
    cot_in.start()
    norm_low(lambda sl: fpool[1, sl, :], ML, V_MG, V_MS)
    cot_in.wait()
    for slot, index in ((LAT, S_SL), (Q, S_SQ), (K, S_SK), (V, S_SV), (MIX, S_SMIX)):
        keep(slot, index).wait()
    keep_f(1, 1).wait()
    keep_f(0, 0).wait()

    ACT, GH = 8, 9
    PAIR = (6, 4)
    GD, GU = 10, 12
    GIN = 0
    CH = 512
    R = 256
    small[...] = jnp.zeros_like(small)

    def spread(chunk):
        i, h = divmod(chunk, 2)
        down, up = PAIR[i % 2], PAIR[i % 2] + 1
        cols = pl.ds(h * CH, CH)
        values = dot(pool[ML], pool[up, :, cols]), dot(pool[COT], pool[down, cols, :], NT)
        fpool[2, :, 0:CH] = values[0]
        fpool[2, :, CH : 2 * CH] = values[1]

    def bend(chunk, sl):
        i, h = divmod(chunk, 2)
        cols = pl.ds(h * CH, CH)
        value, slope = gelu_parts(fpool[2, sl, 0:CH] + vec[V_BU + i : V_BU + i + 1, cols])
        value, grad = value.astype(BF16), (slope * fpool[2, sl, CH : 2 * CH]).astype(BF16)
        total = jnp.sum(grad.astype(F32), axis=0, keepdims=True)

        def store():
            out = pl.ds((chunk % 2) * CH, CH)
            pool[ACT, sl, out] = value
            pool[GH, sl, out] = grad
            small[i : i + 1, cols] += total

        return store

    def fold(chunk, sl):
        i, h = divmod(chunk, 2)
        down, up = PAIR[i % 2], PAIR[i % 2] + 1
        cols = pl.ds(h * CH, CH)
        out = pl.ds((chunk % 2) * CH, CH)
        result = fpool[1, sl, :] + dot(pool[ACT, sl, out], pool[down, cols, :])
        grad = dot(pool[GH, sl, out], pool[up, :, cols], NT)
        if chunk > 0:
            grad = grad + fpool[GIN, sl, :]

        def store():
            fpool[1, sl, :] = result
            fpool[GIN, sl, :] = grad

        return store

    def grad_out(i):
        return [
            pltpu.make_async_copy(pool.at[GD + i % 2], g_mlp.at[2 * i], sem_g.at[2 * i]),
            pltpu.make_async_copy(pool.at[GU + i % 2], g_mlp.at[2 * i + 1], sem_g.at[2 * i + 1]),
        ]

    def weigh(chunk):
        i, h = divmod(chunk, 2)
        cols = pl.ds(h * CH, CH)
        out = pl.ds((chunk % 2) * CH, CH)
        down = dot(pool[ACT, :, out], pool[COT], TN)
        up = dot(pool[ML], pool[GH, :, out], TN)
        pool[GD + i % 2, cols, :] = down.astype(BF16)
        pool[GU + i % 2, :, cols] = up.astype(BF16)

    def fetch_pair(i):
        fetch(U_D + 2 * i, PAIR[i % 2])
        fetch(U_U + 2 * i, PAIR[i % 2] + 1)

    for chunk in range(8):
        i, h = divmod(chunk, 2)
        if h == 0:
            if i == 0:
                fetch_pair(0)
            load(U_D + 2 * i, PAIR[i % 2]).wait()
            load(U_U + 2 * i, PAIR[i % 2] + 1).wait()
            spread(chunk)
            ticks.one()
        else:
            spread(chunk)
            if i < 3:
                fetch_pair(i + 1)

        def rows_step(r):
            sl = part(r, R)
            stores = [bend(chunk, sl)]
            if chunk > 0:
                stores.append(fold(chunk - 1, sl))
            for store in stores:
                store()

        for_each(D // R, rows_step)
        if h == 0 and i >= 2:
            for job in (2 * i - 4, 2 * i - 3):
                for copy in sums.waits.pop(job, ()):
                    copy.wait()
        weigh(chunk)
        if h == 1:
            for job, copy in enumerate(grad_out(i), 2 * i):
                copy.start()
                sums.waits[job] = (copy,)
            limit[0] = 2 * i + 2
        if chunk >= 5:
            tick()

    A, B, C, DD, E, F, G, S1, S2 = 9, 1, 5, COT, 6, 7, 0, GD, GU

    def load_f(index, slot):
        return pltpu.make_async_copy(kept_f.at[index], fpool.at[slot], sem_f.at[slot])

    def bring(source, slot):
        return pltpu.make_async_copy(source, pool.at[slot], sem_w.at[slot])

    first = [
        bring(kept.at[S_SMIX], B),
        bring(kept.at[S_SQ], E),
        bring(kept.at[S_SK], F),
        bring(kept.at[S_SV], G),
        bring(full.at[U_SO], C),
        load_f(1, 1),
    ]

    def last(r):
        sl = part(r, R)
        fold(7, sl)()
        pool[ML, sl, :] = (fpool[1, sl, :] + vector(V_BD)).astype(BF16)

    for copy in first[:4]:
        copy.start()
    for_each(D // R, last)
    first[4].start()
    first[5].start()
    done = pltpu.make_async_copy(pool.at[ML], finished, sem_in.at[4])
    done.start()
    while ticks.done < ticks.last:
        ticks.one()
    for job in jobs:
        job.drain()

    vacc[...] = jnp.zeros_like(vacc)

    def norm_back(read_x, grad_slot, gain, shift, write):
        def step(i, carry):
            sl = part(i, 64)
            center, rate = norm_stats(read_x(sl))
            normal = center * rate
            grad = fpool[grad_slot, sl, :]
            sums_gain = carry[0] + fold_rows(grad * normal)
            sums_shift = carry[1] + fold_rows(grad)
            grad = grad * vec[gain : gain + 1, :]
            mean_1 = jnp.mean(grad, axis=-1, keepdims=True)
            mean_2 = jnp.mean(grad * normal, axis=-1, keepdims=True)
            write(sl, rate * (grad - mean_1 - normal * mean_2))
            return sums_gain, sums_shift

        zero = jnp.zeros((8, D), F32)
        carry = (zero, zero)
        carry = lax.fori_loop(0, 16, step, carry)
        vacc[gain] = carry[0]
        vacc[shift] = carry[1]
        tick()

    staging = [S1, S2]
    saved = [4, 5]

    def weight_grad(index, left, right):
        turn = index % 2
        if saved[turn] is not None and saved[turn] in sums.waits:
            for copy in sums.waits.pop(saved[turn]):
                copy.wait()
        slot = staging[turn]

        values = [dot(pool[left], pool[right, :, sl], TN) for sl in HALVES]
        for sl, value in zip(HALVES, values):
            pool[slot, :, sl] = value.astype(BF16)
        copy = pltpu.make_async_copy(pool.at[slot], g_att.at[index], sem_g.at[8 + index])
        copy.start()
        sums.waits[8 + index] = (copy,)
        saved[turn] = 8 + index
        limit[0] = 8 + index + 1

    def back_product(out, left, weight):
        values = [dot(pool[left], pool[weight, sl, :], NT) for sl in HALVES]
        for sl, value in zip(HALVES, values):
            pool[out, :, sl] = value.astype(BF16)

    def back_sum(out, left, weight, fresh):
        values = [dot(pool[left], pool[weight, sl, :], NT) for sl in HALVES]
        if not fresh:
            values = [value + fpool[out, :, sl] for sl, value in zip(HALVES, values)]
        for sl, value in zip(HALVES, values):
            fpool[out, :, sl] = value

    def attend_back(q, k, v, grad, ids):
        def step(g, carry):
            sl = part(g, GROUP)
            mask = group_mask(ids[pl.ds(g, 1), :], lat_ids[pl.ds(g, 1), :])
            scores = [dot(pool[k, sl, hs], pool[q, sl, hs], NT) for hs in HEAD_COLUMNS]
            slopes = [dot(pool[v, sl, hs], pool[grad, sl, hs], NT) for hs in HEAD_COLUMNS]
            weights = [softmax_columns(jnp.where(mask, x * SCALE, -1e30)) for x in scores]
            inner = [jnp.sum(x * y, axis=0, keepdims=True) for x, y in zip(weights, slopes)]
            slopes = [(x * (y - z)).astype(BF16) for x, y, z in zip(weights, slopes, inner)]
            weights = [x.astype(BF16) for x in weights]
            grad_v = [dot(x, pool[grad, sl, hs]) for x, hs in zip(weights, HEAD_COLUMNS)]
            grad_k = [dot(x, pool[q, sl, hs]) * SCALE for x, hs in zip(slopes, HEAD_COLUMNS)]
            grad_q = [dot(x, pool[k, sl, hs], TN) * SCALE for x, hs in zip(slopes, HEAD_COLUMNS)]
            for slot, values in ((v, grad_v), (k, grad_k), (q, grad_q)):
                for x, hs in zip(values, HEAD_COLUMNS):
                    pool[slot, sl, hs] = x.astype(BF16)
            return carry

        lax.fori_loop(0, 8, step, 0)
        tick()

    first[5].wait()

    def after_self(sl, grad):
        cot_rows = pool[DD, sl, :].astype(F32)
        vacc[V_BD] += fold_rows(cot_rows)
        total = cot_rows + grad
        fpool[2, sl, :] = total
        pool[A, sl, :] = total.astype(BF16)

    norm_back(lambda sl: fpool[1, sl, :], 0, V_MG, V_MS, after_self)
    load_f(0, 1).start()

    for copy in first[:5]:
        copy.wait()
    weight_grad(G_SO, B, A)
    bring(kept.at[S_SL], B).start()
    back_product(DD, A, C)
    bring(full.at[U_SQ], A).start()
    bring(full.at[U_SK], C).start()
    tick()
    attend_back(E, F, G, DD, lat_ids)
    bring(full.at[U_SV], DD).start()
    bring(kept.at[S_SL], B).wait()
    for index, slot, weight, unit in ((G_SQ, E, A, U_SQ), (G_SK, F, C, U_SK), (G_SV, G, DD, U_SV)):
        weight_grad(index, B, slot)
        bring(full.at[unit], weight).wait()
        back_sum(0, slot, weight, index == G_SQ)
        tick()
        if index == G_SQ:
            bring(kept.at[S_Q], E).start()
            bring(full.at[U_CO], A).start()
        elif index == G_SK:
            bring(kept.at[S_K], F).start()
        else:
            bring(kept.at[S_V], G).start()
            bring(kept.at[S_MIX], B).start()
    load_f(0, 1).wait()

    def after_cross(sl, grad):
        total = fpool[2, sl, :] + grad
        fpool[2, sl, :] = total
        pool[C, sl, :] = total.astype(BF16)

    norm_back(lambda sl: fpool[1, sl, :], 0, V_SG, V_SS, after_cross)

    bring(kept.at[S_MIX], B).wait()
    weight_grad(G_CO, B, C)
    bring(kept.at[S_LAT], B).start()
    bring(full.at[U_CO], A).wait()
    back_product(DD, C, A)
    bring(full.at[U_Q], A).start()
    bring(kept.at[S_SRC], C).start()
    tick()
    bring(kept.at[S_Q], E).wait()
    bring(kept.at[S_K], F).wait()
    bring(kept.at[S_V], G).wait()
    attend_back(E, F, G, DD, in_ids)
    bring(full.at[U_K], DD).start()
    bring(kept.at[S_LAT], B).wait()
    weight_grad(G_Q, B, E)
    bring(latents, B).start()
    bring(full.at[U_Q], A).wait()
    back_sum(0, E, A, True)
    bring(full.at[U_V], A).start()
    tick()
    bring(kept.at[S_SRC], C).wait()
    weight_grad(G_K, C, F)
    tick()
    weight_grad(G_V, C, G)
    bring(inputs, C).start()
    tick()
    bring(full.at[U_K], DD).wait()
    back_sum(1, F, DD, True)
    bring(full.at[U_V], A).wait()
    back_sum(1, G, A, False)
    bring(latents, B).wait()

    def latent_out(sl, grad):
        pool[E, sl, :] = (fpool[2, sl, :] + grad).astype(BF16)

    norm_back(lambda sl: pool[B, sl, :].astype(F32), 0, V_CG, V_CS, latent_out)
    done_1 = pltpu.make_async_copy(pool.at[E], latent_grad, sem_o.at[0])
    done_1.start()
    bring(inputs, C).wait()

    def input_out(sl, grad):
        pool[F, sl, :] = grad.astype(BF16)

    norm_back(lambda sl: pool[C, sl, :].astype(F32), 1, V_IG, V_IS, input_out)
    done_2 = pltpu.make_async_copy(pool.at[F], input_grad, sem_o.at[1])
    done_2.start()

    lane_groups = D // 128
    per = sizes[0] * sizes[1] // lane_groups
    for k in range(9):
        vacc[k, 0:1, :] = jnp.sum(vacc[k], axis=0, keepdims=True)
    for g in range(lane_groups):
        lanes = slice(g * 128, (g + 1) * 128)
        block = [vacc[k, 0:1, lanes] for k in range(9)]
        block += [small[0:4, lanes], jnp.zeros((3, 128), F32)]
        block = jnp.concatenate(block, axis=0)

        def put(j, carry):
            vec_all[part(g * per + j, VECTORS), :] = block
            return carry

        lax.fori_loop(0, per, put, 0)
    copy = pltpu.make_async_copy(vec_all, vec_sent, sem_o.at[2])
    copy.start()
    copy.wait()
    limit[0] = len(sum_jobs)
    sums.finish()
    done.wait()
    done_1.wait()
    done_2.wait()


def run_layer(vec_shard, shards, latents, inputs, cot, lat_ids, in_ids):
    sizes = (lax.axis_size("wide"), lax.axis_size("narrow"))
    everyone = sizes[0] * sizes[1]
    rows = D // everyone
    columns = sizes[0] // 2
    n_2 = 2 if columns % 2 == 0 else 1
    n_1 = columns // n_2
    n = sizes[1]
    widths = ((4 * rows, D), (rows, 4 * D), (rows, D), (rows, 3 * D), (rows, D), (rows, D), (rows, 2 * D))
    gslots = gather_slots(*sizes)
    slots = scatter_slots(*sizes)
    any_spec = pl.BlockSpec(memory_space=pl.ANY)
    vmem_spec = pl.BlockSpec(memory_space=pltpu.VMEM)
    dma = pltpu.SemaphoreType.DMA
    total = UNITS + 1
    return pl.pallas_call(
        partial(layer_kernel, sizes),
        out_shape=[
            jax.ShapeDtypeStruct((D, D), BF16),
            jax.ShapeDtypeStruct((D, D), BF16),
            jax.ShapeDtypeStruct((D, D), BF16),
            jax.ShapeDtypeStruct((UNITS, D, D), BF16),
            jax.ShapeDtypeStruct((everyone * VECTORS, 128), F32),
            jax.ShapeDtypeStruct((11, D, D), BF16),
            jax.ShapeDtypeStruct((2, D, D), F32),
            jax.ShapeDtypeStruct((8, D, D), BF16),
            jax.ShapeDtypeStruct((8, D, D), BF16),
            jax.ShapeDtypeStruct((everyone * VECTORS, 128), F32),
            jax.ShapeDtypeStruct((VECTORS, 128), F32),
        ]
        + [jax.ShapeDtypeStruct(shape, F32) for shape in widths],
        in_specs=[any_spec] * 11 + [vmem_spec] * 2,
        out_specs=[any_spec] * 10 + [vmem_spec] * 8,
        scratch_shapes=[
            pltpu.VMEM((VECTORS, 128), F32),
            pltpu.VMEM((everyone * VECTORS, 128), F32),
            pltpu.VMEM((VECTORS, D), F32),
            pltpu.VMEM((8, D), F32),
            pltpu.VMEM((14, D, D), BF16),
            pltpu.VMEM((3, D, D), F32),
            pltpu.VMEM((9, 8, D), F32),
            pltpu.VMEM((HELD, columns, n * rows, D), BF16),
            pltpu.VMEM((NEAR, columns, n * rows, D), BF16),
            pltpu.VMEM((FROM, (n_2 - 1) * n_1, n * rows, D), BF16),
            pltpu.VMEM((FROM, n_1 - 1, n * rows, D), BF16),
            pltpu.VMEM((FROM, n - 1, rows, D), BF16),
            pltpu.VMEM((columns, n * VECTORS, 128), F32),
            pltpu.VMEM((columns, n * VECTORS, 128), F32),
            pltpu.VMEM(((n_2 - 1) * n_1, n * VECTORS, 128), F32),
            pltpu.VMEM((n_1 - 1, n * VECTORS, 128), F32),
            pltpu.VMEM((n - 1, VECTORS, 128), F32),
            dma((UNITS, gslots)),
            dma((UNITS, gslots)),
            dma((gslots,)),
            dma((gslots,)),
            dma((total, slots)),
            dma((total, slots)),
            dma((total, columns)),
            pltpu.SemaphoreType.REGULAR,
            dma((UNITS + 1,)),
            dma((UNITS + 1,)),
            dma((5,)),
            dma((14,)),
            dma((3,)),
            dma((11,)),
            dma((2,)),
            dma((16,)),
            dma((3,)),
        ],
        compiler_params=pltpu.CompilerParams(
            collective_id=0, has_side_effects=True, vmem_limit_bytes=67_043_328
        ),
        name="layer",
    )(vec_shard, *shards, latents, inputs, cot, lat_ids, in_ids)


def body(
    latents,
    group_inputs,
    latent_images,
    input_images,
    cotangent,
    cross_gain,
    cross_shift,
    source_gain,
    source_shift,
    query_weight,
    keyval_weight,
    cross_out_weight,
    self_gain,
    self_shift,
    self_qkv_weight,
    self_out_weight,
    mlp_gain,
    mlp_shift,
    up_weight,
    up_bias,
    down_weight,
    down_bias,
):
    lat_ids = latent_images.reshape(-1, GROUP)
    in_ids = input_images.reshape(-1, GROUP)
    sizes = (lax.axis_size("wide"), lax.axis_size("narrow"))
    everyone = sizes[0] * sizes[1]
    short = cross_gain.shape[0]
    per = 128 // short
    me = lax.axis_index(("wide", "narrow"))
    vectors = (
        cross_gain,
        cross_shift,
        source_gain,
        source_shift,
        self_gain,
        self_shift,
        mlp_gain,
        mlp_shift,
        down_bias,
    )
    stacked = jnp.concatenate(
        [jnp.stack(vectors), up_bias.reshape(4, short), jnp.zeros((3, short), BF16)]
    ).astype(F32)
    lane = lax.broadcasted_iota(jnp.int32, (VECTORS, 128), 1) // short
    packed = jnp.where(lane == lax.rem(me, per), jnp.tile(stacked, (1, per)), 0.0)
    up_chunks = up_weight.reshape(short, everyone, 4, short).transpose(0, 2, 1, 3).reshape(short, -1)
    finished, latent_grad, input_grad, *_, own_vec, g_down, g_up, g_so, g_qkv, g_co, g_q, g_kv = run_layer(
        packed,
        (
            query_weight,
            keyval_weight,
            cross_out_weight,
            self_qkv_weight,
            self_out_weight,
            down_weight,
            up_chunks,
        ),
        latents,
        group_inputs,
        cotangent,
        lat_ids,
        in_ids,
    )
    vec = lax.dynamic_slice_in_dim(own_vec, lax.rem(me, per) * short, short, axis=1)
    own_up_bias = vec[9:13].reshape(-1)
    g_up = g_up.reshape(short, 4, everyone, short).transpose(0, 2, 1, 3).reshape(short, -1)
    return (
        finished,
        latent_grad,
        input_grad,
        vec[0],
        vec[1],
        vec[2],
        vec[3],
        g_q,
        g_kv,
        g_co,
        vec[4],
        vec[5],
        g_qkv,
        g_so,
        vec[6],
        vec[7],
        g_up,
        own_up_bias,
        g_down,
        vec[8],
    )


def solution(mesh):
    rows = P(("wide", "narrow"), None)
    line = P(("wide", "narrow"))
    return jax.shard_map(
        body,
        mesh=mesh,
        in_specs=(rows,) * 5
        + (line,) * 4
        + (rows,) * 3
        + (line,) * 2
        + (rows,) * 2
        + (line,) * 2
        + (rows, line, rows, line),
        out_specs=(rows,) * 3
        + (line,) * 4
        + (rows,) * 3
        + (line,) * 2
        + (rows,) * 2
        + (line,) * 2
        + (rows, line, rows, line),
        check_vma=False,
    )
```

```python
from functools import partial

import jax
import jax.numpy as jnp
from jax import lax
from jax.experimental import pallas as pl
from jax.experimental.pallas import tpu as pltpu
from jax.sharding import PartitionSpec as P

MESH = pl.DeviceIdType.MESH
BF16 = jnp.bfloat16
F32 = jnp.float32


def remembered(method):
    def look_up(self, *args):
        key = (method.__name__,) + args
        if key not in self.known:
            self.known[key] = method(self, *args)
        return self.known[key]

    return look_up


class Place:
    def __init__(self, wide_size, narrow_size):
        self.known = {}
        self.wide = lax.axis_index("wide")
        self.narrow = lax.axis_index("narrow")
        self.n_narrow = narrow_size
        self.wide_count = wide_size
        self.columns = wide_size // 2
        self.n_a = 2 if self.columns % 2 == 0 else 1
        self.n_b = self.columns // self.n_a
        self.core = lax.rem(self.wide, 2)
        column = self.wide // 2
        self.a = column // self.n_b
        self.b = lax.rem(column, self.n_b)
        self.coloured = self.n_a == self.n_b

    def index(self, a, b, core):
        return (a * self.n_b + b) * 2 + core

    @remembered
    def sibling(self):
        return self.wide + 1 - 2 * self.core

    @remembered
    def along_a(self, step):
        return self.index(lax.rem(self.a + step, self.n_a), self.b, self.core)

    @remembered
    def along_b(self, step):
        return self.index(self.a, lax.rem(self.b + step, self.n_b), self.core)

    def first_count(self):
        return self.n_b

    def second_count(self):
        return self.n_a

    @remembered
    def first(self, step):
        if not self.coloured:
            return self.along_b(step)
        return jnp.where(self.core == 0, self.along_b(step), self.along_a(step))

    @remembered
    def second(self, step):
        if not self.coloured:
            return self.along_a(step)
        return jnp.where(self.core == 0, self.along_a(step), self.along_b(step))

    @remembered
    def corner(self, first_step, second_step):
        if not self.coloured:
            return self.index(
                lax.rem(self.a + second_step, self.n_a),
                lax.rem(self.b + first_step, self.n_b),
                self.core,
            )
        step_a = jnp.where(self.core == 0, second_step, first_step)
        step_b = jnp.where(self.core == 0, first_step, second_step)
        return self.index(
            lax.rem(self.a + step_a, self.n_a), lax.rem(self.b + step_b, self.n_b), self.core
        )

    @remembered
    def depth(self, step):
        return lax.rem(self.narrow + step, self.n_narrow)

    @remembered
    def beside(self, first_step, second_step):
        step_a, step_b = second_step, first_step
        if self.coloured:
            step_a = jnp.where(self.core == 1, second_step, first_step)
            step_b = jnp.where(self.core == 1, first_step, second_step)
        return self.index(
            lax.rem(self.a + step_a, self.n_a), lax.rem(self.b + step_b, self.n_b), 1 - self.core
        )

    def greet(self):
        barrier = pltpu.get_barrier_semaphore()
        count = 0
        for step in range(1, self.n_narrow):
            pl.semaphore_signal(
                barrier, inc=1, device_id=(self.wide, self.depth(step)), device_id_type=MESH
            )
            count += 1
        for step in range(1, self.n_b):
            pl.semaphore_signal(
                barrier, inc=1, device_id=(self.along_b(step), self.narrow), device_id_type=MESH
            )
            count += 1
        for step in range(1, self.n_a):
            pl.semaphore_signal(
                barrier, inc=1, device_id=(self.along_a(step), self.narrow), device_id_type=MESH
            )
            count += 1
        pl.semaphore_signal(
            barrier, inc=1, device_id=(self.sibling(), self.narrow), device_id_type=MESH
        )
        pl.semaphore_wait(barrier, count + 1)


class Gather:
    def __init__(self, place, own, full, sems):
        self.place = place
        self.own = own
        self.full = full
        self.send, self.recv = sems
        self.rows = own.shape[0]
        self.pending = []
        p = place
        self.n_z = p.n_narrow - 1
        self.n_1 = (p.first_count() - 1) * p.n_narrow
        self.n_2 = (p.second_count() - 1) * p.first_count()

    def view(self, wide, narrow=None):
        n = self.place.n_narrow
        if narrow is None:
            start, size = wide * n * self.rows, n * self.rows
        else:
            start, size = (wide * n + narrow) * self.rows, self.rows
        return self.full.at[pl.ds(pl.multiple_of(start, self.rows), size), :]

    def copy(self, src, dst, slot, device):
        return pltpu.make_async_remote_copy(
            src_ref=src,
            dst_ref=dst,
            send_sem=self.send.at[slot],
            recv_sem=self.recv.at[slot],
            device_id=device,
            device_id_type=MESH,
        )

    def go(self, copy):
        copy.start()
        self.pending.append(copy)

    def landed(self, view, slot):
        self.copy(view, view, slot, (self.place.sibling(), self.place.narrow)).wait_recv()

    def slot_first(self, step, k):
        return self.n_z + (step - 1) * self.place.n_narrow + k

    def slot_second(self, step, k):
        return self.n_z + self.n_1 + (step - 1) * self.place.first_count() + k

    def slot_sibling(self, k):
        return self.n_z + self.n_1 + self.n_2 + k

    def stage_1(self):
        p = self.place
        for step in range(1, p.n_narrow):
            self.go(
                self.copy(
                    self.own,
                    self.view(p.wide, p.narrow),
                    step - 1,
                    (p.wide, p.depth(step)),
                )
            )
        for step in range(1, p.first_count()):
            self.go(
                self.copy(
                    self.own,
                    self.view(p.wide, p.narrow),
                    self.slot_first(step, 0),
                    (p.first(step), p.narrow),
                )
            )

    def stage_2(self):
        p = self.place
        for step in range(1, p.n_narrow):
            source = p.depth(p.n_narrow - step)
            view = self.view(p.wide, source)
            self.landed(view, step - 1)
            for hop in range(1, p.first_count()):
                self.go(
                    self.copy(view, view, self.slot_first(hop, step), (p.first(hop), p.narrow))
                )
        view = self.view(p.wide)
        for hop in range(1, p.second_count()):
            self.go(self.copy(view, view, self.slot_second(hop, 0), (p.second(hop), p.narrow)))
        self.go(self.copy(view, view, self.slot_sibling(0), (p.sibling(), p.narrow)))

    def stage_3(self):
        p = self.place
        for step in range(1, p.first_count()):
            column = p.first(p.first_count() - step)
            for k in range(p.n_narrow):
                source = p.depth(p.n_narrow - k)
                self.landed(self.view(column, source), self.slot_first(step, k))
            view = self.view(column)
            for hop in range(1, p.second_count()):
                self.go(
                    self.copy(view, view, self.slot_second(hop, step), (p.second(hop), p.narrow))
                )
            self.go(self.copy(view, view, self.slot_sibling(step), (p.sibling(), p.narrow)))

    def stage_4(self):
        p = self.place
        for hop in range(1, p.second_count()):
            back = p.second_count() - hop
            for k in range(p.first_count()):
                column = p.corner((p.first_count() - k) % p.first_count(), back)
                view = self.view(column)
                self.landed(view, self.slot_second(hop, k))
                slot = self.slot_sibling(hop * p.first_count() + k)
                self.go(self.copy(view, view, slot, (p.sibling(), p.narrow)))

    def stage_5(self):
        p = self.place
        for hop in range(p.second_count()):
            for k in range(p.first_count()):
                back_1 = (p.first_count() - k) % p.first_count()
                back_2 = (p.second_count() - hop) % p.second_count()
                column = p.beside(back_1, back_2)
                self.landed(self.view(column), self.slot_sibling(hop * p.first_count() + k))

    def drain(self):
        for copy in self.pending:
            copy.wait_send()


def gather_slots(wide_size, narrow_size):
    columns = wide_size // 2
    n_a = 2 if columns % 2 == 0 else 1
    n_b = columns // n_a
    return (narrow_size - 1) + (n_b - 1) * narrow_size + (n_a - 1) * n_b + n_a * n_b


class Scatter:
    def __init__(self, place, grad, out, bufs, sems):
        self.place = place
        self.grad = grad
        self.out = out
        self.held, self.from_sibling, self.from_second, self.from_first, self.from_depth = bufs
        self.send, self.recv, self.local = sems
        self.pending = []
        p = place
        self.n_1 = p.first_count()
        self.n_2 = p.second_count()
        self.blocks = self.n_1 * self.n_2
        self.rows = out.shape[0]
        self.store = partial(out.__setitem__, ...)

    def view(self, wide):
        size = self.place.n_narrow * self.rows
        return self.grad.at[pl.ds(pl.multiple_of(wide * size, size), size), :]

    def copy(self, src, dst, slot, device):
        return pltpu.make_async_remote_copy(
            src_ref=src,
            dst_ref=dst,
            send_sem=self.send.at[slot],
            recv_sem=self.recv.at[slot],
            device_id=device,
            device_id_type=MESH,
        )

    def go(self, copy):
        copy.start()
        self.pending.append(copy)

    def landed(self, ref, slot):
        self.copy(ref, ref, slot, (self.place.sibling(), self.place.narrow)).wait_recv()

    def loads(self):
        p = self.place
        result = []
        for s in range(self.n_2):
            for f in range(self.n_1):
                block = s * self.n_1 + f
                result.append(
                    pltpu.make_async_copy(
                        self.view(p.corner(f, s)), self.held.at[block], self.local.at[block]
                    )
                )
        return result

    def stage_0(self):
        p = self.place
        for s in range(self.n_2):
            for f in range(self.n_1):
                column = p.beside(f, s)
                block = s * self.n_1 + f
                self.go(
                    self.copy(
                        self.view(column),
                        self.from_sibling.at[block],
                        block,
                        (p.sibling(), p.narrow),
                    )
                )
        for load in self.loads():
            load.start()

    def add(self, block, *others):
        total = self.held[block]
        for other in others:
            total = total + other[...]
        self.held[block] = total

    def piece(self, narrow):
        return pl.ds(pl.multiple_of(narrow * self.rows, self.rows), self.rows)

    def stage_1(self):
        p = self.place
        for load in self.loads():
            load.wait()
        for block in range(self.blocks):
            self.landed(self.from_sibling.at[block], block)
        for s in range(self.n_2 - 1, -1, -1):
            for f in range(self.n_1):
                block = s * self.n_1 + f
                self.add(block, self.from_sibling.at[block])
                if s > 0:
                    slot = (s - 1) * self.n_1 + f
                    self.go(
                        self.copy(
                            self.held.at[block],
                            self.from_second.at[slot],
                            self.blocks + slot,
                            (p.second(s), p.narrow),
                        )
                    )

    def stage_2(self):
        p = self.place
        base = self.blocks + (self.n_2 - 1) * self.n_1
        for f in range(self.n_1 - 1, -1, -1):
            slots = [s * self.n_1 + f for s in range(self.n_2 - 1)]
            for slot in slots:
                self.landed(self.from_second.at[slot], self.blocks + slot)
            self.add(f, *[self.from_second.at[slot] for slot in slots])
            if f > 0:
                self.go(
                    self.copy(
                        self.held.at[f],
                        self.from_first.at[f - 1],
                        base + f - 1,
                        (p.first(f), p.narrow),
                    )
                )

    def stage_3(self):
        p = self.place
        first_base = self.blocks + (self.n_2 - 1) * self.n_1
        base = first_base + self.n_1 - 1
        for f in range(1, self.n_1):
            self.landed(self.from_first.at[f - 1], first_base + f - 1)
        self.add(0, *[self.from_first.at[f - 1] for f in range(1, self.n_1)])
        for step in range(1, p.n_narrow):
            self.go(
                self.copy(
                    self.held.at[0, self.piece(p.depth(step)), :],
                    self.from_depth.at[step - 1],
                    base + step - 1,
                    (p.wide, p.depth(step)),
                )
            )

    def stage_4(self):
        p = self.place
        base = self.blocks + (self.n_2 - 1) * self.n_1 + self.n_1 - 1
        for step in range(1, p.n_narrow):
            self.landed(self.from_depth.at[step - 1], base + step - 1)
        total = self.held[0, self.piece(p.narrow), :].astype(F32)
        for step in range(1, p.n_narrow):
            total = total + self.from_depth[step - 1].astype(F32)
        self.store(total)

    def drain(self):
        for copy in self.pending:
            copy.wait_send()


def scatter_slots(wide_size, narrow_size):
    columns = wide_size // 2
    n_a = 2 if columns % 2 == 0 else 1
    n_b = columns // n_a
    return n_a * n_b + (n_a - 1) * n_b + (n_b - 1) + (narrow_size - 1)


D = 1024
HEADS = 8
HD = 128
GROUP = 128
EPSILON = 1e-05
SCALE = HD ** (-0.5)
NN = (((1,), (0,)), ((), ()))
NT = (((1,), (1,)), ((), ()))
TN = (((0,), (0,)), ((), ()))

U_Q, U_K, U_V, U_CO, U_SQ, U_SK, U_SV, U_SO, U_D, U_U = 0, 1, 2, 3, 4, 5, 6, 7, 8, 9
UNITS = 16
VECTORS = 16
V_CG, V_CS, V_IG, V_IS, V_SG, V_SS, V_MG, V_MS, V_BD, V_BU = range(10)
(S_LAT, S_SRC, S_Q, S_K, S_V, S_MIX, S_SL, S_SQ, S_SK, S_SV, S_SMIX) = range(11)


def dot(left, right, dims=NN):
    return lax.dot_general(left, right, dims, preferred_element_type=F32)


def for_each(count, step, unroll=1):
    def run(i, carry):
        step(i)
        return carry

    lax.fori_loop(0, count, run, 0, unroll=unroll)


def part(i, size):
    return pl.ds(pl.multiple_of(i * size, size), size)


def gather_units(sizes, shards):
    rows = D // (sizes[0] * sizes[1])
    q, kv, co, qkv, so, down, up = range(7)
    units = [(q, 0, 0), (kv, 0, 0), (kv, 0, 1), (co, 0, 0), (qkv, 0, 0), (qkv, 0, 1), (qkv, 0, 2)]
    units.append((so, 0, 0))
    for i in range(4):
        units.append((down, i * rows, 0))
        units.append((up, 0, i))
    return rows, units


def norm_stats(x):
    mean = jnp.mean(x, axis=-1, keepdims=True)
    center = x - mean
    spread = jnp.mean(center * center, axis=-1, keepdims=True)
    return center, lax.rsqrt(spread + EPSILON)


def group_mask(row_ids, column_ids):
    across = jnp.broadcast_to(row_ids.astype(F32), (GROUP, GROUP)).T
    return across == jnp.broadcast_to(column_ids.astype(F32), (GROUP, GROUP))


def softmax_columns(scores):
    raised = jnp.exp(scores - jnp.max(scores, axis=0, keepdims=True))
    return raised * (1.0 / jnp.sum(raised, axis=0, keepdims=True))


HEAD_COLUMNS = [slice(h * HD, (h + 1) * HD) for h in range(HEADS)]
HALVES = (slice(0, 512), slice(512, 1024))


def gelu_parts(x):
    half = 0.5 * (1.0 + lax.erf(x * (2.0**-0.5)))
    return x * half, half + x * (jnp.exp(-0.5 * x * x) * ((2.0 * jnp.pi) ** -0.5))


def reorder_up(pool, raw, stage, rows):
    lane = lax.broadcasted_iota(jnp.int32, (rows, 128), 1)
    for i in range(4):
        for g in range(D // 128):
            total = jnp.zeros((rows, 128), F32)
            for k in range(128 // rows):
                column = (g * (128 // rows) + k) * 4 * rows + i * rows
                block, inside = divmod(column, D)
                group, offset = divmod(inside, 128)
                piece = pool[raw, pl.ds(block * rows, rows), group * 128 : (group + 1) * 128]
                piece = piece.astype(F32)
                shift = (k * rows - offset) % 128
                if shift:
                    piece = pltpu.roll(piece, shift, axis=1)
                total = jnp.where(lane // rows == k, piece, total)
            unit = U_U + 2 * i
            pool[stage, pl.ds(unit * rows, rows), g * 128 : (g + 1) * 128] = total.astype(BF16)


def restore_up(out, value, i, rows):
    for g in range(D // 128):
        lanes = value[:, g * 128 : (g + 1) * 128]
        for k in range(128 // rows):
            column = (g * (128 // rows) + k) * 4 * rows + i * rows
            offset = column % 128
            shift = (offset - k * rows) % 128
            piece = pltpu.roll(lanes, shift, axis=1) if shift else lanes
            out[:, column : column + rows] = piece[:, offset : offset + rows]


class Ticks:
    def __init__(self, jobs):
        self.jobs = jobs
        self.done = 0
        self.last = len(jobs) + 3

    def one(self):
        t = self.done
        if t >= self.last:
            return
        for back, stage in ((3, "stage_5"), (2, "stage_4"), (1, "stage_3"), (0, "stage_2"), (-1, "stage_1")):
            if 0 <= t - back < len(self.jobs):
                getattr(self.jobs[t - back], stage)()
        self.done = t + 1

    def until(self, job):
        while self.done < job + 4:
            self.one()


HELD = 5
FROM = 4
NEAR = 3
(G_SO, G_SQ, G_SK, G_SV, G_CO, G_Q, G_K, G_V) = range(8)


def fold_rows(value):
    return jnp.sum(value.reshape(-1, 8, D), axis=0)


def scatter_targets():
    targets = []
    for i in range(4):
        targets.append((0, i, 0))
        targets.append((1, 0, i))
    targets.append((2, 0, 0))
    for c in range(3):
        targets.append((3, 0, c))
    targets += [(4, 0, 0), (5, 0, 0), (6, 0, 0), (6, 0, 1)]
    return targets


class Sums:
    STAGES = ("stage_0", "stage_1", "stage_2", "stage_3", "stage_4")

    def __init__(self, jobs, credit, place):
        self.jobs = jobs
        self.credit = credit
        self.place = place
        self.stage = [0] * len(jobs)
        self.started = 0
        self.drained = 0
        self.waits = {}

    def one(self, start=True):
        big = len(self.jobs) - 1
        running = [j for j in range(self.started) if self.stage[j] < 5]
        if start and self.started < len(self.jobs):
            j = self.started
            for copy in self.waits.pop(j, ()):
                copy.wait()
            if j < big and j >= NEAR:
                pl.semaphore_wait(self.credit, 1)
            if j < big and j >= HELD:
                self.jobs[j - HELD].drain()
                self.drained = j - HELD + 1
            running.append(j)
            self.started += 1
        for j in running[::-1]:
            getattr(self.jobs[j], self.STAGES[self.stage[j]])()
            if self.stage[j] == 1 and j + NEAR < big:
                pl.semaphore_signal(
                    self.credit,
                    inc=1,
                    device_id=(self.place.sibling(), self.place.narrow),
                    device_id_type=MESH,
                )
            self.stage[j] += 1

    def finish(self):
        while self.started < len(self.jobs) or self.stage[-1] < 5:
            self.one()
        for job in self.jobs[self.drained :]:
            job.drain()


def layer_kernel(sizes, *refs):
    vec_shard, shards, rest = refs[0], refs[1:8], refs[8:]
    latents, inputs, cot, lat_ids, in_ids = rest[:5]
    finished, latent_grad, input_grad, full, vec_full, kept, kept_f, g_mlp, g_att, vec_sent = rest[5:15]
    vec_out, *outs = rest[15:23]
    (
        vec_staged,
        vec_all,
        vec,
        small,
        pool,
        fpool,
        vacc,
        held,
        near,
        from_second,
        from_first,
        from_depth,
        vheld,
        vnear,
        vsecond,
        vfirst,
        vdepth,
        send,
        recv,
        vsend,
        vrecv,
        rsend,
        rrecv,
        local,
        credit,
        sem_stage,
        sem_own,
        sem_in,
        sem_w,
        sem_f,
        sem_keep,
        sem_keep_f,
        sem_g,
        sem_o,
    ) = rest[23:]
    place = Place(*sizes)
    rows, units = gather_units(sizes, shards)
    mine = place.wide * place.n_narrow + place.narrow

    LAT, INP, LLOW, SLOW, Q, K, V, MIX = 0, 1, 2, 3, 8, 9, 10, 11
    W0 = 4
    SELF = (12, 13, 4, 5)
    ML, COT = 2, 3
    STAGE, RAW = 13, 12

    copies_in = [
        pltpu.make_async_copy(latents, pool.at[LAT], sem_in.at[0]),
        pltpu.make_async_copy(inputs, pool.at[INP], sem_in.at[1]),
    ]
    stage_in = []
    for u, (k, r0, c0) in enumerate(units):
        source = shards[k].at[pl.ds(r0, rows), pl.ds(c0 * D, D)]
        target = pool.at[RAW, part(c0, rows), :] if k == 6 else pool.at[STAGE, part(u, rows), :]
        stage_in.append(pltpu.make_async_copy(source, target, sem_stage.at[u]))
    stage_in.append(pltpu.make_async_copy(vec_shard, vec_staged, sem_stage.at[UNITS]))
    own_out = [
        pltpu.make_async_copy(
            pool.at[STAGE, part(u, rows), :], full.at[u, part(mine, rows), :], sem_own.at[u]
        )
        for u in range(UNITS)
    ]
    own_out.append(
        pltpu.make_async_copy(vec_staged, vec_full.at[part(mine, VECTORS), :], sem_own.at[UNITS])
    )
    for copy in stage_in[::-1]:
        copy.start()
    for copy in copies_in:
        copy.start()
    place.greet()
    jobs = [Gather(place, vec_shard, vec_full, (vsend, vrecv))]
    for u, (k, r0, c0) in enumerate(units):
        source = shards[k].at[pl.ds(r0, rows), pl.ds(c0 * D, D)]
        if k == 6:
            source = full.at[u, part(mine, rows), :]
        jobs.append(Gather(place, source, full.at[u], (send.at[u], recv.at[u])))
    ticks = Ticks(jobs)
    limit = [0]
    sum_jobs = []
    for i, (p, r, c) in enumerate(scatter_targets()):
        grad = g_mlp.at[i] if i < 8 else g_att.at[i - 8]
        out = outs[p].at[pl.ds(r * rows, rows), pl.ds(c * D, D)]
        turn = i % HELD
        bufs = (
            held.at[turn],
            near.at[i % NEAR],
            from_second.at[i % FROM],
            from_first.at[i % FROM],
            from_depth.at[i % FROM],
        )
        sum_jobs.append(Scatter(place, grad, out, bufs, (rsend.at[i], rrecv.at[i], local.at[i])))
        if p == 1:
            sum_jobs[-1].store = partial(restore_up, outs[1], i=c, rows=rows)
    sum_jobs.append(
        Scatter(
            place,
            vec_sent,
            vec_out,
            (vheld, vnear, vsecond, vfirst, vdepth),
            (rsend.at[UNITS], rrecv.at[UNITS], local.at[UNITS]),
        )
    )
    sums = Sums(sum_jobs, credit, place)

    def tick():
        sums.one(start=sums.started < limit[0])

    jobs[0].stage_1()
    for i in range(UNITS, -1, -1):
        stage_in[i].wait()
    reorder_up(pool, RAW, STAGE, rows)
    for i in range(UNITS, -1, -1):
        own_out[i].start()
    for i in range(UNITS, -1, -1):
        own_out[i].wait()

    def load(unit, slot):
        return pltpu.make_async_copy(full.at[unit], pool.at[slot], sem_w.at[slot])

    def fetch(unit, slot):
        ticks.until(unit + 1)
        load(unit, slot).start()

    def keep(slot, index):
        return pltpu.make_async_copy(pool.at[slot], kept.at[index], sem_keep.at[index])

    def keep_f(slot, index):
        return pltpu.make_async_copy(fpool.at[slot], kept_f.at[index], sem_keep_f.at[index])

    def vector(k, columns=slice(None)):
        return vec[k : k + 1, columns]

    ticks.until(0)
    copy = pltpu.make_async_copy(vec_full, vec_all, sem_in.at[2])
    copy.start()
    copy.wait()
    lane_groups = D // 128
    per = place.wide_count * place.n_narrow // lane_groups
    for g in range(lane_groups):
        total = vec_all[pl.ds(g * per * VECTORS, VECTORS), :]
        for j in range(1, per):
            total = total + vec_all[pl.ds((g * per + j) * VECTORS, VECTORS), :]
        vec[:, g * 128 : (g + 1) * 128] = total

    def norm_low(read, slot, gain, shift):
        def step(i):
            sl = part(i, 64)
            center, rate = norm_stats(read(sl))
            pool[slot, sl, :] = (center * rate * vector(gain) + vector(shift)).astype(BF16)

        for_each(16, step)

    def product(out, left, weight):
        values = [dot(pool[left], pool[weight, :, sl]) for sl in HALVES]
        for sl, value in zip(HALVES, values):
            pool[out, :, sl] = value.astype(BF16)

    def attend(q, k, v, out, ids, groups):
        def step(g):
            sl = part(g, GROUP)
            mask = group_mask(ids[pl.ds(g, 1), :], lat_ids[pl.ds(g, 1), :])
            scores = [dot(pool[k, sl, hs], pool[q, sl, hs], NT) for hs in HEAD_COLUMNS]
            weights = [softmax_columns(jnp.where(mask, x * SCALE, -1e30)).astype(BF16) for x in scores]
            mixed = [dot(x, pool[v, sl, hs], TN) for x, hs in zip(weights, HEAD_COLUMNS)]
            for x, hs in zip(mixed, HEAD_COLUMNS):
                pool[out, sl, hs] = x.astype(BF16)

        lo, hi = groups

        def run(g, carry):
            step(g)
            return carry

        lax.fori_loop(lo, hi, run, 0)

    copies_in[0].wait()
    norm_low(lambda sl: pool[LAT, sl, :].astype(F32), LLOW, V_CG, V_CS)
    keep(LLOW, S_LAT).start()
    fetch(U_Q, W0)
    copies_in[1].wait()
    norm_low(lambda sl: pool[INP, sl, :].astype(F32), SLOW, V_IG, V_IS)
    keep(SLOW, S_SRC).start()
    load(U_Q, W0).wait()
    product(Q, LLOW, W0)
    keep(Q, S_Q).start()
    fetch(U_K, W0 + 1)
    load(U_K, W0 + 1).wait()
    product(K, SLOW, W0 + 1)
    keep(K, S_K).start()
    fetch(U_V, W0 + 2)
    load(U_V, W0 + 2).wait()
    product(V, SLOW, W0 + 2)
    keep(V, S_V).start()
    attend(Q, K, V, MIX, in_ids, (0, 4))
    fetch(U_CO, W0 + 3)
    attend(Q, K, V, MIX, in_ids, (4, 8))
    keep(MIX, S_MIX).start()
    load(U_CO, W0 + 3).wait()

    values = [dot(pool[MIX], pool[W0 + 3, :, sl]) for sl in HALVES]
    for sl, value in zip(HALVES, values):
        fpool[0, :, sl] = pool[LAT, :, sl].astype(F32) + value
    keep_f(0, 0).start()
    fetch(U_SQ, SELF[0])
    norm_low(lambda sl: fpool[0, sl, :], LAT, V_SG, V_SS)
    keep(LAT, S_SL).start()
    keep(Q, S_Q).wait()
    keep(K, S_K).wait()
    keep(V, S_V).wait()
    for offset, (slot, index, before) in enumerate(((Q, S_SQ, 0), (K, S_SK, 0), (V, S_SV, 0))):
        load(U_SQ + offset, SELF[offset]).wait()
        product(slot, LAT, SELF[offset])
        keep(slot, index).start()
        fetch(U_SQ + offset + 1, SELF[offset + 1])
    keep(MIX, S_MIX).wait()
    attend(Q, K, V, MIX, lat_ids, (0, 4))
    ticks.one()
    attend(Q, K, V, MIX, lat_ids, (4, 8))
    keep(MIX, S_SMIX).start()
    load(U_SO, SELF[3]).wait()

    values = [dot(pool[MIX], pool[SELF[3], :, sl]) for sl in HALVES]
    for sl, value in zip(HALVES, values):
        fpool[1, :, sl] = fpool[0, :, sl] + value
    keep_f(1, 1).start()
    keep(LLOW, S_LAT).wait()
    keep(SLOW, S_SRC).wait()
    cot_in = pltpu.make_async_copy(cot, pool.at[COT], sem_in.at[3])
    cot_in.start()
    norm_low(lambda sl: fpool[1, sl, :], ML, V_MG, V_MS)
    cot_in.wait()
    for slot, index in ((LAT, S_SL), (Q, S_SQ), (K, S_SK), (V, S_SV), (MIX, S_SMIX)):
        keep(slot, index).wait()
    keep_f(1, 1).wait()
    keep_f(0, 0).wait()

    ACT, GH = 8, 9
    PAIR = (6, 4)
    GD, GU = 10, 12
    GIN = 0
    CH = 512
    R = 256
    small[...] = jnp.zeros_like(small)

    def spread(chunk):
        i, h = divmod(chunk, 2)
        down, up = PAIR[i % 2], PAIR[i % 2] + 1
        cols = pl.ds(h * CH, CH)
        values = dot(pool[ML], pool[up, :, cols]), dot(pool[COT], pool[down, cols, :], NT)
        fpool[2, :, 0:CH] = values[0]
        fpool[2, :, CH : 2 * CH] = values[1]

    def bend(chunk, sl):
        i, h = divmod(chunk, 2)
        cols = pl.ds(h * CH, CH)
        value, slope = gelu_parts(fpool[2, sl, 0:CH] + vec[V_BU + i : V_BU + i + 1, cols])
        value, grad = value.astype(BF16), (slope * fpool[2, sl, CH : 2 * CH]).astype(BF16)
        total = jnp.sum(grad.astype(F32), axis=0, keepdims=True)

        def store():
            out = pl.ds((chunk % 2) * CH, CH)
            pool[ACT, sl, out] = value
            pool[GH, sl, out] = grad
            small[i : i + 1, cols] += total

        return store

    def fold(chunk, sl):
        i, h = divmod(chunk, 2)
        down, up = PAIR[i % 2], PAIR[i % 2] + 1
        cols = pl.ds(h * CH, CH)
        out = pl.ds((chunk % 2) * CH, CH)
        result = fpool[1, sl, :] + dot(pool[ACT, sl, out], pool[down, cols, :])
        grad = dot(pool[GH, sl, out], pool[up, :, cols], NT)
        if chunk > 0:
            grad = grad + fpool[GIN, sl, :]

        def store():
            fpool[1, sl, :] = result
            fpool[GIN, sl, :] = grad

        return store

    def grad_out(i):
        return [
            pltpu.make_async_copy(pool.at[GD + i % 2], g_mlp.at[2 * i], sem_g.at[2 * i]),
            pltpu.make_async_copy(pool.at[GU + i % 2], g_mlp.at[2 * i + 1], sem_g.at[2 * i + 1]),
        ]

    def weigh(chunk):
        i, h = divmod(chunk, 2)
        cols = pl.ds(h * CH, CH)
        out = pl.ds((chunk % 2) * CH, CH)
        down = dot(pool[ACT, :, out], pool[COT], TN)
        up = dot(pool[ML], pool[GH, :, out], TN)
        pool[GD + i % 2, cols, :] = down.astype(BF16)
        pool[GU + i % 2, :, cols] = up.astype(BF16)

    def fetch_pair(i):
        fetch(U_D + 2 * i, PAIR[i % 2])
        fetch(U_U + 2 * i, PAIR[i % 2] + 1)

    for chunk in range(8):
        i, h = divmod(chunk, 2)
        if h == 0:
            if i == 0:
                fetch_pair(0)
            load(U_D + 2 * i, PAIR[i % 2]).wait()
            load(U_U + 2 * i, PAIR[i % 2] + 1).wait()
            spread(chunk)
            ticks.one()
        else:
            spread(chunk)
            if i < 3:
                fetch_pair(i + 1)

        def rows_step(r):
            sl = part(r, R)
            stores = [bend(chunk, sl)]
            if chunk > 0:
                stores.append(fold(chunk - 1, sl))
            for store in stores:
                store()

        for_each(D // R, rows_step)
        if h == 0 and i >= 2:
            for job in (2 * i - 4, 2 * i - 3):
                for copy in sums.waits.pop(job, ()):
                    copy.wait()
        weigh(chunk)
        if h == 1:
            for job, copy in enumerate(grad_out(i), 2 * i):
                copy.start()
                sums.waits[job] = (copy,)
            limit[0] = 2 * i + 2
        if chunk >= 3:
            tick()

    A, B, C, DD, E, F, G, S1, S2 = 9, 1, 5, COT, 6, 7, 0, GD, GU

    def load_f(index, slot):
        return pltpu.make_async_copy(kept_f.at[index], fpool.at[slot], sem_f.at[slot])

    def bring(source, slot):
        return pltpu.make_async_copy(source, pool.at[slot], sem_w.at[slot])

    first = [
        bring(kept.at[S_SMIX], B),
        bring(kept.at[S_SQ], E),
        bring(kept.at[S_SK], F),
        bring(kept.at[S_SV], G),
        bring(full.at[U_SO], C),
        load_f(1, 1),
    ]

    def last(r):
        sl = part(r, R)
        fold(7, sl)()
        pool[ML, sl, :] = (fpool[1, sl, :] + vector(V_BD)).astype(BF16)

    for copy in first[:4]:
        copy.start()
    for_each(D // R, last)
    first[4].start()
    first[5].start()
    done = pltpu.make_async_copy(pool.at[ML], finished, sem_in.at[4])
    done.start()
    while ticks.done < ticks.last:
        ticks.one()
    for job in jobs:
        job.drain()

    vacc[...] = jnp.zeros_like(vacc)

    def norm_back(read_x, grad_slot, gain, shift, write):
        def step(i, carry):
            sl = part(i, 64)
            center, rate = norm_stats(read_x(sl))
            normal = center * rate
            grad = fpool[grad_slot, sl, :]
            sums_gain = carry[0] + fold_rows(grad * normal)
            sums_shift = carry[1] + fold_rows(grad)
            grad = grad * vec[gain : gain + 1, :]
            mean_1 = jnp.mean(grad, axis=-1, keepdims=True)
            mean_2 = jnp.mean(grad * normal, axis=-1, keepdims=True)
            write(sl, rate * (grad - mean_1 - normal * mean_2))
            return sums_gain, sums_shift

        zero = jnp.zeros((8, D), F32)
        carry = (zero, zero)
        carry = lax.fori_loop(0, 16, step, carry)
        vacc[gain] = carry[0]
        vacc[shift] = carry[1]
        tick()

    staging = [S1, S2]
    saved = [4, 5]

    def weight_grad(index, left, right):
        turn = index % 2
        if saved[turn] is not None and saved[turn] in sums.waits:
            for copy in sums.waits.pop(saved[turn]):
                copy.wait()
        slot = staging[turn]

        values = [dot(pool[left], pool[right, :, sl], TN) for sl in HALVES]
        for sl, value in zip(HALVES, values):
            pool[slot, :, sl] = value.astype(BF16)
        copy = pltpu.make_async_copy(pool.at[slot], g_att.at[index], sem_g.at[8 + index])
        copy.start()
        sums.waits[8 + index] = (copy,)
        saved[turn] = 8 + index
        limit[0] = 8 + index + 1

    def back_product(out, left, weight):
        values = [dot(pool[left], pool[weight, sl, :], NT) for sl in HALVES]
        for sl, value in zip(HALVES, values):
            pool[out, :, sl] = value.astype(BF16)

    def back_sum(out, left, weight, fresh):
        values = [dot(pool[left], pool[weight, sl, :], NT) for sl in HALVES]
        if not fresh:
            values = [value + fpool[out, :, sl] for sl, value in zip(HALVES, values)]
        for sl, value in zip(HALVES, values):
            fpool[out, :, sl] = value

    def attend_back(q, k, v, grad, ids):
        def step(g, carry):
            sl = part(g, GROUP)
            mask = group_mask(ids[pl.ds(g, 1), :], lat_ids[pl.ds(g, 1), :])
            scores = [dot(pool[k, sl, hs], pool[q, sl, hs], NT) for hs in HEAD_COLUMNS]
            slopes = [dot(pool[v, sl, hs], pool[grad, sl, hs], NT) for hs in HEAD_COLUMNS]
            weights = [softmax_columns(jnp.where(mask, x * SCALE, -1e30)) for x in scores]
            inner = [jnp.sum(x * y, axis=0, keepdims=True) for x, y in zip(weights, slopes)]
            slopes = [(x * (y - z)).astype(BF16) for x, y, z in zip(weights, slopes, inner)]
            weights = [x.astype(BF16) for x in weights]
            grad_v = [dot(x, pool[grad, sl, hs]) for x, hs in zip(weights, HEAD_COLUMNS)]
            grad_k = [dot(x, pool[q, sl, hs]) * SCALE for x, hs in zip(slopes, HEAD_COLUMNS)]
            grad_q = [dot(x, pool[k, sl, hs], TN) * SCALE for x, hs in zip(slopes, HEAD_COLUMNS)]
            for slot, values in ((v, grad_v), (k, grad_k), (q, grad_q)):
                for x, hs in zip(values, HEAD_COLUMNS):
                    pool[slot, sl, hs] = x.astype(BF16)
            return carry

        lax.fori_loop(0, 8, step, 0)
        tick()

    first[5].wait()

    def after_self(sl, grad):
        cot_rows = pool[DD, sl, :].astype(F32)
        vacc[V_BD] += fold_rows(cot_rows)
        total = cot_rows + grad
        fpool[2, sl, :] = total
        pool[A, sl, :] = total.astype(BF16)

    norm_back(lambda sl: fpool[1, sl, :], 0, V_MG, V_MS, after_self)
    load_f(0, 1).start()

    for copy in first[:5]:
        copy.wait()
    weight_grad(G_SO, B, A)
    bring(kept.at[S_SL], B).start()
    back_product(DD, A, C)
    bring(full.at[U_SQ], A).start()
    bring(full.at[U_SK], C).start()
    tick()
    attend_back(E, F, G, DD, lat_ids)
    bring(full.at[U_SV], DD).start()
    bring(kept.at[S_SL], B).wait()
    for index, slot, weight, unit in ((G_SQ, E, A, U_SQ), (G_SK, F, C, U_SK), (G_SV, G, DD, U_SV)):
        weight_grad(index, B, slot)
        bring(full.at[unit], weight).wait()
        back_sum(0, slot, weight, index == G_SQ)
        tick()
        if index == G_SQ:
            bring(kept.at[S_Q], E).start()
            bring(full.at[U_CO], A).start()
        elif index == G_SK:
            bring(kept.at[S_K], F).start()
        else:
            bring(kept.at[S_V], G).start()
            bring(kept.at[S_MIX], B).start()
    load_f(0, 1).wait()

    def after_cross(sl, grad):
        total = fpool[2, sl, :] + grad
        fpool[2, sl, :] = total
        pool[C, sl, :] = total.astype(BF16)

    norm_back(lambda sl: fpool[1, sl, :], 0, V_SG, V_SS, after_cross)

    bring(kept.at[S_MIX], B).wait()
    weight_grad(G_CO, B, C)
    bring(kept.at[S_LAT], B).start()
    bring(full.at[U_CO], A).wait()
    back_product(DD, C, A)
    bring(full.at[U_Q], A).start()
    bring(kept.at[S_SRC], C).start()
    tick()
    bring(kept.at[S_Q], E).wait()
    bring(kept.at[S_K], F).wait()
    bring(kept.at[S_V], G).wait()
    attend_back(E, F, G, DD, in_ids)
    bring(full.at[U_K], DD).start()
    bring(kept.at[S_LAT], B).wait()
    weight_grad(G_Q, B, E)
    bring(latents, B).start()
    tick()
    bring(kept.at[S_SRC], C).wait()
    weight_grad(G_K, C, F)
    tick()
    weight_grad(G_V, C, G)
    bring(inputs, C).start()
    tick()
    bring(full.at[U_Q], A).wait()
    back_sum(0, E, A, True)
    bring(full.at[U_V], A).start()
    bring(latents, B).wait()

    def latent_out(sl, grad):
        pool[E, sl, :] = (fpool[2, sl, :] + grad).astype(BF16)

    norm_back(lambda sl: pool[B, sl, :].astype(F32), 0, V_CG, V_CS, latent_out)
    done_1 = pltpu.make_async_copy(pool.at[E], latent_grad, sem_o.at[0])
    done_1.start()
    bring(full.at[U_K], DD).wait()
    back_sum(1, F, DD, True)
    bring(full.at[U_V], A).wait()
    back_sum(1, G, A, False)
    bring(inputs, C).wait()

    def input_out(sl, grad):
        pool[F, sl, :] = grad.astype(BF16)

    norm_back(lambda sl: pool[C, sl, :].astype(F32), 1, V_IG, V_IS, input_out)
    done_2 = pltpu.make_async_copy(pool.at[F], input_grad, sem_o.at[1])
    done_2.start()

    lane_groups = D // 128
    per = sizes[0] * sizes[1] // lane_groups
    for k in range(9):
        vacc[k, 0:1, :] = jnp.sum(vacc[k], axis=0, keepdims=True)
    for g in range(lane_groups):
        lanes = slice(g * 128, (g + 1) * 128)
        block = [vacc[k, 0:1, lanes] for k in range(9)]
        block += [small[0:4, lanes], jnp.zeros((3, 128), F32)]
        block = jnp.concatenate(block, axis=0)

        def put(j, carry):
            vec_all[part(g * per + j, VECTORS), :] = block
            return carry

        lax.fori_loop(0, per, put, 0)
    copy = pltpu.make_async_copy(vec_all, vec_sent, sem_o.at[2])
    copy.start()
    copy.wait()
    limit[0] = len(sum_jobs)
    sums.finish()
    done.wait()
    done_1.wait()
    done_2.wait()


def run_layer(vec_shard, shards, latents, inputs, cot, lat_ids, in_ids):
    sizes = (lax.axis_size("wide"), lax.axis_size("narrow"))
    everyone = sizes[0] * sizes[1]
    rows = D // everyone
    columns = sizes[0] // 2
    n_2 = 2 if columns % 2 == 0 else 1
    n_1 = columns // n_2
    n = sizes[1]
    widths = ((4 * rows, D), (rows, 4 * D), (rows, D), (rows, 3 * D), (rows, D), (rows, D), (rows, 2 * D))
    gslots = gather_slots(*sizes)
    slots = scatter_slots(*sizes)
    any_spec = pl.BlockSpec(memory_space=pl.ANY)
    vmem_spec = pl.BlockSpec(memory_space=pltpu.VMEM)
    dma = pltpu.SemaphoreType.DMA
    total = UNITS + 1
    return pl.pallas_call(
        partial(layer_kernel, sizes),
        out_shape=[
            jax.ShapeDtypeStruct((D, D), BF16),
            jax.ShapeDtypeStruct((D, D), BF16),
            jax.ShapeDtypeStruct((D, D), BF16),
            jax.ShapeDtypeStruct((UNITS, D, D), BF16),
            jax.ShapeDtypeStruct((everyone * VECTORS, 128), F32),
            jax.ShapeDtypeStruct((11, D, D), BF16),
            jax.ShapeDtypeStruct((2, D, D), F32),
            jax.ShapeDtypeStruct((8, D, D), BF16),
            jax.ShapeDtypeStruct((8, D, D), BF16),
            jax.ShapeDtypeStruct((everyone * VECTORS, 128), F32),
            jax.ShapeDtypeStruct((VECTORS, 128), F32),
        ]
        + [jax.ShapeDtypeStruct(shape, F32) for shape in widths],
        in_specs=[any_spec] * 11 + [vmem_spec] * 2,
        out_specs=[any_spec] * 10 + [vmem_spec] * 8,
        scratch_shapes=[
            pltpu.VMEM((VECTORS, 128), F32),
            pltpu.VMEM((everyone * VECTORS, 128), F32),
            pltpu.VMEM((VECTORS, D), F32),
            pltpu.VMEM((8, D), F32),
            pltpu.VMEM((14, D, D), BF16),
            pltpu.VMEM((3, D, D), F32),
            pltpu.VMEM((9, 8, D), F32),
            pltpu.VMEM((HELD, columns, n * rows, D), BF16),
            pltpu.VMEM((NEAR, columns, n * rows, D), BF16),
            pltpu.VMEM((FROM, (n_2 - 1) * n_1, n * rows, D), BF16),
            pltpu.VMEM((FROM, n_1 - 1, n * rows, D), BF16),
            pltpu.VMEM((FROM, n - 1, rows, D), BF16),
            pltpu.VMEM((columns, n * VECTORS, 128), F32),
            pltpu.VMEM((columns, n * VECTORS, 128), F32),
            pltpu.VMEM(((n_2 - 1) * n_1, n * VECTORS, 128), F32),
            pltpu.VMEM((n_1 - 1, n * VECTORS, 128), F32),
            pltpu.VMEM((n - 1, VECTORS, 128), F32),
            dma((UNITS, gslots)),
            dma((UNITS, gslots)),
            dma((gslots,)),
            dma((gslots,)),
            dma((total, slots)),
            dma((total, slots)),
            dma((total, columns)),
            pltpu.SemaphoreType.REGULAR,
            dma((UNITS + 1,)),
            dma((UNITS + 1,)),
            dma((5,)),
            dma((14,)),
            dma((3,)),
            dma((11,)),
            dma((2,)),
            dma((16,)),
            dma((3,)),
        ],
        compiler_params=pltpu.CompilerParams(
            collective_id=0, has_side_effects=True, vmem_limit_bytes=67_043_328
        ),
        name="layer",
    )(vec_shard, *shards, latents, inputs, cot, lat_ids, in_ids)


def body(
    latents,
    group_inputs,
    latent_images,
    input_images,
    cotangent,
    cross_gain,
    cross_shift,
    source_gain,
    source_shift,
    query_weight,
    keyval_weight,
    cross_out_weight,
    self_gain,
    self_shift,
    self_qkv_weight,
    self_out_weight,
    mlp_gain,
    mlp_shift,
    up_weight,
    up_bias,
    down_weight,
    down_bias,
):
    lat_ids = latent_images.reshape(-1, GROUP)
    in_ids = input_images.reshape(-1, GROUP)
    short = cross_gain.shape[0]
    per = 128 // short
    me = lax.axis_index(("wide", "narrow"))
    vectors = (
        cross_gain,
        cross_shift,
        source_gain,
        source_shift,
        self_gain,
        self_shift,
        mlp_gain,
        mlp_shift,
        down_bias,
    )
    stacked = jnp.concatenate(
        [jnp.stack(vectors), up_bias.reshape(4, short), jnp.zeros((3, short), BF16)]
    ).astype(F32)
    lane = lax.broadcasted_iota(jnp.int32, (VECTORS, 128), 1) // short
    packed = jnp.where(lane == lax.rem(me, per), jnp.tile(stacked, (1, per)), 0.0)
    finished, latent_grad, input_grad, *_, own_vec, g_down, g_up, g_so, g_qkv, g_co, g_q, g_kv = run_layer(
        packed,
        (
            query_weight,
            keyval_weight,
            cross_out_weight,
            self_qkv_weight,
            self_out_weight,
            down_weight,
            up_weight,
        ),
        latents,
        group_inputs,
        cotangent,
        lat_ids,
        in_ids,
    )
    vec = lax.dynamic_slice_in_dim(own_vec, lax.rem(me, per) * short, short, axis=1)
    own_up_bias = vec[9:13].reshape(-1)
    return (
        finished,
        latent_grad,
        input_grad,
        vec[0],
        vec[1],
        vec[2],
        vec[3],
        g_q,
        g_kv,
        g_co,
        vec[4],
        vec[5],
        g_qkv,
        g_so,
        vec[6],
        vec[7],
        g_up,
        own_up_bias,
        g_down,
        vec[8],
    )


def solution(mesh):
    rows = P(("wide", "narrow"), None)
    line = P(("wide", "narrow"))
    return jax.shard_map(
        body,
        mesh=mesh,
        in_specs=(rows,) * 5
        + (line,) * 4
        + (rows,) * 3
        + (line,) * 2
        + (rows,) * 2
        + (line,) * 2
        + (rows, line, rows, line),
        out_specs=(rows,) * 3
        + (line,) * 4
        + (rows,) * 3
        + (line,) * 2
        + (rows,) * 2
        + (line,) * 2
        + (rows, line, rows, line),
        check_vma=False,
    )
```

```python
from functools import partial

import jax
import jax.numpy as jnp
from jax import lax
from jax.experimental import pallas as pl
from jax.experimental.pallas import tpu as pltpu
from jax.sharding import PartitionSpec as P

MESH = pl.DeviceIdType.MESH
BF16 = jnp.bfloat16
F32 = jnp.float32


def remembered(method):
    def look_up(self, *args):
        key = (method.__name__,) + args
        if key not in self.known:
            self.known[key] = method(self, *args)
        return self.known[key]

    return look_up


class Place:
    def __init__(self, wide_size, narrow_size):
        self.known = {}
        self.wide = lax.axis_index("wide")
        self.narrow = lax.axis_index("narrow")
        self.n_narrow = narrow_size
        self.wide_count = wide_size
        self.columns = wide_size // 2
        self.n_a = 2 if self.columns % 2 == 0 else 1
        self.n_b = self.columns // self.n_a
        self.core = lax.rem(self.wide, 2)
        column = self.wide // 2
        self.a = column // self.n_b
        self.b = lax.rem(column, self.n_b)
        self.coloured = self.n_a == self.n_b

    def index(self, a, b, core):
        return (a * self.n_b + b) * 2 + core

    @remembered
    def sibling(self):
        return self.wide + 1 - 2 * self.core

    @remembered
    def along_a(self, step):
        return self.index(lax.rem(self.a + step, self.n_a), self.b, self.core)

    @remembered
    def along_b(self, step):
        return self.index(self.a, lax.rem(self.b + step, self.n_b), self.core)

    def first_count(self):
        return self.n_b

    def second_count(self):
        return self.n_a

    @remembered
    def first(self, step):
        if not self.coloured:
            return self.along_b(step)
        return jnp.where(self.core == 0, self.along_b(step), self.along_a(step))

    @remembered
    def second(self, step):
        if not self.coloured:
            return self.along_a(step)
        return jnp.where(self.core == 0, self.along_a(step), self.along_b(step))

    @remembered
    def corner(self, first_step, second_step):
        if not self.coloured:
            return self.index(
                lax.rem(self.a + second_step, self.n_a),
                lax.rem(self.b + first_step, self.n_b),
                self.core,
            )
        step_a = jnp.where(self.core == 0, second_step, first_step)
        step_b = jnp.where(self.core == 0, first_step, second_step)
        return self.index(
            lax.rem(self.a + step_a, self.n_a), lax.rem(self.b + step_b, self.n_b), self.core
        )

    @remembered
    def depth(self, step):
        return lax.rem(self.narrow + step, self.n_narrow)

    @remembered
    def beside(self, first_step, second_step):
        step_a, step_b = second_step, first_step
        if self.coloured:
            step_a = jnp.where(self.core == 1, second_step, first_step)
            step_b = jnp.where(self.core == 1, first_step, second_step)
        return self.index(
            lax.rem(self.a + step_a, self.n_a), lax.rem(self.b + step_b, self.n_b), 1 - self.core
        )

    def greet(self):
        barrier = pltpu.get_barrier_semaphore()
        count = 0
        for step in range(1, self.n_narrow):
            pl.semaphore_signal(
                barrier, inc=1, device_id=(self.wide, self.depth(step)), device_id_type=MESH
            )
            count += 1
        for step in range(1, self.n_b):
            pl.semaphore_signal(
                barrier, inc=1, device_id=(self.along_b(step), self.narrow), device_id_type=MESH
            )
            count += 1
        for step in range(1, self.n_a):
            pl.semaphore_signal(
                barrier, inc=1, device_id=(self.along_a(step), self.narrow), device_id_type=MESH
            )
            count += 1
        pl.semaphore_signal(
            barrier, inc=1, device_id=(self.sibling(), self.narrow), device_id_type=MESH
        )
        pl.semaphore_wait(barrier, count + 1)


class Gather:
    def __init__(self, place, own, full, sems):
        self.place = place
        self.own = own
        self.full = full
        self.send, self.recv = sems
        self.rows = own.shape[0]
        self.pending = []
        p = place
        self.n_z = p.n_narrow - 1
        self.n_1 = (p.first_count() - 1) * p.n_narrow
        self.n_2 = (p.second_count() - 1) * p.first_count()

    def view(self, wide, narrow=None):
        n = self.place.n_narrow
        if narrow is None:
            start, size = wide * n * self.rows, n * self.rows
        else:
            start, size = (wide * n + narrow) * self.rows, self.rows
        return self.full.at[pl.ds(pl.multiple_of(start, self.rows), size), :]

    def copy(self, src, dst, slot, device):
        return pltpu.make_async_remote_copy(
            src_ref=src,
            dst_ref=dst,
            send_sem=self.send.at[slot],
            recv_sem=self.recv.at[slot],
            device_id=device,
            device_id_type=MESH,
        )

    def go(self, copy):
        copy.start()
        self.pending.append(copy)

    def landed(self, view, slot):
        self.copy(view, view, slot, (self.place.sibling(), self.place.narrow)).wait_recv()

    def slot_first(self, step, k):
        return self.n_z + (step - 1) * self.place.n_narrow + k

    def slot_second(self, step, k):
        return self.n_z + self.n_1 + (step - 1) * self.place.first_count() + k

    def slot_sibling(self, k):
        return self.n_z + self.n_1 + self.n_2 + k

    def stage_1(self):
        p = self.place
        for step in range(1, p.n_narrow):
            self.go(
                self.copy(
                    self.own,
                    self.view(p.wide, p.narrow),
                    step - 1,
                    (p.wide, p.depth(step)),
                )
            )
        for step in range(1, p.first_count()):
            self.go(
                self.copy(
                    self.own,
                    self.view(p.wide, p.narrow),
                    self.slot_first(step, 0),
                    (p.first(step), p.narrow),
                )
            )

    def stage_2(self):
        p = self.place
        for step in range(1, p.n_narrow):
            source = p.depth(p.n_narrow - step)
            view = self.view(p.wide, source)
            self.landed(view, step - 1)
            for hop in range(1, p.first_count()):
                self.go(
                    self.copy(view, view, self.slot_first(hop, step), (p.first(hop), p.narrow))
                )
        view = self.view(p.wide)
        for hop in range(1, p.second_count()):
            self.go(self.copy(view, view, self.slot_second(hop, 0), (p.second(hop), p.narrow)))
        self.go(self.copy(view, view, self.slot_sibling(0), (p.sibling(), p.narrow)))

    def stage_3(self):
        p = self.place
        for step in range(1, p.first_count()):
            column = p.first(p.first_count() - step)
            for k in range(p.n_narrow):
                source = p.depth(p.n_narrow - k)
                self.landed(self.view(column, source), self.slot_first(step, k))
            view = self.view(column)
            for hop in range(1, p.second_count()):
                self.go(
                    self.copy(view, view, self.slot_second(hop, step), (p.second(hop), p.narrow))
                )
            self.go(self.copy(view, view, self.slot_sibling(step), (p.sibling(), p.narrow)))

    def stage_4(self):
        p = self.place
        for hop in range(1, p.second_count()):
            back = p.second_count() - hop
            for k in range(p.first_count()):
                column = p.corner((p.first_count() - k) % p.first_count(), back)
                view = self.view(column)
                self.landed(view, self.slot_second(hop, k))
                slot = self.slot_sibling(hop * p.first_count() + k)
                self.go(self.copy(view, view, slot, (p.sibling(), p.narrow)))

    def stage_5(self):
        p = self.place
        for hop in range(p.second_count()):
            for k in range(p.first_count()):
                back_1 = (p.first_count() - k) % p.first_count()
                back_2 = (p.second_count() - hop) % p.second_count()
                column = p.beside(back_1, back_2)
                self.landed(self.view(column), self.slot_sibling(hop * p.first_count() + k))

    def drain(self):
        for copy in self.pending:
            copy.wait_send()


def gather_slots(wide_size, narrow_size):
    columns = wide_size // 2
    n_a = 2 if columns % 2 == 0 else 1
    n_b = columns // n_a
    return (narrow_size - 1) + (n_b - 1) * narrow_size + (n_a - 1) * n_b + n_a * n_b


class Scatter:
    def __init__(self, place, grad, out, bufs, sems):
        self.place = place
        self.grad = grad
        self.out = out
        self.held, self.from_sibling, self.from_second, self.from_first, self.from_depth = bufs
        self.send, self.recv, self.local = sems
        self.pending = []
        p = place
        self.n_1 = p.first_count()
        self.n_2 = p.second_count()
        self.blocks = self.n_1 * self.n_2
        self.rows = out.shape[0]
        self.store = partial(out.__setitem__, ...)

    def view(self, wide):
        size = self.place.n_narrow * self.rows
        return self.grad.at[pl.ds(pl.multiple_of(wide * size, size), size), :]

    def copy(self, src, dst, slot, device):
        return pltpu.make_async_remote_copy(
            src_ref=src,
            dst_ref=dst,
            send_sem=self.send.at[slot],
            recv_sem=self.recv.at[slot],
            device_id=device,
            device_id_type=MESH,
        )

    def go(self, copy):
        copy.start()
        self.pending.append(copy)

    def landed(self, ref, slot):
        self.copy(ref, ref, slot, (self.place.sibling(), self.place.narrow)).wait_recv()

    def loads(self):
        p = self.place
        result = []
        for s in range(self.n_2):
            for f in range(self.n_1):
                block = s * self.n_1 + f
                result.append(
                    pltpu.make_async_copy(
                        self.view(p.corner(f, s)), self.held.at[block], self.local.at[block]
                    )
                )
        return result

    def stage_0(self):
        p = self.place
        for s in range(self.n_2):
            for f in range(self.n_1):
                column = p.beside(f, s)
                block = s * self.n_1 + f
                self.go(
                    self.copy(
                        self.view(column),
                        self.from_sibling.at[block],
                        block,
                        (p.sibling(), p.narrow),
                    )
                )
        for load in self.loads():
            load.start()

    def add(self, block, *others):
        total = self.held[block]
        for other in others:
            total = total + other[...]
        self.held[block] = total

    def piece(self, narrow):
        return pl.ds(pl.multiple_of(narrow * self.rows, self.rows), self.rows)

    def stage_1(self):
        p = self.place
        for load in self.loads():
            load.wait()
        for block in range(self.blocks):
            self.landed(self.from_sibling.at[block], block)
        for s in range(self.n_2 - 1, -1, -1):
            for f in range(self.n_1):
                block = s * self.n_1 + f
                self.add(block, self.from_sibling.at[block])
                if s > 0:
                    slot = (s - 1) * self.n_1 + f
                    self.go(
                        self.copy(
                            self.held.at[block],
                            self.from_second.at[slot],
                            self.blocks + slot,
                            (p.second(s), p.narrow),
                        )
                    )

    def stage_2(self):
        p = self.place
        base = self.blocks + (self.n_2 - 1) * self.n_1
        for f in range(self.n_1 - 1, -1, -1):
            slots = [s * self.n_1 + f for s in range(self.n_2 - 1)]
            for slot in slots:
                self.landed(self.from_second.at[slot], self.blocks + slot)
            self.add(f, *[self.from_second.at[slot] for slot in slots])
            if f > 0:
                self.go(
                    self.copy(
                        self.held.at[f],
                        self.from_first.at[f - 1],
                        base + f - 1,
                        (p.first(f), p.narrow),
                    )
                )

    def stage_3(self):
        p = self.place
        first_base = self.blocks + (self.n_2 - 1) * self.n_1
        base = first_base + self.n_1 - 1
        for f in range(1, self.n_1):
            self.landed(self.from_first.at[f - 1], first_base + f - 1)
        self.add(0, *[self.from_first.at[f - 1] for f in range(1, self.n_1)])
        for step in range(1, p.n_narrow):
            self.go(
                self.copy(
                    self.held.at[0, self.piece(p.depth(step)), :],
                    self.from_depth.at[step - 1],
                    base + step - 1,
                    (p.wide, p.depth(step)),
                )
            )

    def stage_4(self):
        p = self.place
        base = self.blocks + (self.n_2 - 1) * self.n_1 + self.n_1 - 1
        for step in range(1, p.n_narrow):
            self.landed(self.from_depth.at[step - 1], base + step - 1)
        total = self.held[0, self.piece(p.narrow), :].astype(F32)
        for step in range(1, p.n_narrow):
            total = total + self.from_depth[step - 1].astype(F32)
        self.store(total)

    def drain(self):
        for copy in self.pending:
            copy.wait_send()


def scatter_slots(wide_size, narrow_size):
    columns = wide_size // 2
    n_a = 2 if columns % 2 == 0 else 1
    n_b = columns // n_a
    return n_a * n_b + (n_a - 1) * n_b + (n_b - 1) + (narrow_size - 1)


D = 1024
HEADS = 8
HD = 128
GROUP = 128
EPSILON = 1e-05
SCALE = HD ** (-0.5)
NN = (((1,), (0,)), ((), ()))
NT = (((1,), (1,)), ((), ()))
TN = (((0,), (0,)), ((), ()))

U_Q, U_K, U_V, U_CO, U_SQ, U_SK, U_SV, U_SO, U_D, U_U = 0, 1, 2, 3, 4, 5, 6, 7, 8, 9
UNITS = 16
VECTORS = 16
V_CG, V_CS, V_IG, V_IS, V_SG, V_SS, V_MG, V_MS, V_BD, V_BU = range(10)
(S_LAT, S_SRC, S_Q, S_K, S_V, S_MIX, S_SL, S_SQ, S_SK, S_SV, S_SMIX) = range(11)


def dot(left, right, dims=NN):
    return lax.dot_general(left, right, dims, preferred_element_type=F32)


def for_each(count, step, unroll=1):
    def run(i, carry):
        step(i)
        return carry

    lax.fori_loop(0, count, run, 0, unroll=unroll)


def part(i, size):
    return pl.ds(pl.multiple_of(i * size, size), size)


def gather_units(sizes, shards):
    rows = D // (sizes[0] * sizes[1])
    q, kv, co, qkv, so, down, up = range(7)
    units = [(q, 0, 0), (kv, 0, 0), (kv, 0, 1), (co, 0, 0), (qkv, 0, 0), (qkv, 0, 1), (qkv, 0, 2)]
    units.append((so, 0, 0))
    for i in range(4):
        units.append((down, i * rows, 0))
        units.append((up, 0, i))
    return rows, units


def norm_stats(x):
    mean = jnp.mean(x, axis=-1, keepdims=True)
    center = x - mean
    spread = jnp.mean(center * center, axis=-1, keepdims=True)
    return center, lax.rsqrt(spread + EPSILON)


def group_mask(row_ids, column_ids):
    across = jnp.broadcast_to(row_ids.astype(F32), (GROUP, GROUP)).T
    return across == jnp.broadcast_to(column_ids.astype(F32), (GROUP, GROUP))


def softmax_columns(scores):
    raised = jnp.exp(scores - jnp.max(scores, axis=0, keepdims=True))
    return raised * (1.0 / jnp.sum(raised, axis=0, keepdims=True))


HEAD_COLUMNS = [slice(h * HD, (h + 1) * HD) for h in range(HEADS)]
HALVES = (slice(0, 512), slice(512, 1024))


def gelu_parts(x):
    half = 0.5 * (1.0 + lax.erf(x * (2.0**-0.5)))
    return x * half, half + x * (jnp.exp(-0.5 * x * x) * ((2.0 * jnp.pi) ** -0.5))


def reorder_up(pool, raw, stage, rows):
    lane = lax.broadcasted_iota(jnp.int32, (rows, 128), 1)
    for i in range(4):
        for g in range(D // 128):
            total = jnp.zeros((rows, 128), F32)
            for k in range(128 // rows):
                column = (g * (128 // rows) + k) * 4 * rows + i * rows
                block, inside = divmod(column, D)
                group, offset = divmod(inside, 128)
                piece = pool[raw, pl.ds(block * rows, rows), group * 128 : (group + 1) * 128]
                piece = piece.astype(F32)
                shift = (k * rows - offset) % 128
                if shift:
                    piece = pltpu.roll(piece, shift, axis=1)
                total = jnp.where(lane // rows == k, piece, total)
            unit = U_U + 2 * i
            pool[stage, pl.ds(unit * rows, rows), g * 128 : (g + 1) * 128] = total.astype(BF16)


def restore_up(out, value, i, rows):
    for g in range(D // 128):
        lanes = value[:, g * 128 : (g + 1) * 128]
        for k in range(128 // rows):
            column = (g * (128 // rows) + k) * 4 * rows + i * rows
            offset = column % 128
            shift = (offset - k * rows) % 128
            piece = pltpu.roll(lanes, shift, axis=1) if shift else lanes
            out[:, column : column + rows] = piece[:, offset : offset + rows]


class Ticks:
    def __init__(self, jobs):
        self.jobs = jobs
        self.done = 0
        self.last = len(jobs) + 3

    def one(self):
        t = self.done
        if t >= self.last:
            return
        for back, stage in ((3, "stage_5"), (2, "stage_4"), (1, "stage_3"), (0, "stage_2"), (-1, "stage_1")):
            if 0 <= t - back < len(self.jobs):
                getattr(self.jobs[t - back], stage)()
        self.done = t + 1

    def until(self, job):
        while self.done < job + 4:
            self.one()


HELD = 5
FROM = 4
NEAR = 3
(G_SO, G_SQ, G_SK, G_SV, G_CO, G_Q, G_K, G_V) = range(8)


def fold_rows(value):
    return jnp.sum(value.reshape(-1, 8, D), axis=0)


def scatter_targets():
    targets = []
    for i in range(4):
        targets.append((0, i, 0))
        targets.append((1, 0, i))
    targets.append((2, 0, 0))
    for c in range(3):
        targets.append((3, 0, c))
    targets += [(4, 0, 0), (5, 0, 0), (6, 0, 0), (6, 0, 1)]
    return targets


class Sums:
    STAGES = ("stage_0", "stage_1", "stage_2", "stage_3", "stage_4")

    def __init__(self, jobs, credit, place):
        self.jobs = jobs
        self.credit = credit
        self.place = place
        self.stage = [0] * len(jobs)
        self.started = 0
        self.drained = 0
        self.waits = {}

    def one(self, start=True):
        big = len(self.jobs) - 1
        running = [j for j in range(self.started) if self.stage[j] < 5]
        if start and self.started < len(self.jobs):
            j = self.started
            for copy in self.waits.pop(j, ()):
                copy.wait()
            if j < big and j >= NEAR:
                pl.semaphore_wait(self.credit, 1)
            if j < big and j >= HELD:
                self.jobs[j - HELD].drain()
                self.drained = j - HELD + 1
            running.append(j)
            self.started += 1
        for j in running[::-1]:
            getattr(self.jobs[j], self.STAGES[self.stage[j]])()
            if self.stage[j] == 1 and j + NEAR < big:
                pl.semaphore_signal(
                    self.credit,
                    inc=1,
                    device_id=(self.place.sibling(), self.place.narrow),
                    device_id_type=MESH,
                )
            self.stage[j] += 1

    def finish(self):
        while self.started < len(self.jobs) or self.stage[-1] < 5:
            self.one()
        for job in self.jobs[self.drained :]:
            job.drain()


def layer_kernel(sizes, *refs):
    vec_shard, shards, rest = refs[0], refs[1:8], refs[8:]
    latents, inputs, cot, lat_ids, in_ids = rest[:5]
    finished, latent_grad, input_grad, full, vec_full, kept, kept_f, g_mlp, g_att, vec_sent = rest[5:15]
    vec_out, *outs = rest[15:23]
    (
        vec_staged,
        vec_all,
        vec,
        small,
        pool,
        fpool,
        vacc,
        held,
        near,
        from_second,
        from_first,
        from_depth,
        vheld,
        vnear,
        vsecond,
        vfirst,
        vdepth,
        send,
        recv,
        vsend,
        vrecv,
        rsend,
        rrecv,
        local,
        credit,
        sem_stage,
        sem_own,
        sem_in,
        sem_w,
        sem_f,
        sem_keep,
        sem_keep_f,
        sem_g,
        sem_o,
    ) = rest[23:]
    place = Place(*sizes)
    rows, units = gather_units(sizes, shards)
    mine = place.wide * place.n_narrow + place.narrow

    LAT, INP, LLOW, SLOW, Q, K, V, MIX = 0, 1, 2, 3, 8, 9, 10, 11
    W0 = 4
    SELF = (12, 13, 4, 5)
    ML, COT = 2, 3
    STAGE, RAW = 13, 12

    copies_in = [
        pltpu.make_async_copy(latents, pool.at[LAT], sem_in.at[0]),
        pltpu.make_async_copy(inputs, pool.at[INP], sem_in.at[1]),
    ]
    stage_in = []
    for u, (k, r0, c0) in enumerate(units):
        source = shards[k].at[pl.ds(r0, rows), pl.ds(c0 * D, D)]
        target = pool.at[RAW, part(c0, rows), :] if k == 6 else pool.at[STAGE, part(u, rows), :]
        stage_in.append(pltpu.make_async_copy(source, target, sem_stage.at[u]))
    stage_in.append(pltpu.make_async_copy(vec_shard, vec_staged, sem_stage.at[UNITS]))
    own_out = [
        pltpu.make_async_copy(
            pool.at[STAGE, part(u, rows), :], full.at[u, part(mine, rows), :], sem_own.at[u]
        )
        for u in range(UNITS)
    ]
    own_out.append(
        pltpu.make_async_copy(vec_staged, vec_full.at[part(mine, VECTORS), :], sem_own.at[UNITS])
    )
    for copy in stage_in[::-1]:
        copy.start()
    for copy in copies_in:
        copy.start()
    place.greet()
    jobs = [Gather(place, vec_shard, vec_full, (vsend, vrecv))]
    for u, (k, r0, c0) in enumerate(units):
        source = shards[k].at[pl.ds(r0, rows), pl.ds(c0 * D, D)]
        if k == 6:
            source = full.at[u, part(mine, rows), :]
        jobs.append(Gather(place, source, full.at[u], (send.at[u], recv.at[u])))
    ticks = Ticks(jobs)
    limit = [0]
    sum_jobs = []
    for i, (p, r, c) in enumerate(scatter_targets()):
        grad = g_mlp.at[i] if i < 8 else g_att.at[i - 8]
        out = outs[p].at[pl.ds(r * rows, rows), pl.ds(c * D, D)]
        turn = i % HELD
        bufs = (
            held.at[turn],
            near.at[i % NEAR],
            from_second.at[i % FROM],
            from_first.at[i % FROM],
            from_depth.at[i % FROM],
        )
        sum_jobs.append(Scatter(place, grad, out, bufs, (rsend.at[i], rrecv.at[i], local.at[i])))
        if p == 1:
            sum_jobs[-1].store = partial(restore_up, outs[1], i=c, rows=rows)
    sum_jobs.append(
        Scatter(
            place,
            vec_sent,
            vec_out,
            (vheld, vnear, vsecond, vfirst, vdepth),
            (rsend.at[UNITS], rrecv.at[UNITS], local.at[UNITS]),
        )
    )
    sums = Sums(sum_jobs, credit, place)

    def tick():
        sums.one(start=sums.started < limit[0])

    jobs[0].stage_1()
    for i in range(UNITS, -1, -1):
        stage_in[i].wait()
    reorder_up(pool, RAW, STAGE, rows)
    for i in range(UNITS, -1, -1):
        own_out[i].start()
    for i in range(UNITS, -1, -1):
        own_out[i].wait()

    def load(unit, slot):
        return pltpu.make_async_copy(full.at[unit], pool.at[slot], sem_w.at[slot])

    def fetch(unit, slot):
        ticks.until(unit + 1)
        load(unit, slot).start()

    def keep(slot, index):
        return pltpu.make_async_copy(pool.at[slot], kept.at[index], sem_keep.at[index])

    def keep_f(slot, index):
        return pltpu.make_async_copy(fpool.at[slot], kept_f.at[index], sem_keep_f.at[index])

    def vector(k, columns=slice(None)):
        return vec[k : k + 1, columns]

    ticks.until(0)
    copy = pltpu.make_async_copy(vec_full, vec_all, sem_in.at[2])
    copy.start()
    copy.wait()
    lane_groups = D // 128
    per = place.wide_count * place.n_narrow // lane_groups
    for g in range(lane_groups):
        total = vec_all[pl.ds(g * per * VECTORS, VECTORS), :]
        for j in range(1, per):
            total = total + vec_all[pl.ds((g * per + j) * VECTORS, VECTORS), :]
        vec[:, g * 128 : (g + 1) * 128] = total

    def norm_low(read, slot, gain, shift):
        def step(i):
            sl = part(i, 64)
            center, rate = norm_stats(read(sl))
            pool[slot, sl, :] = (center * rate * vector(gain) + vector(shift)).astype(BF16)

        for_each(16, step)

    def product(out, left, weight):
        values = [dot(pool[left], pool[weight, :, sl]) for sl in HALVES]
        for sl, value in zip(HALVES, values):
            pool[out, :, sl] = value.astype(BF16)

    def attend(q, k, v, out, ids, groups):
        def step(g):
            sl = part(g, GROUP)
            mask = group_mask(ids[pl.ds(g, 1), :], lat_ids[pl.ds(g, 1), :])
            scores = [dot(pool[k, sl, hs], pool[q, sl, hs], NT) for hs in HEAD_COLUMNS]
            weights = [softmax_columns(jnp.where(mask, x * SCALE, -1e30)).astype(BF16) for x in scores]
            mixed = [dot(x, pool[v, sl, hs], TN) for x, hs in zip(weights, HEAD_COLUMNS)]
            for x, hs in zip(mixed, HEAD_COLUMNS):
                pool[out, sl, hs] = x.astype(BF16)

        lo, hi = groups

        def run(g, carry):
            step(g)
            return carry

        lax.fori_loop(lo, hi, run, 0)

    copies_in[0].wait()
    norm_low(lambda sl: pool[LAT, sl, :].astype(F32), LLOW, V_CG, V_CS)
    keep(LLOW, S_LAT).start()
    fetch(U_Q, W0)
    copies_in[1].wait()
    norm_low(lambda sl: pool[INP, sl, :].astype(F32), SLOW, V_IG, V_IS)
    keep(SLOW, S_SRC).start()
    load(U_Q, W0).wait()
    product(Q, LLOW, W0)
    keep(Q, S_Q).start()
    fetch(U_K, W0 + 1)
    load(U_K, W0 + 1).wait()
    product(K, SLOW, W0 + 1)
    keep(K, S_K).start()
    fetch(U_V, W0 + 2)
    load(U_V, W0 + 2).wait()
    product(V, SLOW, W0 + 2)
    keep(V, S_V).start()
    attend(Q, K, V, MIX, in_ids, (0, 4))
    fetch(U_CO, W0 + 3)
    attend(Q, K, V, MIX, in_ids, (4, 8))
    keep(MIX, S_MIX).start()
    load(U_CO, W0 + 3).wait()

    values = [dot(pool[MIX], pool[W0 + 3, :, sl]) for sl in HALVES]
    for sl, value in zip(HALVES, values):
        fpool[0, :, sl] = pool[LAT, :, sl].astype(F32) + value
    keep_f(0, 0).start()
    fetch(U_SQ, SELF[0])
    norm_low(lambda sl: fpool[0, sl, :], LAT, V_SG, V_SS)
    keep(LAT, S_SL).start()
    keep(Q, S_Q).wait()
    keep(K, S_K).wait()
    keep(V, S_V).wait()
    for offset, (slot, index, before) in enumerate(((Q, S_SQ, 0), (K, S_SK, 0), (V, S_SV, 0))):
        load(U_SQ + offset, SELF[offset]).wait()
        product(slot, LAT, SELF[offset])
        keep(slot, index).start()
        fetch(U_SQ + offset + 1, SELF[offset + 1])
    keep(MIX, S_MIX).wait()
    attend(Q, K, V, MIX, lat_ids, (0, 4))
    ticks.one()
    attend(Q, K, V, MIX, lat_ids, (4, 8))
    keep(MIX, S_SMIX).start()
    load(U_SO, SELF[3]).wait()

    values = [dot(pool[MIX], pool[SELF[3], :, sl]) for sl in HALVES]
    for sl, value in zip(HALVES, values):
        fpool[1, :, sl] = fpool[0, :, sl] + value
    keep_f(1, 1).start()
    keep(LLOW, S_LAT).wait()
    keep(SLOW, S_SRC).wait()
    cot_in = pltpu.make_async_copy(cot, pool.at[COT], sem_in.at[3])
    cot_in.start()
    norm_low(lambda sl: fpool[1, sl, :], ML, V_MG, V_MS)
    cot_in.wait()
    for slot, index in ((LAT, S_SL), (Q, S_SQ), (K, S_SK), (V, S_SV), (MIX, S_SMIX)):
        keep(slot, index).wait()
    keep_f(1, 1).wait()
    keep_f(0, 0).wait()

    ACT, GH = 8, 9
    PAIR = (6, 4)
    GD, GU = 10, 12
    GIN = 0
    CH = 512
    R = 256
    small[...] = jnp.zeros_like(small)

    def spread(chunk):
        i, h = divmod(chunk, 2)
        down, up = PAIR[i % 2], PAIR[i % 2] + 1
        cols = pl.ds(h * CH, CH)
        values = dot(pool[ML], pool[up, :, cols]), dot(pool[COT], pool[down, cols, :], NT)
        fpool[2, :, 0:CH] = values[0]
        fpool[2, :, CH : 2 * CH] = values[1]

    def bend(chunk, sl):
        i, h = divmod(chunk, 2)
        cols = pl.ds(h * CH, CH)
        value, slope = gelu_parts(fpool[2, sl, 0:CH] + vec[V_BU + i : V_BU + i + 1, cols])
        value, grad = value.astype(BF16), (slope * fpool[2, sl, CH : 2 * CH]).astype(BF16)
        total = jnp.sum(grad.astype(F32), axis=0, keepdims=True)

        def store():
            out = pl.ds((chunk % 2) * CH, CH)
            pool[ACT, sl, out] = value
            pool[GH, sl, out] = grad
            small[i : i + 1, cols] += total

        return store

    def fold(chunk, sl):
        i, h = divmod(chunk, 2)
        down, up = PAIR[i % 2], PAIR[i % 2] + 1
        cols = pl.ds(h * CH, CH)
        out = pl.ds((chunk % 2) * CH, CH)
        result = fpool[1, sl, :] + dot(pool[ACT, sl, out], pool[down, cols, :])
        grad = dot(pool[GH, sl, out], pool[up, :, cols], NT)
        if chunk > 0:
            grad = grad + fpool[GIN, sl, :]

        def store():
            fpool[1, sl, :] = result
            fpool[GIN, sl, :] = grad

        return store

    def grad_out(i):
        return [
            pltpu.make_async_copy(pool.at[GD + i % 2], g_mlp.at[2 * i], sem_g.at[2 * i]),
            pltpu.make_async_copy(pool.at[GU + i % 2], g_mlp.at[2 * i + 1], sem_g.at[2 * i + 1]),
        ]

    def weigh(chunk):
        i, h = divmod(chunk, 2)
        cols = pl.ds(h * CH, CH)
        out = pl.ds((chunk % 2) * CH, CH)
        down = dot(pool[ACT, :, out], pool[COT], TN)
        up = dot(pool[ML], pool[GH, :, out], TN)
        pool[GD + i % 2, cols, :] = down.astype(BF16)
        pool[GU + i % 2, :, cols] = up.astype(BF16)

    def fetch_pair(i):
        fetch(U_D + 2 * i, PAIR[i % 2])
        fetch(U_U + 2 * i, PAIR[i % 2] + 1)

    for chunk in range(8):
        i, h = divmod(chunk, 2)
        if h == 0:
            if i == 0:
                fetch_pair(0)
            load(U_D + 2 * i, PAIR[i % 2]).wait()
            load(U_U + 2 * i, PAIR[i % 2] + 1).wait()
            spread(chunk)
            ticks.one()
        else:
            spread(chunk)
            if i < 3:
                fetch_pair(i + 1)

        def rows_step(r):
            sl = part(r, R)
            stores = [bend(chunk, sl)]
            if chunk > 0:
                stores.append(fold(chunk - 1, sl))
            for store in stores:
                store()

        for_each(D // R, rows_step)
        if h == 0 and i >= 2:
            for job in (2 * i - 4, 2 * i - 3):
                for copy in sums.waits.pop(job, ()):
                    copy.wait()
        weigh(chunk)
        if h == 1:
            for job, copy in enumerate(grad_out(i), 2 * i):
                copy.start()
                sums.waits[job] = (copy,)
            limit[0] = 2 * i + 2
        if chunk >= 3:
            tick()

    A, B, C, DD, E, F, G, S1, S2 = 9, 1, 5, COT, 6, 7, 0, GD, GU

    def load_f(index, slot):
        return pltpu.make_async_copy(kept_f.at[index], fpool.at[slot], sem_f.at[slot])

    def bring(source, slot):
        return pltpu.make_async_copy(source, pool.at[slot], sem_w.at[slot])

    first = [
        bring(kept.at[S_SMIX], B),
        bring(kept.at[S_SQ], E),
        bring(kept.at[S_SK], F),
        bring(kept.at[S_SV], G),
        bring(full.at[U_SO], C),
        load_f(1, 1),
    ]

    def last(r):
        sl = part(r, R)
        fold(7, sl)()
        pool[ML, sl, :] = (fpool[1, sl, :] + vector(V_BD)).astype(BF16)

    for copy in first[:4]:
        copy.start()
    for_each(D // R, last)
    first[4].start()
    first[5].start()
    done = pltpu.make_async_copy(pool.at[ML], finished, sem_in.at[4])
    done.start()
    while ticks.done < ticks.last:
        ticks.one()
    for job in jobs:
        job.drain()

    vacc[...] = jnp.zeros_like(vacc)

    def norm_back(read_x, grad_slot, gain, shift, write):
        def step(i, carry):
            sl = part(i, 64)
            center, rate = norm_stats(read_x(sl))
            normal = center * rate
            grad = fpool[grad_slot, sl, :]
            sums_gain = carry[0] + fold_rows(grad * normal)
            sums_shift = carry[1] + fold_rows(grad)
            grad = grad * vec[gain : gain + 1, :]
            mean_1 = jnp.mean(grad, axis=-1, keepdims=True)
            mean_2 = jnp.mean(grad * normal, axis=-1, keepdims=True)
            write(sl, rate * (grad - mean_1 - normal * mean_2))
            return sums_gain, sums_shift

        zero = jnp.zeros((8, D), F32)
        carry = (zero, zero)
        carry = lax.fori_loop(0, 16, step, carry)
        vacc[gain] = carry[0]
        vacc[shift] = carry[1]
        tick()

    staging = [S1, S2]
    saved = [4, 5]

    def weight_grad(index, left, right):
        turn = index % 2
        if saved[turn] is not None and saved[turn] in sums.waits:
            for copy in sums.waits.pop(saved[turn]):
                copy.wait()
        slot = staging[turn]

        values = [dot(pool[left], pool[right, :, sl], TN) for sl in HALVES]
        for sl, value in zip(HALVES, values):
            pool[slot, :, sl] = value.astype(BF16)
        copy = pltpu.make_async_copy(pool.at[slot], g_att.at[index], sem_g.at[8 + index])
        copy.start()
        sums.waits[8 + index] = (copy,)
        saved[turn] = 8 + index
        limit[0] = 8 + index + 1

    def back_product(out, left, weight):
        values = [dot(pool[left], pool[weight, sl, :], NT) for sl in HALVES]
        for sl, value in zip(HALVES, values):
            pool[out, :, sl] = value.astype(BF16)

    def back_sum(out, left, weight, fresh):
        values = [dot(pool[left], pool[weight, sl, :], NT) for sl in HALVES]
        if not fresh:
            values = [value + fpool[out, :, sl] for sl, value in zip(HALVES, values)]
        for sl, value in zip(HALVES, values):
            fpool[out, :, sl] = value

    def attend_back(q, k, v, grad, ids):
        def step(g, carry):
            sl = part(g, GROUP)
            mask = group_mask(ids[pl.ds(g, 1), :], lat_ids[pl.ds(g, 1), :])
            scores = [dot(pool[k, sl, hs], pool[q, sl, hs], NT) for hs in HEAD_COLUMNS]
            slopes = [dot(pool[v, sl, hs], pool[grad, sl, hs], NT) for hs in HEAD_COLUMNS]
            weights = [softmax_columns(jnp.where(mask, x * SCALE, -1e30)) for x in scores]
            inner = [jnp.sum(x * y, axis=0, keepdims=True) for x, y in zip(weights, slopes)]
            slopes = [(x * (y - z)).astype(BF16) for x, y, z in zip(weights, slopes, inner)]
            weights = [x.astype(BF16) for x in weights]
            grad_v = [dot(x, pool[grad, sl, hs]) for x, hs in zip(weights, HEAD_COLUMNS)]
            grad_k = [dot(x, pool[q, sl, hs]) * SCALE for x, hs in zip(slopes, HEAD_COLUMNS)]
            grad_q = [dot(x, pool[k, sl, hs], TN) * SCALE for x, hs in zip(slopes, HEAD_COLUMNS)]
            for slot, values in ((v, grad_v), (k, grad_k), (q, grad_q)):
                for x, hs in zip(values, HEAD_COLUMNS):
                    pool[slot, sl, hs] = x.astype(BF16)
            return carry

        lax.fori_loop(0, 8, step, 0)
        tick()

    first[5].wait()

    def after_self(sl, grad):
        cot_rows = pool[DD, sl, :].astype(F32)
        vacc[V_BD] += fold_rows(cot_rows)
        total = cot_rows + grad
        fpool[2, sl, :] = total
        pool[A, sl, :] = total.astype(BF16)

    norm_back(lambda sl: fpool[1, sl, :], 0, V_MG, V_MS, after_self)
    load_f(0, 1).start()

    for copy in first[:5]:
        copy.wait()
    weight_grad(G_SO, B, A)
    bring(kept.at[S_SL], B).start()
    back_product(DD, A, C)
    bring(full.at[U_SQ], A).start()
    bring(full.at[U_SK], C).start()
    tick()
    attend_back(E, F, G, DD, lat_ids)
    bring(full.at[U_SV], DD).start()
    bring(kept.at[S_SL], B).wait()
    for index, slot, weight, unit in ((G_SQ, E, A, U_SQ), (G_SK, F, C, U_SK), (G_SV, G, DD, U_SV)):
        weight_grad(index, B, slot)
        bring(full.at[unit], weight).wait()
        back_sum(0, slot, weight, index == G_SQ)
        tick()
        if index == G_SQ:
            bring(kept.at[S_Q], E).start()
            bring(full.at[U_CO], A).start()
        elif index == G_SK:
            bring(kept.at[S_K], F).start()
        else:
            bring(kept.at[S_V], G).start()
            bring(kept.at[S_MIX], B).start()
    load_f(0, 1).wait()

    def after_cross(sl, grad):
        total = fpool[2, sl, :] + grad
        fpool[2, sl, :] = total
        pool[C, sl, :] = total.astype(BF16)

    norm_back(lambda sl: fpool[1, sl, :], 0, V_SG, V_SS, after_cross)

    bring(kept.at[S_MIX], B).wait()
    weight_grad(G_CO, B, C)
    bring(kept.at[S_LAT], B).start()
    bring(full.at[U_CO], A).wait()
    back_product(DD, C, A)
    bring(full.at[U_Q], A).start()
    bring(kept.at[S_SRC], C).start()
    tick()
    bring(kept.at[S_Q], E).wait()
    bring(kept.at[S_K], F).wait()
    bring(kept.at[S_V], G).wait()
    attend_back(E, F, G, DD, in_ids)
    bring(full.at[U_K], DD).start()
    bring(kept.at[S_LAT], B).wait()
    weight_grad(G_Q, B, E)
    bring(latents, B).start()
    tick()
    bring(kept.at[S_SRC], C).wait()
    weight_grad(G_K, C, F)
    tick()
    weight_grad(G_V, C, G)
    bring(inputs, C).start()
    tick()
    bring(full.at[U_Q], A).wait()
    back_sum(0, E, A, True)
    bring(full.at[U_V], A).start()
    bring(latents, B).wait()

    def latent_out(sl, grad):
        pool[E, sl, :] = (fpool[2, sl, :] + grad).astype(BF16)

    norm_back(lambda sl: pool[B, sl, :].astype(F32), 0, V_CG, V_CS, latent_out)
    done_1 = pltpu.make_async_copy(pool.at[E], latent_grad, sem_o.at[0])
    done_1.start()
    bring(full.at[U_K], DD).wait()
    back_sum(1, F, DD, True)
    bring(full.at[U_V], A).wait()
    back_sum(1, G, A, False)
    bring(inputs, C).wait()

    def input_out(sl, grad):
        pool[F, sl, :] = grad.astype(BF16)

    norm_back(lambda sl: pool[C, sl, :].astype(F32), 1, V_IG, V_IS, input_out)
    done_2 = pltpu.make_async_copy(pool.at[F], input_grad, sem_o.at[1])
    done_2.start()

    lane_groups = D // 128
    per = sizes[0] * sizes[1] // lane_groups
    for k in range(9):
        vacc[k, 0:1, :] = jnp.sum(vacc[k], axis=0, keepdims=True)
    for g in range(lane_groups):
        lanes = slice(g * 128, (g + 1) * 128)
        block = [vacc[k, 0:1, lanes] for k in range(9)]
        block += [small[0:4, lanes], jnp.zeros((3, 128), F32)]
        block = jnp.concatenate(block, axis=0)

        def put(j, carry):
            vec_all[part(g * per + j, VECTORS), :] = block
            return carry

        lax.fori_loop(0, per, put, 0)
    copy = pltpu.make_async_copy(vec_all, vec_sent, sem_o.at[2])
    copy.start()
    copy.wait()
    limit[0] = len(sum_jobs)
    sums.finish()
    done.wait()
    done_1.wait()
    done_2.wait()


def run_layer(vec_shard, shards, latents, inputs, cot, lat_ids, in_ids):
    sizes = (lax.axis_size("wide"), lax.axis_size("narrow"))
    everyone = sizes[0] * sizes[1]
    rows = D // everyone
    columns = sizes[0] // 2
    n_2 = 2 if columns % 2 == 0 else 1
    n_1 = columns // n_2
    n = sizes[1]
    widths = ((4 * rows, D), (rows, 4 * D), (rows, D), (rows, 3 * D), (rows, D), (rows, D), (rows, 2 * D))
    gslots = gather_slots(*sizes)
    slots = scatter_slots(*sizes)
    any_spec = pl.BlockSpec(memory_space=pl.ANY)
    vmem_spec = pl.BlockSpec(memory_space=pltpu.VMEM)
    dma = pltpu.SemaphoreType.DMA
    total = UNITS + 1
    return pl.pallas_call(
        partial(layer_kernel, sizes),
        out_shape=[
            jax.ShapeDtypeStruct((D, D), BF16),
            jax.ShapeDtypeStruct((D, D), BF16),
            jax.ShapeDtypeStruct((D, D), BF16),
            jax.ShapeDtypeStruct((UNITS, D, D), BF16),
            jax.ShapeDtypeStruct((everyone * VECTORS, 128), F32),
            jax.ShapeDtypeStruct((11, D, D), BF16),
            jax.ShapeDtypeStruct((2, D, D), F32),
            jax.ShapeDtypeStruct((8, D, D), BF16),
            jax.ShapeDtypeStruct((8, D, D), BF16),
            jax.ShapeDtypeStruct((everyone * VECTORS, 128), F32),
            jax.ShapeDtypeStruct((VECTORS, 128), F32),
        ]
        + [jax.ShapeDtypeStruct(shape, F32) for shape in widths],
        in_specs=[any_spec] * 11 + [vmem_spec] * 2,
        out_specs=[any_spec] * 10 + [vmem_spec] * 8,
        scratch_shapes=[
            pltpu.VMEM((VECTORS, 128), F32),
            pltpu.VMEM((everyone * VECTORS, 128), F32),
            pltpu.VMEM((VECTORS, D), F32),
            pltpu.VMEM((8, D), F32),
            pltpu.VMEM((14, D, D), BF16),
            pltpu.VMEM((3, D, D), F32),
            pltpu.VMEM((9, 8, D), F32),
            pltpu.VMEM((HELD, columns, n * rows, D), BF16),
            pltpu.VMEM((NEAR, columns, n * rows, D), BF16),
            pltpu.VMEM((FROM, (n_2 - 1) * n_1, n * rows, D), BF16),
            pltpu.VMEM((FROM, n_1 - 1, n * rows, D), BF16),
            pltpu.VMEM((FROM, n - 1, rows, D), BF16),
            pltpu.VMEM((columns, n * VECTORS, 128), F32),
            pltpu.VMEM((columns, n * VECTORS, 128), F32),
            pltpu.VMEM(((n_2 - 1) * n_1, n * VECTORS, 128), F32),
            pltpu.VMEM((n_1 - 1, n * VECTORS, 128), F32),
            pltpu.VMEM((n - 1, VECTORS, 128), F32),
            dma((UNITS, gslots)),
            dma((UNITS, gslots)),
            dma((gslots,)),
            dma((gslots,)),
            dma((total, slots)),
            dma((total, slots)),
            dma((total, columns)),
            pltpu.SemaphoreType.REGULAR,
            dma((UNITS + 1,)),
            dma((UNITS + 1,)),
            dma((5,)),
            dma((14,)),
            dma((3,)),
            dma((11,)),
            dma((2,)),
            dma((16,)),
            dma((3,)),
        ],
        compiler_params=pltpu.CompilerParams(
            collective_id=0, has_side_effects=True, vmem_limit_bytes=67_043_328
        ),
        name="layer",
    )(vec_shard, *shards, latents, inputs, cot, lat_ids, in_ids)


HAND_OVER_STEPS = 8


def hand_over_kernel(*refs):
    half = len(refs) // 2
    for source, target in zip(refs[:half], refs[half:]):
        target[...] = source[...]


def hand_over(arrays):
    steps = HAND_OVER_STEPS
    specs = []
    for member in arrays:
        height, width = member.shape
        if height == D:
            specs.append(pl.BlockSpec((height // steps, width), lambda i: (i, 0)))
        else:
            specs.append(pl.BlockSpec((height, width // steps), lambda i: (0, i)))
    return pl.pallas_call(
        hand_over_kernel,
        grid=(steps,),
        out_shape=[jax.ShapeDtypeStruct(member.shape, member.dtype) for member in arrays],
        in_specs=specs,
        out_specs=specs,
        name="hand_over",
    )(*arrays)


def body(
    latents,
    group_inputs,
    latent_images,
    input_images,
    cotangent,
    cross_gain,
    cross_shift,
    source_gain,
    source_shift,
    query_weight,
    keyval_weight,
    cross_out_weight,
    self_gain,
    self_shift,
    self_qkv_weight,
    self_out_weight,
    mlp_gain,
    mlp_shift,
    up_weight,
    up_bias,
    down_weight,
    down_bias,
):
    lat_ids = latent_images.reshape(-1, GROUP)
    in_ids = input_images.reshape(-1, GROUP)
    short = cross_gain.shape[0]
    per = 128 // short
    me = lax.axis_index(("wide", "narrow"))
    vectors = (
        cross_gain,
        cross_shift,
        source_gain,
        source_shift,
        self_gain,
        self_shift,
        mlp_gain,
        mlp_shift,
        down_bias,
    )
    stacked = jnp.concatenate(
        [jnp.stack(vectors), up_bias.reshape(4, short), jnp.zeros((3, short), BF16)]
    ).astype(F32)
    lane = lax.broadcasted_iota(jnp.int32, (VECTORS, 128), 1) // short
    packed = jnp.where(lane == lax.rem(me, per), jnp.tile(stacked, (1, per)), 0.0)
    finished, latent_grad, input_grad, *_, own_vec, g_down, g_up, g_so, g_qkv, g_co, g_q, g_kv = run_layer(
        packed,
        (
            query_weight,
            keyval_weight,
            cross_out_weight,
            self_qkv_weight,
            self_out_weight,
            down_weight,
            up_weight,
        ),
        latents,
        group_inputs,
        cotangent,
        lat_ids,
        in_ids,
    )
    finished, latent_grad, input_grad, g_down, g_up, g_so, g_qkv, g_co, g_q, g_kv = hand_over(
        (finished, latent_grad, input_grad, g_down, g_up, g_so, g_qkv, g_co, g_q, g_kv)
    )
    vec = lax.dynamic_slice_in_dim(own_vec, lax.rem(me, per) * short, short, axis=1)
    own_up_bias = vec[9:13].reshape(-1)
    return (
        finished,
        latent_grad,
        input_grad,
        vec[0],
        vec[1],
        vec[2],
        vec[3],
        g_q,
        g_kv,
        g_co,
        vec[4],
        vec[5],
        g_qkv,
        g_so,
        vec[6],
        vec[7],
        g_up,
        own_up_bias,
        g_down,
        vec[8],
    )


def solution(mesh):
    rows = P(("wide", "narrow"), None)
    line = P(("wide", "narrow"))
    return jax.shard_map(
        body,
        mesh=mesh,
        in_specs=(rows,) * 5
        + (line,) * 4
        + (rows,) * 3
        + (line,) * 2
        + (rows,) * 2
        + (line,) * 2
        + (rows, line, rows, line),
        out_specs=(rows,) * 3
        + (line,) * 4
        + (rows,) * 3
        + (line,) * 2
        + (rows,) * 2
        + (line,) * 2
        + (rows, line, rows, line),
        check_vma=False,
    )
```
